256 devices in a mesh: grp: 8 (over x, core), seq: 32 (over z, y).
Axes of the slice: x: 4, y: 4, z: 8, core: 2. Of those that a mesh axis runs over, the one named last changes fastest.
Arguments:
- spikes: bfloat16 [8, 4096, 256], P('grp', 'seq'), may hold values from -6 to 6
- session_of_bin: int32 [8, 4096], P('grp', 'seq'), may hold values from 0 to 15, as said below
- session_slot: int32 [16], replicated, may hold values from 0 to 15, as said below
- readin_weight: bfloat16 [16, 256, 4096], P('grp'), may hold values from -0.375 to 0.375
- short_kernel: float32 [3, 2048], replicated, may hold values from -3.5 to 3.5
- long_filter: float32 [2048, 4096], P('seq')
- skip_gain: float32 [2048], P('seq'), may hold values from 0.5 to 1.5
- readout_weight: bfloat16 [16, 2048, 256], P('grp'), may hold values from -0.125 to 0.125
- out_grad: bfloat16 [8, 4096, 2048], P('grp', 'seq'), may hold values from -0.03125 to 0.03125
Outputs:
- denoised: bfloat16 [8, 4096, 256], P('grp', 'seq')
- filter_grad: float32 [2048, 4096], P('seq')
The draws below stay inside these ranges and needn't reach their ends.
Inputs may be any that keep to these rules, and one draw needn't show every extreme that they name: `session_slot`: each slot holds exactly one session. `session_of_bin`: each sequence is made of aligned runs of 16 bins of one session (trials); among the 128 bins of one device at most 32 belong to sessions whose slots lie in one aligned range of 2 slots, and in every such block some range takes exactly 32.
All inputs are finite; a program needn't handle non-finite values.
Results may differ from the reference program's by a relative error of at most 0.017.
Values may be sent and summed in bfloat16 or wider, within the bound.
No kernel may reach another device: no remote copies, remote signals or barrier semaphores. Data moves between devices by JAX's collectives and lax.ppermute only.
A program may use at most 128 MiB of HBM per device.

```python
import math
import jax
import jax.numpy as jnp
from jax import lax

D = 2048
C_IN = 256
TB = 128
TRIALS_DEV = 8
E_DEV = 2
KS = 3
LEN = 4096
SEQS = 8
SESSIONS = 16
TRIAL = 16


def slot_table(key):
    return jax.random.permutation(jax.random.fold_in(key, 11), SESSIONS).astype(jnp.int32)


def draw_session_slot(key, part):
    return slot_table(key)


def draw_session_of_bin(key, part):
    table = slot_table(key)
    inverse_map = jnp.zeros((SESSIONS,), jnp.int32).at[table].set(jnp.arange(SESSIONS, dtype=jnp.int32))
    block_count = SEQS * LEN // TB

    def one_block(block_index):
        block_key = jax.random.fold_in(jax.random.fold_in(key, 23), block_index)
        owner_key, order_key, local_key = jax.random.split(block_key, 3)
        owners = jax.random.permutation(owner_key, SEQS).astype(jnp.int32)
        trial_owner = owners[jnp.arange(TRIALS_DEV) // 2]
        trial_owner = jax.random.permutation(order_key, trial_owner)
        local_expert = jax.random.randint(local_key, (TRIALS_DEV,), 0, E_DEV).astype(jnp.int32)
        trial_session = inverse_map[trial_owner * E_DEV + local_expert]
        return jnp.repeat(trial_session, TRIAL, total_repeat_length=TB)
    return jax.vmap(one_block)(jnp.arange(block_count)).reshape(SEQS, LEN).astype(jnp.int32)


def draw_long_filter(key, part):
    rate_key, noise_key = jax.random.split(jax.random.fold_in(key, 37))
    low_log = math.log(1.0 / (4.0 * LEN))
    high_log = math.log(1.0 / 30.0)
    noise_part = jax.random.normal(noise_key, (D, LEN), jnp.float32)
    rates = jnp.exp(jax.random.uniform(rate_key, (D, 1), jnp.float32, low_log, high_log))
    lag_index = jnp.arange(LEN, dtype=jnp.float32)[None, :]
    amplitude = jnp.sqrt(jnp.expm1(-2.0 * rates) / jnp.expm1(-2.0 * rates * LEN))
    return (noise_part * jnp.exp(-rates * lag_index) * amplitude).astype(jnp.float32)


def level_of(rng, shape, cuts, low, largest):
    factor_of = 1.0
    for position, parts in cuts:
        steps = jax.random.uniform(jax.random.fold_in(jax.random.fold_in(rng, 6), position), (parts,), jnp.float32, low / len(cuts), largest / len(cuts))
        factor_of = factor_of * jnp.repeat(jnp.exp(steps), shape[position] // parts).reshape((-1,) + (1,) * (len(shape) - 1 - position))
    return factor_of


def gaussian(stream_key, dims, width, bound, cuts=(), held_as=jnp.bfloat16):
    result = width * jax.random.normal(stream_key, dims, jnp.float32)
    if cuts:
        result = result * level_of(stream_key, dims, cuts, -0.22, 0.18)
    return jnp.clip(result, -bound, bound).astype(held_as)


def setup_inputs(seed: int = 0) -> dict:
    key_list = jax.random.split(jax.random.key(seed), 10)
    spikes = gaussian(key_list[0], (SEQS, LEN, C_IN), 1.0, 6.0, ((0, 8), (1, 32)))
    session_of_bin = draw_session_of_bin(jax.random.fold_in(key_list[9], 71), 0)
    session_slot = draw_session_slot(jax.random.fold_in(key_list[9], 71), 0)
    readin_weight = gaussian(key_list[3], (SESSIONS, C_IN, 2 * D), C_IN ** -0.5, 0.375, ((0, 8),))
    short_kernel = gaussian(key_list[4], (KS, D), KS ** -0.5, 3.5, (), jnp.float32)
    long_filter = draw_long_filter(jax.random.fold_in(key_list[9], 71), 0)
    skip_gain = jnp.clip(0.5 + 1.0 * jax.random.uniform(key_list[6], (D,), jnp.float32) ** level_of(key_list[6], (D,), ((0, 32),), -0.2, 0.2), 0.5, 1.5)
    readout_weight = gaussian(key_list[7], (SESSIONS, D, C_IN), D ** -0.5, 0.125, ((0, 8),))
    out_grad = gaussian(key_list[8], (SEQS, LEN, D), (LEN * SEQS) ** -0.5, 0.03125, ((0, 8), (1, 32)))
    return {"spikes": spikes, "session_of_bin": session_of_bin, "session_slot": session_slot, "readin_weight": readin_weight, "short_kernel": short_kernel, "long_filter": long_filter, "skip_gain": skip_gain, "readout_weight": readout_weight, "out_grad": out_grad}


def reference(spikes, session_of_bin, session_slot, readin_weight, short_kernel, long_filter, skip_gain, readout_weight, out_grad):
    seq_count, seq_len, channels = spikes.shape
    model_width = short_kernel.shape[1]
    tap_count = short_kernel.shape[0]
    trial_count = seq_count * seq_len // TRIAL
    bin_slot = session_slot[session_of_bin]
    trial_slot = bin_slot.reshape(trial_count, TRIAL)[:, 0]

    def read_in(item):
        trial_rows, slot_index = item
        return jnp.dot(trial_rows, readin_weight[slot_index], preferred_element_type=jnp.float32).astype(jnp.bfloat16)

    streams = lax.map(read_in, (spikes.reshape(trial_count, TRIAL, channels), trial_slot))
    streams = streams.reshape(seq_count, seq_len, 2 * model_width)
    value_part = streams[:, :, :model_width]
    gate_part = streams[:, :, model_width:]
    padded = jnp.pad(value_part.astype(jnp.float32), ((0, 0), (tap_count - 1, 0), (0, 0)))
    conv_sum = jnp.zeros((seq_count, seq_len, model_width), jnp.float32)
    for tap_index in range(tap_count):
        offset = tap_count - 1 - tap_index
        conv_sum = conv_sum + short_kernel[tap_index] * padded[:, offset:offset + seq_len]
    conv_in = conv_sum.astype(jnp.bfloat16)
    padded_len = 2 * seq_len
    filter_spec = jnp.fft.rfft(long_filter, n=padded_len, axis=1).T

    def per_sequence(spec_total, item):
        conv_seq, gate_seq, grad_seq = item
        conv_float = conv_seq.astype(jnp.float32)
        conv_spec = jnp.fft.rfft(conv_float, n=padded_len, axis=0)
        long_part = jnp.fft.irfft(conv_spec * filter_spec, n=padded_len, axis=0)[:seq_len]
        mixed = (long_part + skip_gain[None, :] * conv_float).astype(jnp.bfloat16)
        gated_rows = (gate_seq.astype(jnp.float32) * mixed.astype(jnp.float32)).astype(jnp.bfloat16)
        mixed_grad = (grad_seq.astype(jnp.float32) * gate_seq.astype(jnp.float32)).astype(jnp.bfloat16)
        grad_spec = jnp.fft.rfft(mixed_grad.astype(jnp.float32), n=padded_len, axis=0)
        return spec_total + jnp.conj(conv_spec) * grad_spec, gated_rows

    spec_total, gated_all = lax.scan(per_sequence, jnp.zeros_like(filter_spec), (conv_in, gate_part, out_grad))
    filter_grad = jnp.fft.irfft(spec_total, n=padded_len, axis=0)[:seq_len].T

    def read_out(item):
        trial_rows, slot_index = item
        return jnp.dot(trial_rows, readout_weight[slot_index], preferred_element_type=jnp.float32).astype(jnp.bfloat16)

    denoised = lax.map(read_out, (gated_all.reshape(trial_count, TRIAL, model_width), trial_slot))
    denoised = denoised.reshape(seq_count, seq_len, channels)
    return denoised, filter_grad
```

```python
import functools

import jax
import jax.numpy as jnp
import numpy as np
from jax import lax
from jax.experimental import pallas as pl
from jax.experimental.pallas import tpu as pltpu
from jax.sharding import PartitionSpec as P

BLOCK = 128
TRIAL = 16
Z = 8
Y = 4
BLOCKS = Z * Y
CHANS = 64
LANE8 = 8
GROUPS = CHANS // LANE8
LENGTH = BLOCKS * BLOCK
PAD_ROWS = 16
Y_STEPS = (0, -1, 1, 2)
f32 = jnp.float32
bf16 = jnp.bfloat16


def transform_tables():
    slow = np.arange(BLOCKS)
    fast = np.arange(BLOCK)
    first = np.exp(-2j * np.pi * (np.outer(slow, slow) / BLOCKS + slow[None, :] / (4.0 * BLOCKS)))
    twist = np.exp(-2j * np.pi * (slow[:, None] + 0.25) * fast[None, :] / LENGTH)
    second = np.exp(-2j * np.pi * np.outer(fast, fast) / BLOCK)
    eye = np.eye(LANE8)
    spread_first = np.concatenate([np.kron(first.real, eye), np.kron(first.imag, eye)], 0)
    forward_second = np.block([[second.real, second.imag], [-second.imag, second.real]])
    back = second.conj()
    back_second = np.block([[back.real, back.imag], [-back.imag, back.real]])
    back_first = first.conj().T / LENGTH
    spread_back = np.concatenate([np.kron(back_first.real, eye), np.kron(-back_first.imag, eye)], 1)
    as_bf16 = lambda table: jnp.asarray(table.astype(np.float32), bf16)
    twists = np.stack([twist.real, twist.imag]).astype(np.float32)
    return (
        as_bf16(spread_first),
        as_bf16(forward_second),
        as_bf16(back_second),
        as_bf16(spread_back),
        jnp.asarray(twists),
    )


def twists_of(twist_ref):
    shape = (BLOCKS, LANE8, BLOCK)
    cosine = jnp.broadcast_to(twist_ref[0][:, None, :], shape).reshape(BLOCKS * LANE8, BLOCK)
    sine = jnp.broadcast_to(twist_ref[1][:, None, :], shape).reshape(BLOCKS * LANE8, BLOCK)
    return cosine, sine


def forward(signal, first_ref, second_ref, cosine, sine):
    rows = BLOCKS * LANE8
    part = jnp.dot(first_ref[...], signal.astype(bf16), preferred_element_type=f32)
    real, imag = part[:rows], part[rows:]
    turned = jnp.concatenate([real * cosine - imag * sine, real * sine + imag * cosine], 1)
    return jnp.dot(turned.astype(bf16), second_ref[...], preferred_element_type=f32)


def backward(real, imag, back_second_ref, back_first_ref, cosine, sine):
    both = jnp.concatenate([real, imag], 1).astype(bf16)
    part = jnp.dot(both, back_second_ref[...], preferred_element_type=f32)
    real, imag = part[:, :BLOCK], part[:, BLOCK:]
    turned = jnp.concatenate([real * cosine + imag * sine, imag * cosine - real * sine], 0)
    return jnp.dot(back_first_ref[...], turned.astype(bf16), preferred_element_type=f32)


def filter_kernel(filter_ref, first_ref, second_ref, twist_ref, spectrum_ref):
    cosine, sine = twists_of(twist_ref)

    def step(group, carry):
        rows = filter_ref[pl.ds(pl.multiple_of(group * LANE8, LANE8), LANE8), :]
        signal = jnp.concatenate([rows[:, i * BLOCK : (i + 1) * BLOCK] for i in range(BLOCKS)], 0)
        spectrum_ref[group] = forward(signal, first_ref, second_ref, cosine, sine)
        return carry

    lax.fori_loop(0, GROUPS, step, 0)


def read_in_kernel(chunk_ref, weight_ref, out_ref):
    blocks = chunk_ref.shape[0]
    slots = weight_ref.shape[0]
    width = weight_ref.shape[2]
    trials = BLOCK // TRIAL
    for index in range(blocks):
        rows = chunk_ref[index, :BLOCK, :]
        marks = chunk_ref[index, BLOCK:, :].astype(f32)[:trials, :width]
        marks = jnp.broadcast_to(marks[:, None, :], (trials, TRIAL, width)).reshape(BLOCK, width)
        chosen = jnp.zeros((BLOCK, width), f32)
        for slot in range(slots):
            product = jnp.dot(rows, weight_ref[slot], preferred_element_type=f32)
            chosen = jnp.where(marks == slot, product, chosen)
        out_ref[index] = chosen.T.astype(bf16)


def read_in(chunk, weights, ordinal):
    blocks = chunk.shape[0]
    width = weights.shape[2]
    flops = 2 * blocks * BLOCK * weights.shape[0] * weights.shape[1] * width
    return pl.pallas_call(
        read_in_kernel,
        out_shape=jax.ShapeDtypeStruct((blocks, width, BLOCK), bf16),
        in_specs=[pl.BlockSpec(memory_space=pltpu.VMEM)] * 2,
        out_specs=pl.BlockSpec(memory_space=pltpu.VMEM),
        compiler_params=pltpu.CompilerParams(vmem_limit_bytes=16 << 20),
        cost_estimate=pl.CostEstimate(flops=flops, bytes_accessed=chunk.size * 2 + weights.size * 2, transcendentals=0),
        name="read_in",
    )(chunk, weights)


def main_kernel(place_ref, taps_ref, gain_ref, filter_ref, first_ref, second_ref, back_second_ref, back_first_ref, twist_ref, *rest):
    chunk_refs = rest[:-5]
    gated_ref, gate_ref, spectrum_ref, value_all, gate_all = rest[-5:]
    z = place_ref[0]
    y = place_ref[1]
    steps = (0, -1, 1, -2, 2, -3, 3, 4)
    for chunk_ref, z_step in zip(chunk_refs, steps):
        for index, y_step in enumerate(Y_STEPS):
            block = lax.rem(z + (z_step + Z), Z) * Y + lax.rem(y + (y_step + Y), Y)
            both = chunk_ref[index].astype(f32)
            value_all[block] = both[:CHANS]
            gate_all[block] = both[CHANS:]
    cosine, sine = twists_of(twist_ref)
    lane = lax.broadcasted_iota(jnp.int32, (BLOCKS, LANE8, BLOCK), 2)
    rows = BLOCKS * LANE8

    def one_group(group):
        here = pl.ds(pl.multiple_of(group * LANE8, LANE8), LANE8)
        value = value_all[:, here, :]
        taps = taps_ref[:, here, :]
        total = taps[0][None] * value
        for shift in (1, 2):
            rolled = pltpu.roll(value.reshape(rows, BLOCK), shift, 1).reshape(BLOCKS, LANE8, BLOCK)
            before = jnp.concatenate([jnp.zeros((1, LANE8, BLOCK), f32), rolled[:-1]], 0)
            total = total + taps[shift][None] * jnp.where(lane < shift, before, rolled)
        signal = total.astype(bf16).astype(f32).reshape(rows, BLOCK)
        spectrum = forward(signal, first_ref, second_ref, cosine, sine)
        spectrum_ref[group] = spectrum
        weight = filter_ref[group]
        real = spectrum[:, :BLOCK] * weight[:, :BLOCK] - spectrum[:, BLOCK:] * weight[:, BLOCK:]
        imag = spectrum[:, :BLOCK] * weight[:, BLOCK:] + spectrum[:, BLOCK:] * weight[:, :BLOCK]
        long_part = backward(real, imag, back_second_ref, back_first_ref, cosine, sine)
        mixed = long_part.reshape(BLOCKS, LANE8, BLOCK) + gain_ref[here, :][None] * signal.reshape(BLOCKS, LANE8, BLOCK)
        gate = gate_all[:, here, :]
        return gate * mixed.astype(bf16).astype(f32), gate

    def step(pair, carry):
        gated_low, gate_low = one_group(pair * 2)
        gated_high, gate_high = one_group(pair * 2 + 1)
        here = pl.ds(pl.multiple_of(pair * 2 * LANE8, 2 * LANE8), 2 * LANE8)
        gated_ref[:, here, :] = jnp.concatenate([gated_low, gated_high], 1).astype(bf16)
        gate_ref[:, here, :] = jnp.concatenate([gate_low, gate_high], 1).astype(bf16)
        return carry

    lax.fori_loop(0, GROUPS // 2, step, 0)


def gradient_kernel(grad_ref, gate_ref, spectrum_ref, first_ref, second_ref, back_second_ref, back_first_ref, twist_ref, out_ref):
    cosine, sine = twists_of(twist_ref)
    rows = BLOCKS * LANE8

    def one_group(product, group):
        grad_spectrum = forward(product.reshape(rows, BLOCK), first_ref, second_ref, cosine, sine)
        spectrum = spectrum_ref[group]
        real = spectrum[:, :BLOCK] * grad_spectrum[:, :BLOCK] + spectrum[:, BLOCK:] * grad_spectrum[:, BLOCK:]
        imag = spectrum[:, :BLOCK] * grad_spectrum[:, BLOCK:] - spectrum[:, BLOCK:] * grad_spectrum[:, :BLOCK]
        result = backward(real, imag, back_second_ref, back_first_ref, cosine, sine)
        return jnp.concatenate([result[i * LANE8 : (i + 1) * LANE8] for i in range(BLOCKS)], 1)

    def step(pair, carry):
        here = pl.ds(pl.multiple_of(pair * 2 * LANE8, 2 * LANE8), 2 * LANE8)
        product = grad_ref[:, here, :].astype(f32) * gate_ref[:, here, :].astype(f32)
        product = product.astype(bf16).astype(f32)
        low = one_group(product[:, :LANE8], pair * 2)
        high = one_group(product[:, LANE8:], pair * 2 + 1)
        out_ref[here, :] = jnp.concatenate([low, high], 0).astype(bf16)
        return carry

    lax.fori_loop(0, GROUPS // 2, step, 0)


def read_out_kernel(place_ref, rows_ref, chunk_ref, weight_ref, out_ref):
    y = place_ref[1]
    trials = BLOCK // TRIAL
    slots = weight_ref.shape[0]
    inner = weight_ref.shape[1]
    width = weight_ref.shape[2]
    pieces = []
    marks = []
    for index, y_step in enumerate(Y_STEPS):
        block = lax.rem(y + (y_step + Y), Y)
        pieces.append(rows_ref[:, block, :, :].reshape(inner, BLOCK).T)
        mark = chunk_ref[index, BLOCK:, :].astype(f32)[:trials, :width]
        marks.append(jnp.broadcast_to(mark[:, None, :], (trials, TRIAL, width)).reshape(BLOCK, width))
    rows = jnp.concatenate(pieces, 0)
    marks = jnp.concatenate(marks, 0)
    chosen = jnp.zeros((Y * BLOCK, width), f32)
    for slot in range(slots):
        product = jnp.dot(rows, weight_ref[slot], preferred_element_type=f32)
        chosen = jnp.where(marks == slot, product, chosen)
    for index, y_step in enumerate(Y_STEPS):
        block = lax.rem(y + (y_step + Y), Y)
        out_ref[block] = chosen[index * BLOCK : (index + 1) * BLOCK].astype(bf16)


def along_y(value, step):
    return lax.ppermute(value, "seq", [(z * Y + y, z * Y + (y + step) % Y) for z in range(Z) for y in range(Y)])


def along_z(value, step):
    return lax.ppermute(value, "seq", [(z * Y + y, (z + step) % Z * Y + y) for z in range(Z) for y in range(Y)])


def whole(count):
    return [pl.BlockSpec(memory_space=pltpu.VMEM)] * count


def local(spikes, session_of_bin, session_slot, readin_weight, short_kernel, long_filter, skip_gain, readout_weight, out_grad):
    experts_here = readin_weight.shape[0]
    in_chans = spikes.shape[2]
    model_width = short_kernel.shape[1]
    place = lax.axis_index("seq")
    scalar = pl.BlockSpec(memory_space=pltpu.SMEM)
    z_groups = [[z * Y + y for z in range(Z)] for y in range(Y)]
    y_groups = [[z * Y + y for y in range(Y)] for z in range(Z)]
    coords = jnp.stack([place // Y, place % Y]).astype(jnp.int32)
    first, second, back_second, back_first, twists = transform_tables()

    split = readin_weight.reshape(experts_here, in_chans, 2, BLOCKS, CHANS)
    own = lax.dynamic_index_in_dim(split, place, 3, keepdims=False).reshape(experts_here, in_chans, 2 * CHANS)
    in_weights = lax.all_gather(own, "grp", axis=0, tiled=True)
    split = readout_weight.reshape(experts_here, Z, Y, CHANS, in_chans)
    own = lax.dynamic_index_in_dim(split, place % Y, 2, keepdims=False).reshape(experts_here, Z * CHANS, in_chans)
    out_weights = lax.all_gather(own, "grp", axis=0, tiled=True)

    sessions = session_of_bin[0, ::TRIAL]
    matches = sessions[:, None] == jnp.arange(session_slot.shape[0], dtype=jnp.int32)[None, :]
    slots = jnp.sum(jnp.where(matches, session_slot[None, :], 0), axis=1)
    marks = jnp.broadcast_to(slots.astype(bf16)[:, None], (slots.shape[0], in_chans))
    padding = jnp.zeros((PAD_ROWS - slots.shape[0], in_chans), bf16)
    block = jnp.concatenate([spikes[0], marks, padding], 0)
    chunk = jnp.stack([block, along_y(block, 1), along_y(block, -1), along_y(block, 2)])
    chunks = [chunk]
    right = left = chunk
    for _ in range(3):
        right, left = along_z(right, 1), along_z(left, -1)
        chunks += [right, left]
    last = [along_z(right[: Y // 2], 1), along_z(left[Y // 2 :], -1)]
    parts = [read_in(piece, in_weights, 0) for piece in chunks]
    parts.append(jnp.concatenate([read_in(piece, in_weights, 0) for piece in last], 0))

    spectrum_shape = jax.ShapeDtypeStruct((GROUPS, BLOCKS * LANE8, 2 * BLOCK), f32)
    plane = (BLOCKS, CHANS, BLOCK)
    params = pltpu.CompilerParams(vmem_limit_bytes=32 << 20)
    work = 2 * GROUPS * (512 * 256 * 128 + 256 * 256 * 256)
    filter_spectrum = pl.pallas_call(
        filter_kernel,
        out_shape=spectrum_shape,
        in_specs=whole(4),
        out_specs=whole(1)[0],
        compiler_params=params,
        cost_estimate=pl.CostEstimate(flops=work, bytes_accessed=4 << 20, transcendentals=0),
        name="filter_transform",
    )(long_filter, first, second, twists)

    taps = lax.dynamic_slice_in_dim(short_kernel, place * CHANS, CHANS, 1)
    taps = jnp.broadcast_to(taps[:, :, None], (short_kernel.shape[0], CHANS, BLOCK))
    gains = jnp.broadcast_to(skip_gain[:, None], (CHANS, BLOCK))
    gated, gates, spectrum = pl.pallas_call(
        main_kernel,
        out_shape=(jax.ShapeDtypeStruct(plane, bf16), jax.ShapeDtypeStruct(plane, bf16), spectrum_shape),
        in_specs=[scalar] + whole(8 + len(parts)),
        out_specs=tuple(whole(3)),
        scratch_shapes=[pltpu.VMEM(plane, f32), pltpu.VMEM(plane, f32)],
        compiler_params=params,
        cost_estimate=pl.CostEstimate(flops=2 * work, bytes_accessed=8 << 20, transcendentals=0),
        name="long_convolution",
    )(coords, taps, gains, filter_spectrum, first, second, back_second, back_first, twists, *parts)

    arrived = lax.all_to_all(gated.reshape(Z, Y, CHANS, BLOCK), "seq", split_axis=0, concat_axis=0, tiled=True, axis_index_groups=z_groups)
    partial = pl.pallas_call(
        read_out_kernel,
        out_shape=jax.ShapeDtypeStruct((Y, BLOCK, in_chans), bf16),
        in_specs=[scalar] + whole(3),
        out_specs=whole(1)[0],
        compiler_params=params,
        cost_estimate=pl.CostEstimate(flops=2 * 512 * 512 * 4096, bytes_accessed=6 << 20, transcendentals=0),
        name="read_out",
    )(coords, arrived, chunk, out_weights)
    pieces = lax.all_to_all(partial, "seq", split_axis=0, concat_axis=0, tiled=True, axis_index_groups=y_groups)
    denoised = jnp.sum(pieces.astype(f32), 0).astype(bf16)

    turned = out_grad[0].T.reshape(BLOCKS, CHANS, BLOCK)
    grads = lax.all_to_all(turned, "seq", split_axis=0, concat_axis=0, tiled=True)
    own_grad = pl.pallas_call(
        gradient_kernel,
        out_shape=jax.ShapeDtypeStruct((CHANS, LENGTH), bf16),
        in_specs=whole(8),
        out_specs=whole(1)[0],
        compiler_params=params,
        cost_estimate=pl.CostEstimate(flops=2 * work, bytes_accessed=5 << 20, transcendentals=0),
        name="filter_gradient",
    )(grads, gates, spectrum, first, second, back_second, back_first, twists)
    all_grads = lax.all_gather(own_grad, "grp", axis=0, tiled=False)
    filter_grad = jnp.sum(all_grads.astype(f32), 0)
    return denoised[None], filter_grad


def solution(mesh):
    placed = (
        P("grp", "seq", None),
        P("grp", "seq"),
        P(),
        P("grp", None, None),
        P(),
        P("seq", None),
        P("seq"),
        P("grp", None, None),
        P("grp", "seq", None),
    )
    return jax.shard_map(
        local,
        mesh=mesh,
        in_specs=placed,
        out_specs=(P("grp", "seq", None), P("seq", None)),
        check_vma=False,
    )
```

```python
import jax
import jax.numpy as jnp
import numpy as np
from jax import lax
from jax.experimental import pallas as pl
from jax.experimental.pallas import tpu as pltpu
from jax.sharding import PartitionSpec as P

BLOCK = 128
TRIAL = 16
Z = 8
Y = 4
BLOCKS = Z * Y
CHANS = 64
LANE8 = 8
GROUPS = CHANS // LANE8
LENGTH = BLOCKS * BLOCK
Y_STEPS = (0, -1, 1, 2)
Z_STEPS = (0, -1, 1, -2, 2, -3, 3, 4)
f32 = jnp.float32
bf16 = jnp.bfloat16


def transform_tables():
    slow = np.arange(BLOCKS)
    fast = np.arange(BLOCK)
    first = np.exp(-2j * np.pi * (np.outer(slow, slow) / BLOCKS + slow[None, :] / (4.0 * BLOCKS)))
    twist = np.exp(-2j * np.pi * (slow[:, None] + 0.25) * fast[None, :] / LENGTH)
    second = np.exp(-2j * np.pi * np.outer(fast, fast) / BLOCK)
    eye = np.eye(LANE8)
    spread_first = np.concatenate([np.kron(first.real, eye), np.kron(first.imag, eye)], 0)
    forward_second = np.block([[second.real, second.imag], [-second.imag, second.real]])
    back = second.conj()
    back_second = np.block([[back.real, back.imag], [-back.imag, back.real]])
    back_first = first.conj().T / LENGTH
    spread_back = np.concatenate([np.kron(back_first.real, eye), np.kron(-back_first.imag, eye)], 1)
    as_bf16 = lambda table: jnp.asarray(table.astype(np.float32), bf16)
    twists = np.stack([twist.real, twist.imag]).astype(np.float32)
    return (
        as_bf16(spread_first),
        as_bf16(forward_second),
        as_bf16(back_second),
        as_bf16(spread_back),
        jnp.asarray(twists),
    )


def twists_of(twist_ref):
    shape = (BLOCKS, LANE8, BLOCK)
    cosine = jnp.broadcast_to(twist_ref[0][:, None, :], shape).reshape(BLOCKS * LANE8, BLOCK)
    sine = jnp.broadcast_to(twist_ref[1][:, None, :], shape).reshape(BLOCKS * LANE8, BLOCK)
    return cosine, sine


def forward(signal, first_ref, second_ref, cosine, sine):
    rows = BLOCKS * LANE8
    part = jnp.dot(first_ref[...], signal.astype(bf16), preferred_element_type=f32)
    real, imag = part[:rows], part[rows:]
    turned = jnp.concatenate([real * cosine - imag * sine, real * sine + imag * cosine], 1)
    return jnp.dot(turned.astype(bf16), second_ref[...], preferred_element_type=f32)


def backward(real, imag, back_second_ref, back_first_ref, cosine, sine):
    both = jnp.concatenate([real, imag], 1).astype(bf16)
    part = jnp.dot(both, back_second_ref[...], preferred_element_type=f32)
    real, imag = part[:, :BLOCK], part[:, BLOCK:]
    turned = jnp.concatenate([real * cosine + imag * sine, imag * cosine - real * sine], 0)
    return jnp.dot(back_first_ref[...], turned.astype(bf16), preferred_element_type=f32)


def filter_kernel(filter_ref, first_ref, second_ref, twist_ref, spectrum_ref):
    cosine, sine = twists_of(twist_ref)

    def step(group, carry):
        rows = filter_ref[pl.ds(pl.multiple_of(group * LANE8, LANE8), LANE8), :]
        signal = jnp.concatenate([rows[:, i * BLOCK : (i + 1) * BLOCK] for i in range(BLOCKS)], 0)
        spectrum_ref[group] = forward(signal, first_ref, second_ref, cosine, sine)
        return carry

    lax.fori_loop(0, GROUPS, step, 0)


def start_all(copies):
    for copy in copies:
        copy.start()


def wait_all(copies):
    for copy in copies:
        copy.wait()


def weight_copies(weight_hbm, weight, sems):
    copies = []
    for slot in range(weight_hbm.shape[0]):
        lanes = pl.ds(slot % 2 * 2 * CHANS, 2 * CHANS)
        copies.append(pltpu.make_async_copy(weight_hbm.at[slot], weight.at[slot // 2, :, lanes], sems.at[slot]))
    return copies


def project(rows_ref, start, weight):
    width = 2 * CHANS
    rows = rows_ref[pl.ds(start, 2), :BLOCK, :].reshape(2 * BLOCK, rows_ref.shape[2])
    marks = rows_ref[pl.ds(start, 2), BLOCK:, :].astype(f32)[:, :, :width].reshape(2 * BLOCK // TRIAL, width)
    marks = jnp.broadcast_to(marks[:, None, :], (2 * BLOCK // TRIAL, TRIAL, width)).reshape(2 * BLOCK, width)
    chosen = jnp.zeros((2 * BLOCK, width), f32)
    for pair in range(weight.shape[0]):
        product = jnp.dot(rows, weight[pair], preferred_element_type=f32)
        chosen = jnp.where(marks == 2 * pair, product[:, :width], chosen)
        chosen = jnp.where(marks == 2 * pair + 1, product[:, width:], chosen)
    return chosen[:BLOCK].T.astype(bf16), chosen[BLOCK:].T.astype(bf16)


def read_in_kernel(weight_hbm, *rest):
    chunk_refs = rest[:-5]
    out_ref, rows, weight, weight_sems, sems = rest[-5:]
    loads = weight_copies(weight_hbm, weight, weight_sems)
    for index, chunk in enumerate(chunk_refs):
        loads.append(pltpu.make_async_copy(chunk, rows.at[pl.ds(index * Y, Y)], sems.at[index]))
    start_all(loads)
    wait_all(loads)

    def step(pair, carry):
        low, high = project(rows, pair * 2, weight)
        out_ref[pair * 2] = low
        out_ref[pair * 2 + 1] = high
        return carry

    lax.fori_loop(0, rows.shape[0] // 2, step, 0)


def read_in(chunks, weights):
    blocks = len(chunks) * Y
    in_chans = weights.shape[1]
    width = weights.shape[2]
    flops = 2 * blocks * BLOCK * weights.shape[0] * in_chans * width
    return pl.pallas_call(
        read_in_kernel,
        out_shape=jax.ShapeDtypeStruct((blocks, width, BLOCK), bf16),
        in_specs=[pl.BlockSpec(memory_space=pltpu.HBM)] * (1 + len(chunks)),
        out_specs=whole(1)[0],
        scratch_shapes=[
            pltpu.VMEM((blocks,) + chunks[0].shape[1:], bf16),
            pltpu.VMEM((weights.shape[0] // 2, in_chans, 2 * width), bf16),
            pltpu.SemaphoreType.DMA((weights.shape[0],)),
            pltpu.SemaphoreType.DMA((len(chunks),)),
        ],
        compiler_params=pltpu.CompilerParams(vmem_limit_bytes=60 << 20),
        cost_estimate=pl.CostEstimate(flops=flops, bytes_accessed=4 << 20, transcendentals=0),
        name="read_in",
    )(weights, *chunks)


def block_of(place_ref, index):
    z = lax.rem(place_ref[0] + (Z_STEPS[index // Y] + Z), Z)
    y = lax.rem(place_ref[1] + (Y_STEPS[index % Y] + Y), Y)
    return z * Y + y


def main_kernel(place_ref, taps_ref, gain_ref, twist_ref, early_hbm, right_hbm, left_hbm, last_right_hbm, last_left_hbm, weight_hbm, filter_hbm, grad_hbm, *rest):
    table_hbms = rest[:4]
    gated_ref, out_ref, both, rows, weight, spectra, grad_all, *rest = rest[4:]
    tables = rest[:4]
    weight_sems, row_sems, early_sems, sems = rest[4:]
    half = Y // 2
    late = [
        pltpu.make_async_copy(right_hbm, rows.at[pl.ds(0, Y)], row_sems.at[0]),
        pltpu.make_async_copy(left_hbm, rows.at[pl.ds(Y, Y)], row_sems.at[1]),
        pltpu.make_async_copy(last_right_hbm, rows.at[pl.ds(2 * Y, half)], row_sems.at[2]),
        pltpu.make_async_copy(last_left_hbm, rows.at[pl.ds(2 * Y + half, half)], row_sems.at[3]),
    ] + weight_copies(weight_hbm, weight, weight_sems)
    early = early_hbm.shape[0]
    others = [
        pltpu.make_async_copy(early_hbm.at[index], both.at[block_of(place_ref, index)], early_sems.at[index])
        for index in range(early)
    ]
    pairs = [(filter_hbm, spectra), (grad_hbm, grad_all)] + list(zip(table_hbms, tables))
    others += [pltpu.make_async_copy(source, target, sems.at[index]) for index, (source, target) in enumerate(pairs)]
    start_all(late)
    start_all(others)
    wait_all(late)
    for index in range(0, rows.shape[0], 2):
        low, high = project(rows, index, weight)
        both[block_of(place_ref, early + index)] = low
        both[block_of(place_ref, early + index + 1)] = high
    cosine, sine = twists_of(twist_ref)
    lane = lax.broadcasted_iota(jnp.int32, (BLOCKS, LANE8, BLOCK), 2)
    count = BLOCKS * LANE8
    cube = (BLOCKS, LANE8, BLOCK)
    wait_all(others)
    first_ref, second_ref, back_second_ref, back_first_ref = tables

    def one_group(group, value, gate, grads):
        here = pl.ds(pl.multiple_of(group * LANE8, LANE8), LANE8)
        taps = taps_ref[:, here, :]
        total = taps[0][None] * value
        for shift in (1, 2):
            rolled = pltpu.roll(value.reshape(count, BLOCK), shift, 1).reshape(cube)
            before = jnp.concatenate([jnp.zeros((1, LANE8, BLOCK), f32), rolled[:-1]], 0)
            total = total + taps[shift][None] * jnp.where(lane < shift, before, rolled)
        signal = total.astype(bf16).astype(f32).reshape(count, BLOCK)
        spectrum = forward(signal, first_ref, second_ref, cosine, sine)
        own_re, own_im = spectrum[:, :BLOCK], spectrum[:, BLOCK:]
        weight = spectra[group]
        real = own_re * weight[:, :BLOCK] - own_im * weight[:, BLOCK:]
        imag = own_re * weight[:, BLOCK:] + own_im * weight[:, :BLOCK]
        long_part = backward(real, imag, back_second_ref, back_first_ref, cosine, sine)
        mixed = long_part.reshape(cube) + gain_ref[here, :][None] * signal.reshape(cube)
        gated = gate * mixed.astype(bf16).astype(f32)
        mixed_grad = (grads * gate).reshape(count, BLOCK)
        turned = forward(mixed_grad, first_ref, second_ref, cosine, sine)
        real = own_re * turned[:, :BLOCK] + own_im * turned[:, BLOCK:]
        imag = own_re * turned[:, BLOCK:] - own_im * turned[:, :BLOCK]
        result = backward(real, imag, back_second_ref, back_first_ref, cosine, sine)
        return gated, jnp.concatenate([result[i * LANE8 : (i + 1) * LANE8] for i in range(BLOCKS)], 1)

    def step(pair, carry):
        here = pl.ds(pl.multiple_of(pair * 2 * LANE8, 2 * LANE8), 2 * LANE8)
        there = pl.ds(pl.multiple_of(CHANS + pair * 2 * LANE8, 2 * LANE8), 2 * LANE8)
        value = both[:, here, :].astype(f32)
        gate = both[:, there, :].astype(f32)
        grads = grad_all[:, here, :].astype(f32)
        gated_low, low = one_group(pair * 2, value[:, :LANE8], gate[:, :LANE8], grads[:, :LANE8])
        gated_high, high = one_group(pair * 2 + 1, value[:, LANE8:], gate[:, LANE8:], grads[:, LANE8:])
        gated_ref[:, here, :] = jnp.concatenate([gated_low, gated_high], 1).astype(bf16)
        out_ref[here, :] = jnp.concatenate([low, high], 0).astype(bf16)
        return carry

    lax.fori_loop(0, GROUPS // 2, step, 0)


def read_out_kernel(place_ref, rows_ref, mark_ref, weight_hbm, out_ref, weight, sems):
    y = place_ref[1]
    trials = BLOCK // TRIAL
    slots, inner, width = weight.shape
    loads = [pltpu.make_async_copy(weight_hbm.at[slot], weight.at[slot], sems.at[slot]) for slot in range(slots)]
    start_all(loads)
    pieces = []
    marks = []
    for index, y_step in enumerate(Y_STEPS):
        block = lax.rem(y + (y_step + Y), Y)
        pieces.append(rows_ref[:, block, :, :].reshape(inner, BLOCK).T)
        mark = mark_ref[index].astype(f32)
        marks.append(jnp.broadcast_to(mark[:, None, :], (trials, TRIAL, width)).reshape(BLOCK, width))
    rows = jnp.concatenate(pieces, 0)
    marks = jnp.concatenate(marks, 0)
    chosen = jnp.zeros((Y * BLOCK, width), f32)
    for slot in range(slots):
        loads[slot].wait()
        product = jnp.dot(rows, weight[slot], preferred_element_type=f32)
        chosen = jnp.where(marks == slot, product, chosen)
    for index, y_step in enumerate(Y_STEPS):
        block = lax.rem(y + (y_step + Y), Y)
        out_ref[block] = chosen[index * BLOCK : (index + 1) * BLOCK].astype(bf16)


def sum_kernel(parts_ref, out_ref):
    total = parts_ref[0].astype(f32)
    for index in range(1, parts_ref.shape[0]):
        total = total + parts_ref[index].astype(f32)
    out_ref[...] = total


def along_y(value, step):
    return lax.ppermute(value, "seq", [(z * Y + y, z * Y + (y + step) % Y) for z in range(Z) for y in range(Y)])


def along_z(value, step):
    return lax.ppermute(value, "seq", [(z * Y + y, (z + step) % Z * Y + y) for z in range(Z) for y in range(Y)])


def whole(count):
    return [pl.BlockSpec(memory_space=pltpu.VMEM)] * count


def local(spikes, session_of_bin, session_slot, readin_weight, short_kernel, long_filter, skip_gain, readout_weight, out_grad):
    experts_here = readin_weight.shape[0]
    in_chans = spikes.shape[2]
    model_width = short_kernel.shape[1]
    place = lax.axis_index("seq")
    scalar = pl.BlockSpec(memory_space=pltpu.SMEM)
    z_groups = [[z * Y + y for z in range(Z)] for y in range(Y)]
    y_groups = [[z * Y + y for y in range(Y)] for z in range(Z)]
    coords = jnp.stack([place // Y, place % Y]).astype(jnp.int32)
    first, second, back_second, back_first, twists = transform_tables()

    own = jnp.concatenate(
        [lax.dynamic_slice_in_dim(readin_weight, start + place * CHANS, CHANS, 2) for start in (0, model_width)], 2
    )
    in_weights = lax.all_gather(own, "grp", axis=0, tiled=True)
    split = readout_weight.reshape(experts_here, Z, Y, CHANS, in_chans)
    own = lax.dynamic_index_in_dim(split, place % Y, 2, keepdims=False).reshape(experts_here, Z * CHANS, in_chans)
    out_weights = lax.all_gather(own, "grp", axis=0, tiled=True)

    sessions = session_of_bin[0, ::TRIAL]
    matches = sessions[:, None] == jnp.arange(session_slot.shape[0], dtype=jnp.int32)[None, :]
    slots = jnp.sum(jnp.where(matches, session_slot[None, :], 0), axis=1)
    marks = jnp.broadcast_to(slots.astype(bf16)[:, None], (slots.shape[0], in_chans))
    block = jnp.concatenate([spikes[0], marks], 0)
    chunk = jnp.stack([block, along_y(block, 1), along_y(block, -1), along_y(block, 2)])
    chunks = [chunk]
    right = left = chunk
    turned = out_grad[0].T.reshape(BLOCKS, CHANS, BLOCK)
    for _ in range(3):
        right, left = along_z(right, 1), along_z(left, -1)
        chunks += [right, left]
    early = read_in(chunks[:5], in_weights)
    right, left, turned, early = lax.optimization_barrier((right, left, turned, early))
    last_right, last_left = along_z(right[: Y // 2], 1), along_z(left[Y // 2 :], -1)
    grads = lax.all_to_all(turned, "seq", split_axis=0, concat_axis=0, tiled=True)

    spectrum_shape = jax.ShapeDtypeStruct((GROUPS, BLOCKS * LANE8, 2 * BLOCK), f32)
    plane = (BLOCKS, CHANS, BLOCK)
    params = pltpu.CompilerParams(vmem_limit_bytes=60 << 20)
    work = 2 * GROUPS * (512 * 256 * 128 + 256 * 256 * 256)
    filter_spectrum = pl.pallas_call(
        filter_kernel,
        out_shape=spectrum_shape,
        in_specs=whole(4),
        out_specs=whole(1)[0],
        compiler_params=params,
        cost_estimate=pl.CostEstimate(flops=work, bytes_accessed=4 << 20, transcendentals=0),
        name="filter_transform",
    )(long_filter, first, second, twists)

    taps = lax.dynamic_slice_in_dim(short_kernel, place * CHANS, CHANS, 1)
    taps = jnp.broadcast_to(taps[:, :, None], (short_kernel.shape[0], CHANS, BLOCK))
    gains = jnp.broadcast_to(skip_gain[:, None], (CHANS, BLOCK))
    tables = (first, second, back_second, back_first)
    late_rows = 2 * Y + Y
    gated, own_grad = pl.pallas_call(
        main_kernel,
        out_shape=(jax.ShapeDtypeStruct(plane, bf16), jax.ShapeDtypeStruct((CHANS, LENGTH), bf16)),
        in_specs=[scalar] + whole(3) + [pl.BlockSpec(memory_space=pltpu.HBM)] * 12,
        out_specs=tuple(whole(2)),
        scratch_shapes=[
            pltpu.VMEM((BLOCKS, 2 * CHANS, BLOCK), bf16),
            pltpu.VMEM((late_rows,) + chunk.shape[1:], bf16),
            pltpu.VMEM((in_weights.shape[0] // 2, in_chans, 4 * CHANS), bf16),
            pltpu.VMEM(spectrum_shape.shape, f32),
            pltpu.VMEM(plane, bf16),
        ]
        + [pltpu.VMEM(table.shape, bf16) for table in tables]
        + [pltpu.SemaphoreType.DMA((count,)) for count in (in_weights.shape[0], 4, early.shape[0], 6)],
        compiler_params=pltpu.CompilerParams(vmem_limit_bytes=60 << 20),
        cost_estimate=pl.CostEstimate(flops=4 * work, bytes_accessed=8 << 20, transcendentals=0),
        name="long_convolution",
    )(coords, taps, gains, twists, early, right, left, last_right, last_left, in_weights, filter_spectrum, grads, *tables)
    all_grads = lax.all_gather(own_grad, "grp", axis=0, tiled=False)

    arrived = lax.all_to_all(gated.reshape(Z, Y, CHANS, BLOCK), "seq", split_axis=0, concat_axis=0, tiled=True, axis_index_groups=z_groups)
    partial = pl.pallas_call(
        read_out_kernel,
        out_shape=jax.ShapeDtypeStruct((Y, BLOCK, in_chans), bf16),
        in_specs=[scalar] + whole(2) + [pl.BlockSpec(memory_space=pltpu.HBM)],
        out_specs=whole(1)[0],
        scratch_shapes=[pltpu.VMEM(out_weights.shape, bf16), pltpu.SemaphoreType.DMA((out_weights.shape[0],))],
        compiler_params=pltpu.CompilerParams(vmem_limit_bytes=60 << 20),
        cost_estimate=pl.CostEstimate(flops=2 * 512 * 512 * 4096, bytes_accessed=6 << 20, transcendentals=0),
        name="read_out",
    )(coords, arrived, chunk[:, BLOCK:, :], out_weights)
    pieces = lax.all_to_all(partial, "seq", split_axis=0, concat_axis=0, tiled=True, axis_index_groups=y_groups)
    denoised = jnp.sum(pieces.astype(f32), 0).astype(bf16)

    step = 2 * LANE8
    filter_grad = pl.pallas_call(
        sum_kernel,
        out_shape=jax.ShapeDtypeStruct((CHANS, LENGTH), f32),
        grid=(CHANS // step,),
        in_specs=[pl.BlockSpec((all_grads.shape[0], step, LENGTH), lambda i: (0, i, 0))],
        out_specs=pl.BlockSpec((step, LENGTH), lambda i: (i, 0)),
        compiler_params=params,
        cost_estimate=pl.CostEstimate(flops=all_grads.size, bytes_accessed=5 << 20, transcendentals=0),
        name="sum_gradients",
    )(all_grads)
    return denoised[None], filter_grad


def solution(mesh):
    placed = (
        P("grp", "seq", None),
        P("grp", "seq"),
        P(),
        P("grp", None, None),
        P(),
        P("seq", None),
        P("seq"),
        P("grp", None, None),
        P("grp", "seq", None),
    )
    return jax.shard_map(
        local,
        mesh=mesh,
        in_specs=placed,
        out_specs=(P("grp", "seq", None), P("seq", None)),
        check_vma=False,
    )
```

```python
import jax
import jax.numpy as jnp
import numpy as np
from jax import lax
from jax.experimental import pallas as pl
from jax.experimental.pallas import tpu as pltpu
from jax.sharding import PartitionSpec as P

BLOCK = 128
TRIAL = 16
Z = 8
Y = 4
BLOCKS = Z * Y
CHANS = 64
LANE8 = 8
GROUPS = CHANS // LANE8
LENGTH = BLOCKS * BLOCK
Y_STEPS = (0, -1, 1, 2)
Z_STEPS = (0, -1, 1, -2, 2, -3, 3, 4)
f32 = jnp.float32
bf16 = jnp.bfloat16


def transform_tables():
    slow = np.arange(BLOCKS)
    fast = np.arange(BLOCK)
    first = np.exp(-2j * np.pi * (np.outer(slow, slow) / BLOCKS + slow[None, :] / (4.0 * BLOCKS)))
    twist = np.exp(-2j * np.pi * (slow[:, None] + 0.25) * fast[None, :] / LENGTH)
    second = np.exp(-2j * np.pi * np.outer(fast, fast) / BLOCK)
    eye = np.eye(LANE8)
    spread_first = np.concatenate([np.kron(first.real, eye), np.kron(first.imag, eye)], 0)
    forward_second = np.block([[second.real, second.imag], [-second.imag, second.real]])
    back = second.conj()
    back_second = np.block([[back.real, back.imag], [-back.imag, back.real]])
    back_first = first.conj().T / LENGTH
    spread_back = np.concatenate([np.kron(back_first.real, eye), np.kron(-back_first.imag, eye)], 1)
    as_bf16 = lambda table: jnp.asarray(table.astype(np.float32), bf16)
    twists = np.stack([twist.real, twist.imag]).astype(np.float32)
    return (
        as_bf16(spread_first),
        as_bf16(forward_second),
        as_bf16(back_second),
        as_bf16(spread_back),
        jnp.asarray(twists),
    )


def twists_of(twist_ref):
    shape = (BLOCKS, LANE8, BLOCK)
    cosine = jnp.broadcast_to(twist_ref[0][:, None, :], shape).reshape(BLOCKS * LANE8, BLOCK)
    sine = jnp.broadcast_to(twist_ref[1][:, None, :], shape).reshape(BLOCKS * LANE8, BLOCK)
    return cosine, sine


def forward(low, high, first_ref, second_ref, cosine, sine):
    rows = BLOCKS * LANE8
    signals = jnp.concatenate([low, high], 1).astype(bf16)
    part = jnp.dot(first_ref[...], signals, preferred_element_type=f32)
    turned = []
    for lanes in (slice(0, BLOCK), slice(BLOCK, 2 * BLOCK)):
        real, imag = part[:rows, lanes], part[rows:, lanes]
        turned.append(jnp.concatenate([real * cosine - imag * sine, real * sine + imag * cosine], 1))
    return jnp.dot(jnp.concatenate(turned, 0).astype(bf16), second_ref[...], preferred_element_type=f32)


def backward(spectra, back_second_ref, back_first_ref, cosine, sine):
    rows = BLOCKS * LANE8
    part = jnp.dot(spectra.astype(bf16), back_second_ref[...], preferred_element_type=f32)
    turned = []
    for start in (0, rows):
        real, imag = part[start : start + rows, :BLOCK], part[start : start + rows, BLOCK:]
        turned.append(jnp.concatenate([real * cosine + imag * sine, imag * cosine - real * sine], 0))
    return jnp.dot(back_first_ref[...], jnp.concatenate(turned, 1).astype(bf16), preferred_element_type=f32)


def filter_kernel(filter_ref, first_ref, second_ref, twist_ref, spectrum_ref):
    cosine, sine = twists_of(twist_ref)
    rows = BLOCKS * LANE8
    signals = []
    for start in (0, LANE8):
        pieces = [filter_ref[start : start + LANE8, i * BLOCK : (i + 1) * BLOCK] for i in range(BLOCKS)]
        signals.append(jnp.concatenate(pieces, 0))
    spectra = forward(*signals, first_ref, second_ref, cosine, sine)
    spectrum_ref[0] = spectra[:rows]
    spectrum_ref[1] = spectra[rows:]


def start_all(copies):
    for copy in copies:
        copy.start()


def wait_all(copies):
    for copy in copies:
        copy.wait()


def weight_copies(weight_hbm, weight, sems):
    copies = []
    for slot in range(weight_hbm.shape[0]):
        lanes = pl.ds(slot % 2 * 2 * CHANS, 2 * CHANS)
        copies.append(pltpu.make_async_copy(weight_hbm.at[slot], weight.at[slot // 2, :, lanes], sems.at[slot]))
    return copies


def masks_of(marks, width):
    trials = marks.shape[0]
    marks = marks[:, :width].astype(jnp.int32)
    marks = jnp.broadcast_to(marks[:, None, :], (trials, TRIAL, width)).reshape(trials * TRIAL, width)
    return marks


def pick(leaf, marks, count):
    level = 0
    stack = []
    for index in range(count):
        node = leaf(index)
        level = 0
        while stack and stack[-1][0] == level:
            node = jnp.where((marks & (1 << level)) != 0, node, stack.pop()[1])
            level += 1
        stack.append((level, node))
    return stack[0][1]


def project(rows_ref, start, weight):
    width = 2 * CHANS
    rows = rows_ref[pl.ds(start, 2), :BLOCK, :].reshape(2 * BLOCK, rows_ref.shape[2])
    marks = rows_ref[pl.ds(start, 2), BLOCK:, :].astype(f32).reshape(2 * BLOCK // TRIAL, rows_ref.shape[2])
    marks = masks_of(marks, width)
    products = {}

    def leaf(slot):
        if slot % 2 == 0:
            products[0] = jnp.dot(rows, weight[slot // 2], preferred_element_type=f32)
            return products[0][:, :width]
        return products[0][:, width:]

    chosen = pick(leaf, marks, 2 * weight.shape[0])
    return chosen[:BLOCK].T.astype(bf16), chosen[BLOCK:].T.astype(bf16)


def read_in_kernel(weight_hbm, *rest):
    chunk_refs = rest[:-5]
    out_ref, rows, weight, weight_sems, sems = rest[-5:]
    loads = weight_copies(weight_hbm, weight, weight_sems)
    for index, chunk in enumerate(chunk_refs):
        loads.append(pltpu.make_async_copy(chunk, rows.at[pl.ds(index * Y, Y)], sems.at[index]))
    start_all(loads)
    wait_all(loads)

    def step(pair, carry):
        low, high = project(rows, pair * 2, weight)
        out_ref[pair * 2] = low
        out_ref[pair * 2 + 1] = high
        return carry

    lax.fori_loop(0, rows.shape[0] // 2, step, 0)


def read_in(chunks, weights):
    blocks = len(chunks) * Y
    in_chans = weights.shape[1]
    width = weights.shape[2]
    flops = 2 * blocks * BLOCK * weights.shape[0] * in_chans * width
    return pl.pallas_call(
        read_in_kernel,
        out_shape=jax.ShapeDtypeStruct((blocks, width, BLOCK), bf16),
        in_specs=[pl.BlockSpec(memory_space=pltpu.HBM)] * (1 + len(chunks)),
        out_specs=whole(1)[0],
        scratch_shapes=[
            pltpu.VMEM((blocks,) + chunks[0].shape[1:], bf16),
            pltpu.VMEM((weights.shape[0] // 2, in_chans, 2 * width), bf16),
            pltpu.SemaphoreType.DMA((weights.shape[0],)),
            pltpu.SemaphoreType.DMA((len(chunks),)),
        ],
        compiler_params=pltpu.CompilerParams(vmem_limit_bytes=60 << 20),
        cost_estimate=pl.CostEstimate(flops=flops, bytes_accessed=4 << 20, transcendentals=0),
        name="read_in",
    )(weights, *chunks)


def block_of(place_ref, index):
    z = lax.rem(place_ref[0] + (Z_STEPS[index // Y] + Z), Z)
    y = lax.rem(place_ref[1] + (Y_STEPS[index % Y] + Y), Y)
    return z * Y + y


def main_kernel(place_ref, taps_ref, gain_ref, twist_ref, early_hbm, right_hbm, left_hbm, last_right_hbm, last_left_hbm, weight_hbm, filter_hbm, grad_hbm, *rest):
    table_hbms = rest[:4]
    gated_ref, out_ref, both, rows, weight, spectra, grad_all, *rest = rest[4:]
    tables = rest[:4]
    weight_sems, row_sems, early_sems, sems = rest[4:]
    half = Y // 2
    late = [
        pltpu.make_async_copy(right_hbm, rows.at[pl.ds(0, Y)], row_sems.at[0]),
        pltpu.make_async_copy(left_hbm, rows.at[pl.ds(Y, Y)], row_sems.at[1]),
        pltpu.make_async_copy(last_right_hbm, rows.at[pl.ds(2 * Y, half)], row_sems.at[2]),
        pltpu.make_async_copy(last_left_hbm, rows.at[pl.ds(2 * Y + half, half)], row_sems.at[3]),
    ] + weight_copies(weight_hbm, weight, weight_sems)
    early = early_hbm.shape[0]
    others = [
        pltpu.make_async_copy(early_hbm.at[index], both.at[block_of(place_ref, index)], early_sems.at[index])
        for index in range(early)
    ]
    pairs = [(filter_hbm, spectra), (grad_hbm, grad_all)] + list(zip(table_hbms, tables))
    others += [pltpu.make_async_copy(source, target, sems.at[index]) for index, (source, target) in enumerate(pairs)]
    start_all(late)
    start_all(others)
    wait_all(late)
    for index in range(0, rows.shape[0], 2):
        low, high = project(rows, index, weight)
        both[block_of(place_ref, early + index)] = low
        both[block_of(place_ref, early + index + 1)] = high
    cosine, sine = twists_of(twist_ref)
    lane = lax.broadcasted_iota(jnp.int32, (BLOCKS, LANE8, BLOCK), 2)
    count = BLOCKS * LANE8
    cube = (BLOCKS, LANE8, BLOCK)
    wait_all(others)
    first_ref, second_ref, back_second_ref, back_first_ref = tables

    def one_group(group, value, gate, grads):
        here = pl.ds(pl.multiple_of(group * LANE8, LANE8), LANE8)
        taps = taps_ref[:, here, :]
        total = taps[0][None] * value
        for shift in (1, 2):
            rolled = pltpu.roll(value.reshape(count, BLOCK), shift, 1).reshape(cube)
            before = jnp.concatenate([jnp.zeros((1, LANE8, BLOCK), f32), rolled[:-1]], 0)
            total = total + taps[shift][None] * jnp.where(lane < shift, before, rolled)
        signal = total.astype(bf16).astype(f32).reshape(count, BLOCK)
        mixed_grad = (grads * gate).reshape(count, BLOCK)
        spectra_two = forward(signal, mixed_grad, first_ref, second_ref, cosine, sine)
        own_re, own_im = spectra_two[:count, :BLOCK], spectra_two[:count, BLOCK:]
        grad_re, grad_im = spectra_two[count:, :BLOCK], spectra_two[count:, BLOCK:]
        weight = spectra[group]
        filter_re, filter_im = weight[:, :BLOCK], weight[:, BLOCK:]
        mix = jnp.concatenate([own_re * filter_re - own_im * filter_im, own_re * filter_im + own_im * filter_re], 1)
        lag = jnp.concatenate([own_re * grad_re + own_im * grad_im, own_re * grad_im - own_im * grad_re], 1)
        result = backward(jnp.concatenate([mix, lag], 0), back_second_ref, back_first_ref, cosine, sine)
        mixed = result[:, :BLOCK].reshape(cube) + gain_ref[here, :][None] * signal.reshape(cube)
        gated = gate * mixed.astype(bf16).astype(f32)
        pieces = [result[i * LANE8 : (i + 1) * LANE8, BLOCK:] for i in range(BLOCKS)]
        return gated, jnp.concatenate(pieces, 1)

    def step(pair, carry):
        here = pl.ds(pl.multiple_of(pair * 2 * LANE8, 2 * LANE8), 2 * LANE8)
        there = pl.ds(pl.multiple_of(CHANS + pair * 2 * LANE8, 2 * LANE8), 2 * LANE8)
        value = both[:, here, :].astype(f32)
        gate = both[:, there, :].astype(f32)
        grads = grad_all[:, here, :].astype(f32)
        gated_low, low = one_group(pair * 2, value[:, :LANE8], gate[:, :LANE8], grads[:, :LANE8])
        gated_high, high = one_group(pair * 2 + 1, value[:, LANE8:], gate[:, LANE8:], grads[:, LANE8:])
        gated = jnp.concatenate([gated_low, gated_high], 1).astype(bf16).reshape(Z, Y, 2 * LANE8, BLOCK)
        for y in range(Y):
            gated_ref[y, :, here, :] = gated[:, y]
        out_ref[here, :] = jnp.concatenate([low, high], 0).astype(bf16)
        return carry

    lax.fori_loop(0, GROUPS // 2, step, 0)


def read_out_kernel(place_ref, rows_ref, mark_ref, weight_ref, out_ref):
    slots, inner, width = weight_ref.shape

    def block_at(index):
        up = (index + 1) // 2
        step = jnp.where(index % 2 == 1, Z - up, index // 2)
        return lax.rem(place_ref[0] + step, Z)

    def step(pair, carry):
        pieces = []
        marks = []
        for index in range(2):
            block = block_at(pair * 2 + index)
            pieces.append(rows_ref[:, block, :, :].reshape(inner, BLOCK).T)
            marks.append(mark_ref[pair * 2 + index].astype(f32))
        rows = jnp.concatenate(pieces, 0)
        marks = masks_of(jnp.concatenate(marks, 0), width)
        leaf = lambda slot: jnp.dot(rows, weight_ref[slot], preferred_element_type=f32)
        chosen = pick(leaf, marks, slots)
        for index in range(2):
            out_ref[block_at(pair * 2 + index)] = chosen[index * BLOCK : (index + 1) * BLOCK].astype(bf16)
        return carry

    lax.fori_loop(0, Z // 2, step, 0)


def along_y(value, step):
    return lax.ppermute(value, "seq", [(z * Y + y, z * Y + (y + step) % Y) for z in range(Z) for y in range(Y)])


def along_z(value, step):
    return lax.ppermute(value, "seq", [(z * Y + y, (z + step) % Z * Y + y) for z in range(Z) for y in range(Y)])


def gather_weights(own):
    groups = lax.axis_size("grp")
    copies = jnp.broadcast_to(own[None], (groups,) + own.shape)
    gathered = lax.all_to_all(copies, "grp", split_axis=0, concat_axis=0, tiled=True)
    return gathered.reshape((groups * own.shape[0],) + own.shape[1:])


def whole(count):
    return [pl.BlockSpec(memory_space=pltpu.VMEM)] * count


def local(spikes, session_of_bin, session_slot, readin_weight, short_kernel, long_filter, skip_gain, readout_weight, out_grad):
    groups = lax.axis_size("grp")
    in_chans = spikes.shape[2]
    model_width = short_kernel.shape[1]
    place = lax.axis_index("seq")
    scalar = pl.BlockSpec(memory_space=pltpu.SMEM)
    z_groups = [[z * Y + y for z in range(Z)] for y in range(Y)]
    y_groups = [[z * Y + y for y in range(Y)] for z in range(Z)]
    coords = jnp.stack([place // Y, place % Y]).astype(jnp.int32)
    first, second, back_second, back_first, twists = transform_tables()

    own = jnp.concatenate(
        [lax.dynamic_slice_in_dim(readin_weight, start + place * CHANS, CHANS, 2) for start in (0, model_width)], 2
    )
    in_weights = gather_weights(own)
    own = lax.dynamic_slice_in_dim(readout_weight, place // Y * (Y * CHANS), Y * CHANS, 1)
    out_weights = gather_weights(own)

    sessions = session_of_bin[0, ::TRIAL]
    matches = sessions[:, None] == jnp.arange(session_slot.shape[0], dtype=jnp.int32)[None, :]
    slots = jnp.sum(jnp.where(matches, session_slot[None, :], 0), axis=1)
    marks = jnp.broadcast_to(slots.astype(bf16)[:, None], (slots.shape[0], in_chans))
    block = jnp.concatenate([spikes[0], marks], 0)
    chunk = jnp.stack([block, along_y(block, 1), along_y(block, -1), along_y(block, 2)])
    chunks = [chunk]
    right = left = chunk
    turned = out_grad[0].T.reshape(BLOCKS, CHANS, BLOCK)
    for _ in range(2):
        right, left = along_z(right, 1), along_z(left, -1)
        chunks += [right, left]
    right, left, in_weights = lax.optimization_barrier((right, left, in_weights))
    right, left = along_z(right, 1), along_z(left, -1)
    early = read_in(chunks, in_weights)
    right, left, turned, early = lax.optimization_barrier((right, left, turned, early))
    last_right, last_left = along_z(right[: Y // 2], 1), along_z(left[Y // 2 :], -1)
    grads = lax.all_to_all(turned, "seq", split_axis=0, concat_axis=0, tiled=True)
    chunks += [right, left]

    spectrum_shape = jax.ShapeDtypeStruct((GROUPS, BLOCKS * LANE8, 2 * BLOCK), f32)
    plane = (BLOCKS, CHANS, BLOCK)
    params = pltpu.CompilerParams(vmem_limit_bytes=60 << 20)
    work = 2 * GROUPS * (512 * 256 * 128 + 256 * 256 * 256)
    pair = 2 * LANE8
    filter_spectrum = pl.pallas_call(
        filter_kernel,
        out_shape=spectrum_shape,
        grid=(GROUPS // 2,),
        in_specs=[pl.BlockSpec((pair, LENGTH), lambda i: (i, 0))]
        + [pl.BlockSpec(table.shape, lambda i, rank=table.ndim: (0,) * rank) for table in (first, second, twists)],
        out_specs=pl.BlockSpec((2,) + spectrum_shape.shape[1:], lambda i: (i, 0, 0)),
        compiler_params=params,
        cost_estimate=pl.CostEstimate(flops=work, bytes_accessed=4 << 20, transcendentals=0),
        name="filter_transform",
    )(long_filter, first, second, twists)

    taps = lax.dynamic_slice_in_dim(short_kernel, place * CHANS, CHANS, 1)
    taps = jnp.broadcast_to(taps[:, :, None], (short_kernel.shape[0], CHANS, BLOCK))
    gains = jnp.broadcast_to(skip_gain[:, None], (CHANS, BLOCK))
    tables = (first, second, back_second, back_first)
    late_rows = 2 * Y + Y
    gated, own_grad = pl.pallas_call(
        main_kernel,
        out_shape=(
            jax.ShapeDtypeStruct((Y, Z, CHANS, BLOCK), bf16),
            jax.ShapeDtypeStruct((CHANS, LENGTH), bf16),
        ),
        in_specs=[scalar] + whole(3) + [pl.BlockSpec(memory_space=pltpu.HBM)] * 12,
        out_specs=tuple(whole(2)),
        scratch_shapes=[
            pltpu.VMEM((BLOCKS, 2 * CHANS, BLOCK), bf16),
            pltpu.VMEM((late_rows,) + chunk.shape[1:], bf16),
            pltpu.VMEM((in_weights.shape[0] // 2, in_chans, 4 * CHANS), bf16),
            pltpu.VMEM(spectrum_shape.shape, f32),
            pltpu.VMEM(plane, bf16),
        ]
        + [pltpu.VMEM(table.shape, bf16) for table in tables]
        + [pltpu.SemaphoreType.DMA((count,)) for count in (in_weights.shape[0], 4, early.shape[0], 6)],
        compiler_params=pltpu.CompilerParams(vmem_limit_bytes=60 << 20),
        cost_estimate=pl.CostEstimate(flops=4 * work, bytes_accessed=8 << 20, transcendentals=0),
        name="long_convolution",
    )(coords, taps, gains, twists, early, right, left, last_right, last_left, in_weights, filter_spectrum, grads, *tables)
    arrived = lax.all_to_all(gated, "seq", split_axis=0, concat_axis=0, tiled=True, axis_index_groups=y_groups)
    shares = lax.all_to_all(own_grad.reshape(groups, CHANS // groups, LENGTH), "grp", split_axis=0, concat_axis=0, tiled=True)
    share = jnp.sum(shares.astype(f32), 0).astype(bf16)
    filter_grad = lax.all_gather(share, "grp", axis=0, tiled=True).astype(f32)
    marks = jnp.stack([piece[0, BLOCK:, :] for piece in chunks + [last_right]])
    partial = pl.pallas_call(
        read_out_kernel,
        out_shape=jax.ShapeDtypeStruct((Z, BLOCK, in_chans), bf16),
        in_specs=[scalar] + whole(3),
        out_specs=whole(1)[0],
        compiler_params=params,
        cost_estimate=pl.CostEstimate(flops=2 * 512 * 512 * 4096, bytes_accessed=6 << 20, transcendentals=0),
        name="read_out",
    )(coords, arrived, marks, out_weights)
    pieces = lax.all_to_all(partial, "seq", split_axis=0, concat_axis=0, tiled=True, axis_index_groups=z_groups)
    denoised = jnp.sum(pieces.astype(f32), 0).astype(bf16)
    return denoised[None], filter_grad


def solution(mesh):
    placed = (
        P("grp", "seq", None),
        P("grp", "seq"),
        P(),
        P("grp", None, None),
        P(),
        P("seq", None),
        P("seq"),
        P("grp", None, None),
        P("grp", "seq", None),
    )
    return jax.shard_map(
        local,
        mesh=mesh,
        in_specs=placed,
        out_specs=(P("grp", "seq", None), P("seq", None)),
        check_vma=False,
    )
```

```python
import jax
import jax.numpy as jnp
import numpy as np
from jax import lax
from jax.experimental import pallas as pl
from jax.experimental.pallas import tpu as pltpu
from jax.sharding import PartitionSpec as P

BLOCK = 128
TRIAL = 16
Z = 8
Y = 4
BLOCKS = Z * Y
CHANS = 64
LANE8 = 8
GROUPS = CHANS // LANE8
LENGTH = BLOCKS * BLOCK
X = 4
CORES = 2
X_STEPS = (0, -1, 1, 2)
f32 = jnp.float32
bf16 = jnp.bfloat16


def transform_tables():
    slow = np.arange(BLOCKS)
    fast = np.arange(BLOCK)
    first = np.exp(-2j * np.pi * (np.outer(slow, slow) / BLOCKS + slow[None, :] / (4.0 * BLOCKS)))
    twist = np.exp(-2j * np.pi * (slow[:, None] + 0.25) * fast[None, :] / LENGTH)
    second = np.exp(-2j * np.pi * np.outer(fast, fast) / BLOCK)
    eye = np.eye(LANE8)
    spread_first = np.concatenate([np.kron(first.real, eye), np.kron(first.imag, eye)], 0)
    forward_second = np.block([[second.real, second.imag], [-second.imag, second.real]])
    back = second.conj()
    back_second = np.block([[back.real, back.imag], [-back.imag, back.real]])
    back_first = first.conj().T / LENGTH
    spread_back = np.concatenate([np.kron(back_first.real, eye), np.kron(-back_first.imag, eye)], 1)
    as_bf16 = lambda table: jnp.asarray(table.astype(np.float32), bf16)
    twists = np.stack([twist.real, twist.imag]).astype(np.float32)
    return (
        as_bf16(spread_first),
        as_bf16(forward_second),
        as_bf16(back_second),
        as_bf16(spread_back),
        jnp.asarray(twists),
    )


def twists_of(twist_ref):
    shape = (BLOCKS, LANE8, BLOCK)
    cosine = jnp.broadcast_to(twist_ref[0][:, None, :], shape).reshape(BLOCKS * LANE8, BLOCK)
    sine = jnp.broadcast_to(twist_ref[1][:, None, :], shape).reshape(BLOCKS * LANE8, BLOCK)
    return cosine, sine


def forward(low, high, first_ref, second_ref, cosine, sine):
    rows = BLOCKS * LANE8
    signals = jnp.concatenate([low, high], 1).astype(bf16)
    part = jnp.dot(first_ref[...], signals, preferred_element_type=f32)
    turned = []
    for lanes in (slice(0, BLOCK), slice(BLOCK, 2 * BLOCK)):
        real, imag = part[:rows, lanes], part[rows:, lanes]
        turned.append(jnp.concatenate([real * cosine - imag * sine, real * sine + imag * cosine], 1))
    return jnp.dot(jnp.concatenate(turned, 0).astype(bf16), second_ref[...], preferred_element_type=f32)


def backward(spectra, back_second_ref, back_first_ref, cosine, sine):
    rows = BLOCKS * LANE8
    part = jnp.dot(spectra.astype(bf16), back_second_ref[...], preferred_element_type=f32)
    turned = []
    for start in (0, rows):
        real, imag = part[start : start + rows, :BLOCK], part[start : start + rows, BLOCK:]
        turned.append(jnp.concatenate([real * cosine + imag * sine, imag * cosine - real * sine], 0))
    return jnp.dot(back_first_ref[...], jnp.concatenate(turned, 1).astype(bf16), preferred_element_type=f32)


def filter_kernel(filter_ref, first_ref, second_ref, twist_ref, spectrum_ref):
    cosine, sine = twists_of(twist_ref)
    rows = BLOCKS * LANE8
    signals = []
    for start in (0, LANE8):
        pieces = [filter_ref[start : start + LANE8, i * BLOCK : (i + 1) * BLOCK] for i in range(BLOCKS)]
        signals.append(jnp.concatenate(pieces, 0))
    spectra = forward(*signals, first_ref, second_ref, cosine, sine)
    spectrum_ref[0] = spectra[:rows]
    spectrum_ref[1] = spectra[rows:]


def start_all(copies):
    for copy in copies:
        copy.start()


def wait_all(copies):
    for copy in copies:
        copy.wait()


def weight_copies(place_ref, weight_hbms, take, sems):
    copies = []
    for other, weight_hbm in enumerate(weight_hbms):
        core = place_ref[3] if other == 0 else 1 - place_ref[3]
        for index, step in enumerate(X_STEPS):
            group = lax.rem(place_ref[2] + (step + X), X) * CORES + core
            for slot in range(2):
                lanes, target = take(group, slot)
                number = (other * X + index) * 2 + slot
                copies.append(pltpu.make_async_copy(weight_hbm.at[index, slot, :, lanes], target, sems.at[number]))
    return copies


def masks_of(marks, width):
    trials = marks.shape[0]
    marks = marks[:, :width].astype(jnp.int32)
    marks = jnp.broadcast_to(marks[:, None, :], (trials, TRIAL, width)).reshape(trials * TRIAL, width)
    return marks


def pick(leaf, marks, count):
    level = 0
    stack = []
    for index in range(count):
        node = leaf(index)
        level = 0
        while stack and stack[-1][0] == level:
            node = jnp.where((marks & (1 << level)) != 0, node, stack.pop()[1])
            level += 1
        stack.append((level, node))
    return stack[0][1]


def project(rows_ref, start, blocks, weight):
    width = 2 * CHANS
    rows = rows_ref[pl.ds(start, blocks), :BLOCK, :].reshape(blocks * BLOCK, rows_ref.shape[2])
    marks = rows_ref[pl.ds(start, blocks), BLOCK:, :].astype(f32).reshape(blocks * BLOCK // TRIAL, rows_ref.shape[2])
    marks = masks_of(marks, width)
    products = {}

    def leaf(slot):
        if slot % 2 == 0:
            products[0] = jnp.dot(rows, weight[slot // 2], preferred_element_type=f32)
            return products[0][:, :width]
        return products[0][:, width:]

    chosen = pick(leaf, marks, 2 * weight.shape[0])
    return [chosen[i * BLOCK : (i + 1) * BLOCK].T.astype(bf16) for i in range(blocks)]


def block_of(place_ref, z_step, y_index):
    y_step = jnp.where(y_index < 2, Y - y_index, y_index - 1)
    return lax.rem(place_ref[0] + z_step, Z) * Y + lax.rem(place_ref[1] + y_step, Y)


def z_step_of(index):
    return jnp.where(index % 2 == 1, Z - (index + 1) // 2, index // 2)


def forward_kernel(place_ref, taps_ref, gain_ref, twist_ref, filter_hbm, own_hbm, other_hbm, *rest):
    chunk_hbms = rest[: Z + 1]
    table_hbms = rest[Z + 1 : Z + 5]
    gated_ref, gate_ref, spectrum_ref, both, rows, weight, spectra, *rest = rest[Z + 5 :]
    tables = rest[:4]
    weight_sems, row_sems, sems = rest[4:]
    half = Y // 2
    width = 2 * CHANS
    place = lambda group, slot: (pl.ds(0, width), weight.at[group, :, pl.ds(slot * width, width)])
    loads = weight_copies(place_ref, (own_hbm, other_hbm), place, weight_sems)
    for index, chunk in enumerate(chunk_hbms[: Z - 1]):
        loads.append(pltpu.make_async_copy(chunk, rows.at[pl.ds(index * Y, Y)], row_sems.at[index]))
    for index, chunk in enumerate(chunk_hbms[Z - 1 :]):
        target = rows.at[pl.ds((Z - 1) * Y + index * half, half)]
        loads.append(pltpu.make_async_copy(chunk, target, row_sems.at[Z - 1 + index]))
    pairs = [(filter_hbm, spectra)] + list(zip(table_hbms, tables))
    others = [pltpu.make_async_copy(source, target, sems.at[index]) for index, (source, target) in enumerate(pairs)]
    start_all(loads)
    start_all(others)
    wait_all(loads)

    def read_in(index, carry):
        blocks = project(rows, index * Y, Y, weight)
        for y_index in range(Y):
            both[block_of(place_ref, z_step_of(index), y_index)] = blocks[y_index]
        return carry

    lax.fori_loop(0, Z, read_in, 0)
    cosine, sine = twists_of(twist_ref)
    lane = lax.broadcasted_iota(jnp.int32, (BLOCKS, LANE8, BLOCK), 2)
    count = BLOCKS * LANE8
    cube = (BLOCKS, LANE8, BLOCK)
    wait_all(others)
    first_ref, second_ref, back_second_ref, back_first_ref = tables

    def short(value, group):
        taps = taps_ref[:, pl.ds(pl.multiple_of(group * LANE8, LANE8), LANE8), :]
        total = taps[0][None] * value
        for shift in (1, 2):
            rolled = pltpu.roll(value.reshape(count, BLOCK), shift, 1).reshape(cube)
            before = jnp.concatenate([jnp.zeros((1, LANE8, BLOCK), f32), rolled[:-1]], 0)
            total = total + taps[shift][None] * jnp.where(lane < shift, before, rolled)
        return total.astype(bf16).astype(f32).reshape(count, BLOCK)

    def step(pair, carry):
        here = pl.ds(pl.multiple_of(pair * 2 * LANE8, 2 * LANE8), 2 * LANE8)
        there = pl.ds(pl.multiple_of(CHANS + pair * 2 * LANE8, 2 * LANE8), 2 * LANE8)
        value = both[:, here, :].astype(f32)
        gate = both[:, there, :]
        signals = [short(value[:, i * LANE8 : (i + 1) * LANE8], pair * 2 + i) for i in range(2)]
        own = forward(*signals, first_ref, second_ref, cosine, sine)
        spectrum_ref[pl.ds(pair * 2, 2)] = own.reshape(2, count, 2 * BLOCK)
        weight = spectra[pl.ds(pair * 2, 2)].reshape(2 * count, 2 * BLOCK)
        own_re, own_im = own[:, :BLOCK], own[:, BLOCK:]
        filter_re, filter_im = weight[:, :BLOCK], weight[:, BLOCK:]
        mix = jnp.concatenate([own_re * filter_re - own_im * filter_im, own_re * filter_im + own_im * filter_re], 1)
        result = backward(mix, back_second_ref, back_first_ref, cosine, sine)
        signal = jnp.concatenate([piece.reshape(cube) for piece in signals], 1)
        long_part = jnp.concatenate([result[:, i * BLOCK : (i + 1) * BLOCK].reshape(cube) for i in range(2)], 1)
        mixed = (long_part + gain_ref[here, :][None] * signal).astype(bf16).astype(f32)
        gated = (gate.astype(f32) * mixed).astype(bf16).reshape(Z, Y, 2 * LANE8, BLOCK)
        for y in range(Y):
            gated_ref[y, :, here, :] = gated[:, y]
        gate_ref[:, here, :] = gate
        return carry

    lax.fori_loop(0, GROUPS // 2, step, 0)


def gradient_kernel(grad_ref, gate_ref, spectrum_ref, first_ref, second_ref, back_second_ref, back_first_ref, twist_ref, out_ref):
    cosine, sine = twists_of(twist_ref)
    count = BLOCKS * LANE8
    products = (grad_ref[...].astype(f32) * gate_ref[...].astype(f32)).astype(bf16).astype(f32)
    signals = [products[:, i * LANE8 : (i + 1) * LANE8].reshape(count, BLOCK) for i in range(2)]
    spectra = forward(*signals, first_ref, second_ref, cosine, sine)
    own = spectrum_ref[...].reshape(2 * count, 2 * BLOCK)
    own_re, own_im = own[:, :BLOCK], own[:, BLOCK:]
    grad_re, grad_im = spectra[:, :BLOCK], spectra[:, BLOCK:]
    lag = jnp.concatenate([own_re * grad_re + own_im * grad_im, own_re * grad_im - own_im * grad_re], 1)
    result = backward(lag, back_second_ref, back_first_ref, cosine, sine)
    both = []
    for half in range(2):
        lanes = slice(half * BLOCK, (half + 1) * BLOCK)
        both.append(jnp.concatenate([result[i * LANE8 : (i + 1) * LANE8, lanes] for i in range(BLOCKS)], 1))
    out_ref[...] = jnp.concatenate(both, 0).astype(bf16)


def read_out_kernel(place_ref, own_hbm, other_hbm, rows_hbm, *rest):
    mark_hbms = rest[:Z]
    out_ref, weight, rows_all, marks_all, weight_sems, mark_sems, row_sem = rest[Z:]
    slots, inner, width = weight.shape
    take = lambda group, slot: (pl.ds(2 * CHANS, width), weight.at[group * 2 + slot])
    loads = [pltpu.make_async_copy(rows_hbm, rows_all, row_sem)]
    for index, mark_hbm in enumerate(mark_hbms):
        source = mark_hbm.at[0, pl.ds(BLOCK, BLOCK // TRIAL), :]
        loads.append(pltpu.make_async_copy(source, marks_all.at[index], mark_sems.at[index]))
    loads += weight_copies(place_ref, (own_hbm, other_hbm), take, weight_sems)
    start_all(loads)
    wait_all(loads)

    def step(quad, carry):
        places = [lax.rem(place_ref[0] + z_step_of(quad * 4 + index), Z) for index in range(4)]
        rows = jnp.concatenate([rows_all[:, block, :, :].reshape(inner, BLOCK).T for block in places], 0)
        marks = marks_all[pl.ds(quad * 4, 4)].astype(f32).reshape(4 * BLOCK // TRIAL, width)
        marks = masks_of(marks, width)
        leaf = lambda slot: jnp.dot(rows, weight[slot], preferred_element_type=f32)
        chosen = pick(leaf, marks, slots)
        for index, block in enumerate(places):
            out_ref[block] = chosen[index * BLOCK : (index + 1) * BLOCK].astype(bf16)
        return carry

    lax.fori_loop(0, Z // 4, step, 0)


def along_y(value, step):
    return lax.ppermute(value, "seq", [(z * Y + y, z * Y + (y + step) % Y) for z in range(Z) for y in range(Y)])


def along_z(value, step):
    return lax.ppermute(value, "seq", [(z * Y + y, (z + step) % Z * Y + y) for z in range(Z) for y in range(Y)])


def along_x(value, step):
    pairs = [(x * CORES + c, (x + step) % X * CORES + c) for x in range(X) for c in range(CORES)]
    return lax.ppermute(value, "grp", pairs)


def other_core(value):
    return lax.ppermute(value, "grp", [(group, group ^ 1) for group in range(X * CORES)])


def whole(count):
    return [pl.BlockSpec(memory_space=pltpu.VMEM)] * count


def local(spikes, session_of_bin, session_slot, readin_weight, short_kernel, long_filter, skip_gain, readout_weight, out_grad):
    groups = lax.axis_size("grp")
    in_chans = spikes.shape[2]
    model_width = short_kernel.shape[1]
    place = lax.axis_index("seq")
    group = lax.axis_index("grp")
    scalar = pl.BlockSpec(memory_space=pltpu.SMEM)
    hbm = pl.BlockSpec(memory_space=pltpu.HBM)
    z_groups = [[z * Y + y for z in range(Z)] for y in range(Y)]
    y_groups = [[z * Y + y for y in range(Y)] for z in range(Z)]
    coords = jnp.stack([place // Y, place % Y, group // CORES, group % CORES]).astype(jnp.int32)
    first, second, back_second, back_first, twists = transform_tables()
    params = pltpu.CompilerParams(vmem_limit_bytes=60 << 20)
    spectrum_shape = jax.ShapeDtypeStruct((GROUPS, BLOCKS * LANE8, 2 * BLOCK), f32)
    plane = (BLOCKS, CHANS, BLOCK)
    work = 2 * GROUPS * (512 * 256 * 128 + 256 * 256 * 256)
    pair = 2 * LANE8
    same = lambda table: pl.BlockSpec(table.shape, lambda i, rank=table.ndim: (0,) * rank)

    sessions = session_of_bin[0, ::TRIAL]
    matches = sessions[:, None] == jnp.arange(session_slot.shape[0], dtype=jnp.int32)[None, :]
    slots = jnp.sum(jnp.where(matches, session_slot[None, :], 0), axis=1)
    marks = jnp.broadcast_to(slots.astype(bf16)[:, None], (slots.shape[0], in_chans))
    block = jnp.concatenate([spikes[0], marks], 0)
    chunk = jnp.stack([block, along_y(block, 1), along_y(block, -1), along_y(block, 2)])
    right, left = along_z(chunk, 1), along_z(chunk, -1)
    chunks = [chunk, right, left]

    pieces = [lax.dynamic_slice_in_dim(readin_weight, start + place * CHANS, CHANS, 2) for start in (0, model_width)]
    pieces.append(lax.dynamic_slice_in_dim(readout_weight, place // Y * (Y * CHANS), Y * CHANS, 1))
    own = jnp.concatenate(pieces, 2)
    own_right, own_left = along_x(own, 1), along_x(own, -1)

    filter_spectrum = pl.pallas_call(
        filter_kernel,
        out_shape=spectrum_shape,
        grid=(GROUPS // 2,),
        in_specs=[pl.BlockSpec((pair, LENGTH), lambda i: (i, 0))] + [same(table) for table in (first, second, twists)],
        out_specs=pl.BlockSpec((2,) + spectrum_shape.shape[1:], lambda i: (i, 0, 0)),
        compiler_params=params,
        cost_estimate=pl.CostEstimate(flops=work, bytes_accessed=4 << 20, transcendentals=0),
        name="filter_transform",
    )(long_filter, first, second, twists)
    turned = out_grad[0].T.reshape(BLOCKS, CHANS, BLOCK)

    right, left, own_right, own_left, filter_spectrum = lax.optimization_barrier((right, left, own_right, own_left, filter_spectrum))
    right, left = along_z(right, 1), along_z(left, -1)
    chunks += [right, left]
    far = jnp.concatenate([along_x(own_right[:1], 1), along_x(own_left[1:], -1)], 0)
    right, left, far, turned = lax.optimization_barrier((right, left, far, turned))
    right, left = along_z(right, 1), along_z(left, -1)
    chunks += [right, left]
    grads = lax.all_to_all(turned, "seq", split_axis=0, concat_axis=0, tiled=True)
    weights = jnp.stack([own, own_right, own_left, far])
    weights_other = other_core(weights)
    taps = lax.dynamic_slice_in_dim(short_kernel, place * CHANS, CHANS, 1)
    taps = jnp.broadcast_to(taps[:, :, None], (short_kernel.shape[0], CHANS, BLOCK))
    gains = jnp.broadcast_to(skip_gain[:, None], (CHANS, BLOCK))
    right, left, weights_other, taps, gains, coords = lax.optimization_barrier((right, left, weights_other, taps, gains, coords))
    last_right, last_left = along_z(right[: Y // 2], 1), along_z(left[Y // 2 :], -1)
    last_right, last_left, grads = lax.optimization_barrier((last_right, last_left, grads))

    tables = (first, second, back_second, back_first)
    slot_count = session_slot.shape[0]
    gated, gates, spectrum = pl.pallas_call(
        forward_kernel,
        out_shape=(
            jax.ShapeDtypeStruct((Y, Z, CHANS, BLOCK), bf16),
            jax.ShapeDtypeStruct(plane, bf16),
            spectrum_shape,
        ),
        in_specs=[scalar] + whole(3) + [hbm] * (3 + Z + 1 + 4),
        out_specs=tuple(whole(3)),
        scratch_shapes=[
            pltpu.VMEM((BLOCKS, 2 * CHANS, BLOCK), bf16),
            pltpu.VMEM((BLOCKS,) + chunk.shape[1:], bf16),
            pltpu.VMEM((slot_count // 2, in_chans, 4 * CHANS), bf16),
            pltpu.VMEM(spectrum_shape.shape, f32),
        ]
        + [pltpu.VMEM(table.shape, bf16) for table in tables]
        + [pltpu.SemaphoreType.DMA((count,)) for count in (slot_count, Z + 1, 5)],
        compiler_params=params,
        cost_estimate=pl.CostEstimate(flops=4 * work, bytes_accessed=8 << 20, transcendentals=0),
        name="long_convolution",
    )(coords, taps, gains, twists, filter_spectrum, weights, weights_other, *chunks, last_right, last_left, *tables)

    arrived = lax.all_to_all(gated, "seq", split_axis=0, concat_axis=0, tiled=True, axis_index_groups=y_groups)
    own_grad = pl.pallas_call(
        gradient_kernel,
        out_shape=jax.ShapeDtypeStruct((CHANS, LENGTH), bf16),
        grid=(GROUPS // 2,),
        in_specs=[pl.BlockSpec((BLOCKS, pair, BLOCK), lambda i: (0, i, 0))] * 2
        + [pl.BlockSpec((2,) + spectrum_shape.shape[1:], lambda i: (i, 0, 0))]
        + [same(table) for table in tables + (twists,)],
        out_specs=pl.BlockSpec((pair, LENGTH), lambda i: (i, 0)),
        compiler_params=params,
        cost_estimate=pl.CostEstimate(flops=2 * work, bytes_accessed=4 << 20, transcendentals=0),
        name="filter_gradient",
    )(grads, gates, spectrum, *tables, twists)
    shares = lax.all_to_all(own_grad.reshape(groups, CHANS // groups, LENGTH), "grp", split_axis=0, concat_axis=0, tiled=True)
    share = jnp.sum(shares.astype(f32), 0).astype(bf16)
    filter_grad = lax.all_gather(share, "grp", axis=0, tiled=True).astype(f32)
    partial = pl.pallas_call(
        read_out_kernel,
        out_shape=jax.ShapeDtypeStruct((Z, BLOCK, in_chans), bf16),
        in_specs=[scalar] + [hbm] * (3 + Z),
        out_specs=whole(1)[0],
        scratch_shapes=[
            pltpu.VMEM((slot_count, Y * CHANS, in_chans), bf16),
            pltpu.VMEM((Y, Z, CHANS, BLOCK), bf16),
            pltpu.VMEM((Z, BLOCK // TRIAL, in_chans), bf16),
        ]
        + [pltpu.SemaphoreType.DMA((count,)) for count in (slot_count, Z)]
        + [pltpu.SemaphoreType.DMA],
        compiler_params=params,
        cost_estimate=pl.CostEstimate(flops=2 * 512 * 512 * 4096, bytes_accessed=6 << 20, transcendentals=0),
        name="read_out",
    )(coords, weights, weights_other, arrived, *chunks, last_right)
    pieces = lax.all_to_all(partial, "seq", split_axis=0, concat_axis=0, tiled=True, axis_index_groups=z_groups)
    denoised = jnp.sum(pieces.astype(f32), 0).astype(bf16)
    return denoised[None], filter_grad


def solution(mesh):
    placed = (
        P("grp", "seq", None),
        P("grp", "seq"),
        P(),
        P("grp", None, None),
        P(),
        P("seq", None),
        P("seq"),
        P("grp", None, None),
        P("grp", "seq", None),
    )
    return jax.shard_map(
        local,
        mesh=mesh,
        in_specs=placed,
        out_specs=(P("grp", "seq", None), P("seq", None)),
        check_vma=False,
    )
```

```python
import jax
import jax.numpy as jnp
import numpy as np
from jax import lax
from jax.experimental import pallas as pl
from jax.experimental.pallas import tpu as pltpu
from jax.sharding import PartitionSpec as P

BLOCK = 128
TRIAL = 16
Z = 8
Y = 4
BLOCKS = Z * Y
CHANS = 64
LANE8 = 8
GROUPS = CHANS // LANE8
LENGTH = BLOCKS * BLOCK
X = 4
CORES = 2
X_STEPS = (0, -1, 1, 2)
f32 = jnp.float32
bf16 = jnp.bfloat16


def transform_tables():
    slow = np.arange(BLOCKS)
    fast = np.arange(BLOCK)
    first = np.exp(-2j * np.pi * (np.outer(slow, slow) / BLOCKS + slow[None, :] / (4.0 * BLOCKS)))
    twist = np.exp(-2j * np.pi * (slow[:, None] + 0.25) * fast[None, :] / LENGTH)
    second = np.exp(-2j * np.pi * np.outer(fast, fast) / BLOCK)
    eye = np.eye(LANE8)
    spread_first = np.concatenate([np.kron(first.real, eye), np.kron(first.imag, eye)], 0)
    forward_second = np.block([[second.real, second.imag], [-second.imag, second.real]])
    back = second.conj()
    back_second = np.block([[back.real, back.imag], [-back.imag, back.real]])
    back_first = first.conj().T / LENGTH
    spread_back = np.concatenate([np.kron(back_first.real, eye), np.kron(-back_first.imag, eye)], 1)
    as_bf16 = lambda table: jnp.asarray(table.astype(np.float32), bf16)
    twists = np.stack([twist.real, twist.imag]).astype(np.float32)
    return (
        as_bf16(spread_first),
        as_bf16(forward_second),
        as_bf16(back_second),
        as_bf16(spread_back),
        jnp.asarray(twists),
    )


def twists_of(twist_ref):
    shape = (BLOCKS, LANE8, BLOCK)
    cosine = jnp.broadcast_to(twist_ref[0][:, None, :], shape).reshape(BLOCKS * LANE8, BLOCK)
    sine = jnp.broadcast_to(twist_ref[1][:, None, :], shape).reshape(BLOCKS * LANE8, BLOCK)
    return cosine, sine


def forward(low, high, first_ref, second_ref, cosine, sine):
    rows = BLOCKS * LANE8
    signals = jnp.concatenate([low, high], 1).astype(bf16)
    part = jnp.dot(first_ref[...], signals, preferred_element_type=f32)
    turned = []
    for lanes in (slice(0, BLOCK), slice(BLOCK, 2 * BLOCK)):
        real, imag = part[:rows, lanes], part[rows:, lanes]
        turned.append(jnp.concatenate([real * cosine - imag * sine, real * sine + imag * cosine], 1))
    return jnp.dot(jnp.concatenate(turned, 0).astype(bf16), second_ref[...], preferred_element_type=f32)


def backward(spectra, back_second_ref, back_first_ref, cosine, sine):
    rows = BLOCKS * LANE8
    part = jnp.dot(spectra.astype(bf16), back_second_ref[...], preferred_element_type=f32)
    turned = []
    for start in (0, rows):
        real, imag = part[start : start + rows, :BLOCK], part[start : start + rows, BLOCK:]
        turned.append(jnp.concatenate([real * cosine + imag * sine, imag * cosine - real * sine], 0))
    return jnp.dot(back_first_ref[...], jnp.concatenate(turned, 1).astype(bf16), preferred_element_type=f32)


def filter_kernel(filter_ref, first_ref, second_ref, twist_ref, spectrum_ref):
    cosine, sine = twists_of(twist_ref)
    rows = BLOCKS * LANE8
    signals = []
    for start in (0, LANE8):
        pieces = [filter_ref[start : start + LANE8, i * BLOCK : (i + 1) * BLOCK] for i in range(BLOCKS)]
        signals.append(jnp.concatenate(pieces, 0))
    spectra = forward(*signals, first_ref, second_ref, cosine, sine)
    spectrum_ref[0] = spectra[:rows]
    spectrum_ref[1] = spectra[rows:]


def start_all(copies):
    for copy in copies:
        copy.start()


def wait_all(copies):
    for copy in copies:
        copy.wait()


def weight_copies(place_ref, weight_hbms, take, sems):
    copies = []
    for other, weight_hbm in enumerate(weight_hbms):
        core = place_ref[3] if other == 0 else 1 - place_ref[3]
        for index, step in enumerate(X_STEPS):
            group = lax.rem(place_ref[2] + (step + X), X) * CORES + core
            for slot in range(2):
                lanes, target = take(group, slot)
                number = (other * X + index) * 2 + slot
                copies.append(pltpu.make_async_copy(weight_hbm.at[index, slot, :, lanes], target, sems.at[number]))
    return copies


def spread(rows, marks, count):
    trials, width = marks.shape
    marks = jnp.broadcast_to(marks[:, None, :], (trials, TRIAL, width)).reshape(trials * TRIAL, width).astype(bf16)
    nothing = jnp.zeros_like(rows)
    return jnp.concatenate([jnp.where(marks == number, rows, nothing) for number in range(count)], 1)


def project(rows_ref, start, blocks, weight):
    width = 2 * CHANS
    in_chans = rows_ref.shape[2]
    rows = rows_ref[pl.ds(start, blocks), :BLOCK, :].reshape(blocks * BLOCK, in_chans)
    marks = rows_ref[pl.ds(start, blocks), BLOCK:, :].astype(f32).reshape(blocks * BLOCK // TRIAL, in_chans)
    wide = spread(rows, jnp.floor(marks * 0.5), weight.shape[0])
    product = jnp.dot(wide, weight[...].reshape(-1, 2 * width), preferred_element_type=f32)
    odd = (marks - 2 * jnp.floor(marks * 0.5))[:, :width]
    trials = odd.shape[0]
    odd = jnp.broadcast_to(odd[:, None, :], (trials, TRIAL, width)).reshape(trials * TRIAL, width)
    chosen = jnp.where(odd > 0.5, product[:, width:], product[:, :width])
    return [chosen[i * BLOCK : (i + 1) * BLOCK].T.astype(bf16) for i in range(blocks)]


def block_of(place_ref, z_step, y_index):
    y_step = jnp.where(y_index < 2, Y - y_index, y_index - 1)
    return lax.rem(place_ref[0] + z_step, Z) * Y + lax.rem(place_ref[1] + y_step, Y)


def z_step_of(index):
    return jnp.where(index % 2 == 1, Z - (index + 1) // 2, index // 2)


def forward_kernel(place_ref, taps_ref, gain_ref, twist_ref, filter_hbm, own_hbm, other_hbm, *rest):
    chunk_hbms = rest[:Z]
    table_hbms = rest[Z : Z + 4]
    gated_ref, gate_ref, spectrum_ref, both, rows, weight, spectra, *rest = rest[Z + 4 :]
    tables = rest[:4]
    weight_sems, row_sems, sems = rest[4:]
    width = 2 * CHANS
    place = lambda group, slot: (pl.ds(0, width), weight.at[group, :, pl.ds(slot * width, width)])
    loads = weight_copies(place_ref, (own_hbm, other_hbm), place, weight_sems)
    chunks = []
    for index, chunk in enumerate(chunk_hbms):
        chunks.append(pltpu.make_async_copy(chunk, rows.at[pl.ds(index * Y, Y)], row_sems.at[index]))
    pairs = [(filter_hbm, spectra)] + list(zip(table_hbms, tables))
    others = [pltpu.make_async_copy(source, target, sems.at[index]) for index, (source, target) in enumerate(pairs)]
    start_all(loads)
    start_all(chunks)
    start_all(others)
    wait_all(loads)
    wait_all(chunks)

    def read_in(index, carry):
        blocks = project(rows, index * Y, Y, weight)
        for y_index in range(Y):
            both[block_of(place_ref, z_step_of(index), y_index)] = blocks[y_index]
        return carry

    lax.fori_loop(0, Z, read_in, 0)
    cosine, sine = twists_of(twist_ref)
    lane = lax.broadcasted_iota(jnp.int32, (BLOCKS, LANE8, BLOCK), 2)
    count = BLOCKS * LANE8
    cube = (BLOCKS, LANE8, BLOCK)
    wait_all(others)
    first_ref, second_ref, back_second_ref, back_first_ref = tables

    def short(value, group):
        taps = taps_ref[:, pl.ds(pl.multiple_of(group * LANE8, LANE8), LANE8), :]
        total = taps[0][None] * value
        for shift in (1, 2):
            rolled = pltpu.roll(value.reshape(count, BLOCK), shift, 1).reshape(cube)
            before = jnp.concatenate([jnp.zeros((1, LANE8, BLOCK), f32), rolled[:-1]], 0)
            total = total + taps[shift][None] * jnp.where(lane < shift, before, rolled)
        return total.astype(bf16).astype(f32).reshape(count, BLOCK)

    def step(pair, carry):
        here = pl.ds(pl.multiple_of(pair * 2 * LANE8, 2 * LANE8), 2 * LANE8)
        there = pl.ds(pl.multiple_of(CHANS + pair * 2 * LANE8, 2 * LANE8), 2 * LANE8)
        value = both[:, here, :].astype(f32)
        gate = both[:, there, :]
        signals = [short(value[:, i * LANE8 : (i + 1) * LANE8], pair * 2 + i) for i in range(2)]
        own = forward(*signals, first_ref, second_ref, cosine, sine)
        spectrum_ref[pl.ds(pair * 2, 2)] = own.reshape(2, count, 2 * BLOCK)
        weight = spectra[pl.ds(pair * 2, 2)].reshape(2 * count, 2 * BLOCK)
        own_re, own_im = own[:, :BLOCK], own[:, BLOCK:]
        filter_re, filter_im = weight[:, :BLOCK], weight[:, BLOCK:]
        mix = jnp.concatenate([own_re * filter_re - own_im * filter_im, own_re * filter_im + own_im * filter_re], 1)
        result = backward(mix, back_second_ref, back_first_ref, cosine, sine)
        signal = jnp.concatenate([piece.reshape(cube) for piece in signals], 1)
        long_part = jnp.concatenate([result[:, i * BLOCK : (i + 1) * BLOCK].reshape(cube) for i in range(2)], 1)
        mixed = (long_part + gain_ref[here, :][None] * signal).astype(bf16).astype(f32)
        gated = (gate.astype(f32) * mixed).astype(bf16).reshape(Z, Y, 2 * LANE8, BLOCK)
        for y in range(Y):
            gated_ref[y, :, here, :] = gated[:, y]
        gate_ref[:, here, :] = gate
        return carry

    lax.fori_loop(0, GROUPS // 2, step, 0)


def gradient_kernel(place_ref, grad_ref, gate_ref, spectrum_ref, first_ref, second_ref, back_second_ref, back_first_ref, twist_ref, out_ref):
    cosine, sine = twists_of(twist_ref)
    count = BLOCKS * LANE8
    products = (grad_ref[...].astype(f32) * gate_ref[...].astype(f32)).astype(bf16).astype(f32)
    signals = [products[:, i * LANE8 : (i + 1) * LANE8].reshape(count, BLOCK) for i in range(2)]
    spectra = forward(*signals, first_ref, second_ref, cosine, sine)
    own = spectrum_ref[...].reshape(2 * count, 2 * BLOCK)
    own_re, own_im = own[:, :BLOCK], own[:, BLOCK:]
    grad_re, grad_im = spectra[:, :BLOCK], spectra[:, BLOCK:]
    lag = jnp.concatenate([own_re * grad_re + own_im * grad_im, own_re * grad_im - own_im * grad_re], 1)
    result = backward(lag, back_second_ref, back_first_ref, cosine, sine)
    both = []
    for half in range(2):
        lanes = slice(half * BLOCK, (half + 1) * BLOCK)
        both.append(jnp.concatenate([result[i * LANE8 : (i + 1) * LANE8, lanes] for i in range(BLOCKS)], 1))
    out_ref[0] = jnp.concatenate(both, 0).astype(bf16)


def read_out_kernel(place_ref, own_hbm, other_hbm, rows_hbm, *rest):
    mark_hbms = rest[:Z]
    out_ref, weight, rows_all, marks_all, weight_sems, mark_sems, row_sem = rest[Z:]
    slots, inner, width = weight.shape
    take = lambda group, slot: (pl.ds(2 * CHANS, width), weight.at[group * 2 + slot])
    loads = [pltpu.make_async_copy(rows_hbm, rows_all, row_sem)]
    for index, mark_hbm in enumerate(mark_hbms):
        source = mark_hbm.at[0, pl.ds(BLOCK, BLOCK // TRIAL), :]
        loads.append(pltpu.make_async_copy(source, marks_all.at[index], mark_sems.at[index]))
    loads += weight_copies(place_ref, (own_hbm, other_hbm), take, weight_sems)
    start_all(loads)
    wait_all(loads)

    def step(quad, carry):
        places = [lax.rem(place_ref[0] + z_step_of(quad * 4 + index), Z) for index in range(4)]
        rows = jnp.concatenate([rows_all[:, block, :, :].reshape(inner, BLOCK).T for block in places], 0)
        marks = marks_all[pl.ds(quad * 4, 4)].astype(f32).reshape(4 * BLOCK // TRIAL, width)
        wide = spread(rows, marks, slots)
        chosen = jnp.dot(wide, weight[...].reshape(slots * inner, width), preferred_element_type=f32)
        for index, block in enumerate(places):
            out_ref[block] = chosen[index * BLOCK : (index + 1) * BLOCK].astype(bf16)
        return carry

    lax.fori_loop(0, Z // 4, step, 0)


def along_y(value, step):
    return lax.ppermute(value, "seq", [(z * Y + y, z * Y + (y + step) % Y) for z in range(Z) for y in range(Y)])


def along_z(value, step):
    return lax.ppermute(value, "seq", [(z * Y + y, (z + step) % Z * Y + y) for z in range(Z) for y in range(Y)])


def along_x(value, step):
    pairs = [(x * CORES + c, (x + step) % X * CORES + c) for x in range(X) for c in range(CORES)]
    return lax.ppermute(value, "grp", pairs)


def other_core(value):
    return lax.ppermute(value, "grp", [(group, group ^ 1) for group in range(X * CORES)])


def whole(count):
    return [pl.BlockSpec(memory_space=pltpu.VMEM)] * count


def local(spikes, session_of_bin, session_slot, readin_weight, short_kernel, long_filter, skip_gain, readout_weight, out_grad):
    in_chans = spikes.shape[2]
    model_width = short_kernel.shape[1]
    place = lax.axis_index("seq")
    group = lax.axis_index("grp")
    scalar = pl.BlockSpec(memory_space=pltpu.SMEM)
    hbm = pl.BlockSpec(memory_space=pltpu.HBM)
    z_groups = [[z * Y + y for z in range(Z)] for y in range(Y)]
    y_groups = [[z * Y + y for y in range(Y)] for z in range(Z)]
    coords = jnp.stack([place // Y, place % Y, group // CORES, group % CORES]).astype(jnp.int32)
    first, second, back_second, back_first, twists = transform_tables()
    params = pltpu.CompilerParams(vmem_limit_bytes=60 << 20)
    spectrum_shape = jax.ShapeDtypeStruct((GROUPS, BLOCKS * LANE8, 2 * BLOCK), f32)
    plane = (BLOCKS, CHANS, BLOCK)
    work = 2 * GROUPS * (512 * 256 * 128 + 256 * 256 * 256)
    pair = 2 * LANE8
    same = lambda table: pl.BlockSpec(table.shape, lambda i, rank=table.ndim: (0,) * rank)

    sessions = session_of_bin[0, ::TRIAL]
    matches = sessions[:, None] == jnp.arange(session_slot.shape[0], dtype=jnp.int32)[None, :]
    slots = jnp.sum(jnp.where(matches, session_slot[None, :], 0), axis=1)
    marks = jnp.broadcast_to(slots.astype(bf16)[:, None], (slots.shape[0], in_chans))
    block = jnp.concatenate([spikes[0], marks], 0)
    chunk = jnp.stack([block, along_y(block, 1), along_y(block, -1), along_y(block, 2)])
    right, left = along_z(chunk, 1), along_z(chunk, -1)
    chunks = [chunk, right, left]

    pieces = [lax.dynamic_slice_in_dim(readin_weight, start + place * CHANS, CHANS, 2) for start in (0, model_width)]
    pieces.append(lax.dynamic_slice_in_dim(readout_weight, place // Y * (Y * CHANS), Y * CHANS, 1))
    own = jnp.concatenate(pieces, 2)
    own_right, own_left = along_x(own, 1), along_x(own, -1)

    filter_spectrum = pl.pallas_call(
        filter_kernel,
        out_shape=spectrum_shape,
        grid=(GROUPS // 2,),
        in_specs=[pl.BlockSpec((pair, LENGTH), lambda i: (i, 0))] + [same(table) for table in (first, second, twists)],
        out_specs=pl.BlockSpec((2,) + spectrum_shape.shape[1:], lambda i: (i, 0, 0)),
        compiler_params=params,
        cost_estimate=pl.CostEstimate(flops=work, bytes_accessed=4 << 20, transcendentals=0),
        name="filter_transform",
    )(long_filter, first, second, twists)

    right, left, own_right, own_left, filter_spectrum = lax.optimization_barrier((right, left, own_right, own_left, filter_spectrum))
    right, left = along_z(right, 1), along_z(left, -1)
    chunks += [right, left]
    far = jnp.concatenate([along_x(own_right[:1], 1), along_x(own_left[1:], -1)], 0)
    right, left, far = lax.optimization_barrier((right, left, far))
    right, left = along_z(right, 1), along_z(left, -1)
    chunks += [right, left]
    weights = jnp.stack([own, own_right, own_left, far])
    weights_other = other_core(weights)
    taps = lax.dynamic_slice_in_dim(short_kernel, place * CHANS, CHANS, 1)
    taps = jnp.broadcast_to(taps[:, :, None], (short_kernel.shape[0], CHANS, BLOCK))
    gains = jnp.broadcast_to(skip_gain[:, None], (CHANS, BLOCK))
    right, left, weights_other = lax.optimization_barrier((right, left, weights_other))
    turned = out_grad[0].T.reshape(BLOCKS, CHANS, BLOCK)
    ready = (along_z(right, 1), taps, gains, coords, turned)
    right, taps, gains, coords, turned = lax.optimization_barrier(ready)
    chunks.append(right)
    grads = lax.all_to_all(turned, "seq", split_axis=0, concat_axis=0, tiled=True)

    tables = (first, second, back_second, back_first)
    slot_count = session_slot.shape[0]
    gated, gates, spectrum = pl.pallas_call(
        forward_kernel,
        out_shape=(
            jax.ShapeDtypeStruct((Y, Z, CHANS, BLOCK), bf16),
            jax.ShapeDtypeStruct(plane, bf16),
            spectrum_shape,
        ),
        in_specs=[scalar] + whole(3) + [hbm] * (3 + Z + 4),
        out_specs=tuple(whole(3)),
        scratch_shapes=[
            pltpu.VMEM((BLOCKS, 2 * CHANS, BLOCK), bf16),
            pltpu.VMEM((BLOCKS,) + chunk.shape[1:], bf16),
            pltpu.VMEM((slot_count // 2, in_chans, 4 * CHANS), bf16),
            pltpu.VMEM(spectrum_shape.shape, f32),
        ]
        + [pltpu.VMEM(table.shape, bf16) for table in tables]
        + [pltpu.SemaphoreType.DMA((count,)) for count in (slot_count, Z, 5)],
        compiler_params=params,
        cost_estimate=pl.CostEstimate(flops=4 * work, bytes_accessed=8 << 20, transcendentals=0),
        name="long_convolution",
    )(coords, taps, gains, twists, filter_spectrum, weights, weights_other, *chunks, *tables)

    arrived = lax.all_to_all(gated, "seq", split_axis=0, concat_axis=0, tiled=True, axis_index_groups=y_groups)
    half = CHANS // CORES
    fixed = lambda table: pl.BlockSpec(table.shape, lambda i, place, rank=table.ndim: (0,) * rank)
    steps = half // pair
    halves = pl.pallas_call(
        gradient_kernel,
        out_shape=jax.ShapeDtypeStruct((CORES, half, LENGTH), bf16),
        grid_spec=pltpu.PrefetchScalarGridSpec(
            num_scalar_prefetch=1,
            grid=(GROUPS // 2,),
            in_specs=[pl.BlockSpec((BLOCKS, pair, BLOCK), lambda i, place: (0, i, 0))] * 2
            + [pl.BlockSpec((2,) + spectrum_shape.shape[1:], lambda i, place: (i, 0, 0))]
            + [fixed(table) for table in tables + (twists,)],
            out_specs=pl.BlockSpec((1, pair, LENGTH), lambda i, place: (lax.rem(i // steps + place[3], 2), i % steps, 0)),
        ),
        compiler_params=params,
        cost_estimate=pl.CostEstimate(flops=2 * work, bytes_accessed=4 << 20, transcendentals=0),
        name="filter_gradient",
    )(coords, grads, gates, spectrum, *tables, twists)
    came, arrived = lax.optimization_barrier((other_core(halves[1]), arrived))
    plus = lambda *terms: sum(term.astype(f32) for term in terms).astype(bf16)
    total = plus(halves[0], came)
    cames = [along_x(total, step) for step in (1, -1, 2)]
    partial = pl.pallas_call(
        read_out_kernel,
        out_shape=jax.ShapeDtypeStruct((Z, BLOCK, in_chans), bf16),
        in_specs=[scalar] + [hbm] * (3 + Z),
        out_specs=whole(1)[0],
        scratch_shapes=[
            pltpu.VMEM((slot_count, Y * CHANS, in_chans), bf16),
            pltpu.VMEM((Y, Z, CHANS, BLOCK), bf16),
            pltpu.VMEM((Z, BLOCK // TRIAL, in_chans), bf16),
        ]
        + [pltpu.SemaphoreType.DMA((count,)) for count in (slot_count, Z)]
        + [pltpu.SemaphoreType.DMA],
        compiler_params=params,
        cost_estimate=pl.CostEstimate(flops=2 * 512 * 512 * 4096, bytes_accessed=6 << 20, transcendentals=0),
        name="read_out",
    )(coords, weights, weights_other, arrived, *chunks)
    cames, partial = lax.optimization_barrier((cames, partial))
    total = plus(total, *cames)
    theirs = other_core(total)
    lower = coords[3] == 0
    filter_grad = jnp.concatenate([jnp.where(lower, total, theirs), jnp.where(lower, theirs, total)], 0).astype(f32)
    pieces = lax.all_to_all(partial, "seq", split_axis=0, concat_axis=0, tiled=True, axis_index_groups=z_groups)
    denoised = jnp.sum(pieces.astype(f32), 0).astype(bf16)
    return denoised[None], filter_grad


def solution(mesh):
    placed = (
        P("grp", "seq", None),
        P("grp", "seq"),
        P(),
        P("grp", None, None),
        P(),
        P("seq", None),
        P("seq"),
        P("grp", None, None),
        P("grp", "seq", None),
    )
    return jax.shard_map(
        local,
        mesh=mesh,
        in_specs=placed,
        out_specs=(P("grp", "seq", None), P("seq", None)),
        check_vma=False,
    )
```

```python
import jax
import jax.numpy as jnp
import numpy as np
from jax import lax
from jax.experimental import pallas as pl
from jax.experimental.pallas import tpu as pltpu
from jax.sharding import PartitionSpec as P

BLOCK = 128
TRIAL = 16
Z = 8
Y = 4
BLOCKS = Z * Y
CHANS = 64
LANE8 = 8
GROUPS = CHANS // LANE8
LENGTH = BLOCKS * BLOCK
X = 4
CORES = 2
X_STEPS = (0, -1, 1, 2)
f32 = jnp.float32
bf16 = jnp.bfloat16


def transform_tables():
    slow = np.arange(BLOCKS)
    fast = np.arange(BLOCK)
    first = np.exp(-2j * np.pi * (np.outer(slow, slow) / BLOCKS + slow[None, :] / (4.0 * BLOCKS)))
    twist = np.exp(-2j * np.pi * (slow[:, None] + 0.25) * fast[None, :] / LENGTH)
    second = np.exp(-2j * np.pi * np.outer(fast, fast) / BLOCK)
    eye = np.eye(LANE8)
    spread_first = np.concatenate([np.kron(first.real, eye), np.kron(first.imag, eye)], 0)
    forward_second = np.block([[second.real, second.imag], [-second.imag, second.real]])
    back = second.conj()
    back_second = np.block([[back.real, back.imag], [-back.imag, back.real]])
    back_first = first.conj().T / LENGTH
    spread_back = np.concatenate([np.kron(back_first.real, eye), np.kron(-back_first.imag, eye)], 1)
    as_bf16 = lambda table: jnp.asarray(table.astype(np.float32), bf16)
    twists = np.stack([twist.real, twist.imag]).astype(np.float32)
    return (
        as_bf16(spread_first),
        as_bf16(forward_second),
        as_bf16(back_second),
        as_bf16(spread_back),
        jnp.asarray(twists),
    )


def twists_of(twist_ref):
    shape = (BLOCKS, LANE8, BLOCK)
    cosine = jnp.broadcast_to(twist_ref[0][:, None, :], shape).reshape(BLOCKS * LANE8, BLOCK)
    sine = jnp.broadcast_to(twist_ref[1][:, None, :], shape).reshape(BLOCKS * LANE8, BLOCK)
    return cosine, sine


def forward(low, high, first_ref, second_ref, cosine, sine):
    rows = BLOCKS * LANE8
    signals = jnp.concatenate([low, high], 1).astype(bf16)
    part = jnp.dot(first_ref[...], signals, preferred_element_type=f32)
    turned = []
    for lanes in (slice(0, BLOCK), slice(BLOCK, 2 * BLOCK)):
        real, imag = part[:rows, lanes], part[rows:, lanes]
        turned.append(jnp.concatenate([real * cosine - imag * sine, real * sine + imag * cosine], 1))
    return jnp.dot(jnp.concatenate(turned, 0).astype(bf16), second_ref[...], preferred_element_type=f32)


def backward(spectra, back_second_ref, back_first_ref, cosine, sine):
    rows = BLOCKS * LANE8
    part = jnp.dot(spectra.astype(bf16), back_second_ref[...], preferred_element_type=f32)
    turned = []
    for start in (0, rows):
        real, imag = part[start : start + rows, :BLOCK], part[start : start + rows, BLOCK:]
        turned.append(jnp.concatenate([real * cosine + imag * sine, imag * cosine - real * sine], 0))
    return jnp.dot(back_first_ref[...], jnp.concatenate(turned, 1).astype(bf16), preferred_element_type=f32)


def filter_kernel(filter_ref, first_ref, second_ref, twist_ref, spectrum_ref):
    cosine, sine = twists_of(twist_ref)
    rows = BLOCKS * LANE8
    signals = []
    for start in (0, LANE8):
        pieces = [filter_ref[start : start + LANE8, i * BLOCK : (i + 1) * BLOCK] for i in range(BLOCKS)]
        signals.append(jnp.concatenate(pieces, 0))
    spectra = forward(*signals, first_ref, second_ref, cosine, sine)
    spectrum_ref[...] = spectra.astype(bf16).reshape(2, rows, 2 * BLOCK)


def start_all(copies):
    for copy in copies:
        copy.start()


def wait_all(copies):
    for copy in copies:
        copy.wait()


def weight_copies(place_ref, weight_hbms, take):
    copies = []
    for number, weight_hbm in enumerate(weight_hbms):
        core = place_ref[3] if number < X else 1 - place_ref[3]
        group = lax.rem(place_ref[2] + (X_STEPS[number % X] + X), X) * CORES + core
        for slot in range(2):
            for lanes, target, sem in take(number * 2 + slot, group, slot):
                copies.append(pltpu.make_async_copy(weight_hbm.at[slot, :, lanes], target, sem))
    return copies


def spread(rows, marks, count):
    trials, width = marks.shape
    marks = jnp.broadcast_to(marks[:, None, :], (trials, TRIAL, width)).reshape(trials * TRIAL, width).astype(bf16)
    nothing = jnp.zeros_like(rows)
    return jnp.concatenate([jnp.where(marks == number, rows, nothing) for number in range(count)], 1)


def project(rows_ref, start, blocks, weight):
    width = 2 * CHANS
    in_chans = rows_ref.shape[2]
    rows = rows_ref[pl.ds(start, blocks), :BLOCK, :].reshape(blocks * BLOCK, in_chans)
    marks = rows_ref[pl.ds(start, blocks), BLOCK:, :].astype(f32).reshape(blocks * BLOCK // TRIAL, in_chans)
    wide = spread(rows, jnp.floor(marks * 0.5), weight.shape[0])
    product = jnp.dot(wide, weight[...].reshape(-1, 2 * width), preferred_element_type=f32)
    odd = (marks - 2 * jnp.floor(marks * 0.5))[:, :width]
    trials = odd.shape[0]
    odd = jnp.broadcast_to(odd[:, None, :], (trials, TRIAL, width)).reshape(trials * TRIAL, width)
    chosen = jnp.where(odd > 0.5, product[:, width:], product[:, :width])
    return [chosen[i * BLOCK : (i + 1) * BLOCK].T.astype(bf16) for i in range(blocks)]


def block_of(place_ref, z_step, y_index):
    y_step = jnp.where(y_index < 2, Y - y_index, y_index - 1)
    return lax.rem(place_ref[0] + z_step, Z) * Y + lax.rem(place_ref[1] + y_step, Y)


def z_step_of(index):
    return jnp.where(index % 2 == 1, Z - (index + 1) // 2, index // 2)


def forward_kernel(place_ref, taps_ref, gain_ref, twist_ref, filter_hbm, *rest):
    devices = X * CORES
    weight_hbms = rest[:devices]
    chunk_hbms = rest[devices : devices + Z]
    table_hbms = rest[devices + Z : devices + Z + 4]
    gated_ref, gate_ref, spectrum_ref, both, rows, weight, spectra, *rest = rest[devices + Z + 4 :]
    tables = rest[:4]
    weight_sems, row_sems, sems = rest[4:]
    width = 2 * CHANS
    take = lambda number, group, slot: [
        (pl.ds(0, width), weight.at[group, :, pl.ds(slot * width, width)], weight_sems.at[number])
    ]
    loads = weight_copies(place_ref, weight_hbms, take)
    chunks = []
    for index, chunk in enumerate(chunk_hbms):
        chunks.append(pltpu.make_async_copy(chunk, rows.at[pl.ds(index * Y, Y)], row_sems.at[index]))
    pairs = [(filter_hbm, spectra)] + list(zip(table_hbms, tables))
    others = [pltpu.make_async_copy(source, target, sems.at[index]) for index, (source, target) in enumerate(pairs)]
    start_all(loads)
    start_all(chunks)
    start_all(others)
    wait_all(loads)
    wait_all(chunks)

    def read_in(index, carry):
        blocks = project(rows, index * Y, Y, weight)
        for y_index in range(Y):
            both[block_of(place_ref, z_step_of(index), y_index)] = blocks[y_index]
        return carry

    lax.fori_loop(0, Z, read_in, 0, unroll=2)
    cosine, sine = twists_of(twist_ref)
    lane = lax.broadcasted_iota(jnp.int32, (BLOCKS, LANE8, BLOCK), 2)
    count = BLOCKS * LANE8
    cube = (BLOCKS, LANE8, BLOCK)
    wait_all(others)
    first_ref, second_ref, back_second_ref, back_first_ref = tables

    def short(value, group):
        taps = taps_ref[:, pl.ds(pl.multiple_of(group * LANE8, LANE8), LANE8), :]
        total = taps[0][None] * value
        for shift in (1, 2):
            rolled = pltpu.roll(value.reshape(count, BLOCK), shift, 1).reshape(cube)
            before = jnp.concatenate([jnp.zeros((1, LANE8, BLOCK), f32), rolled[:-1]], 0)
            total = total + taps[shift][None] * jnp.where(lane < shift, before, rolled)
        return total.astype(bf16).astype(f32).reshape(count, BLOCK)

    def step(pair, carry):
        here = pl.ds(pl.multiple_of(pair * 2 * LANE8, 2 * LANE8), 2 * LANE8)
        there = pl.ds(pl.multiple_of(CHANS + pair * 2 * LANE8, 2 * LANE8), 2 * LANE8)
        value = both[:, here, :].astype(f32)
        gate = both[:, there, :]
        signals = [short(value[:, i * LANE8 : (i + 1) * LANE8], pair * 2 + i) for i in range(2)]
        own = forward(*signals, first_ref, second_ref, cosine, sine)
        spectrum_ref[pl.ds(pair * 2, 2)] = own.reshape(2, count, 2 * BLOCK).astype(bf16)
        weight = spectra[pl.ds(pair * 2, 2)].reshape(2 * count, 2 * BLOCK).astype(f32)
        own_re, own_im = own[:, :BLOCK], own[:, BLOCK:]
        filter_re, filter_im = weight[:, :BLOCK], weight[:, BLOCK:]
        mix = jnp.concatenate([own_re * filter_re - own_im * filter_im, own_re * filter_im + own_im * filter_re], 1)
        result = backward(mix, back_second_ref, back_first_ref, cosine, sine)
        signal = jnp.concatenate([piece.reshape(cube) for piece in signals], 1)
        long_part = jnp.concatenate([result[:, i * BLOCK : (i + 1) * BLOCK].reshape(cube) for i in range(2)], 1)
        mixed = (long_part + gain_ref[here, :][None] * signal).astype(bf16).astype(f32)
        gated_ref[:, here, :] = (gate.astype(f32) * mixed).astype(bf16)
        gate_ref[:, here, :] = gate
        return carry

    lax.fori_loop(0, GROUPS // 2, step, 0)


def gradient_kernel(place_ref, grad_ref, gate_ref, spectrum_ref, first_ref, second_ref, back_second_ref, back_first_ref, twist_ref, out_ref):
    cosine, sine = twists_of(twist_ref)
    count = BLOCKS * LANE8
    products = (grad_ref[...].astype(f32) * gate_ref[...].astype(f32)).astype(bf16).astype(f32)
    signals = [products[:, i * LANE8 : (i + 1) * LANE8].reshape(count, BLOCK) for i in range(2)]
    spectra = forward(*signals, first_ref, second_ref, cosine, sine)
    own = spectrum_ref[...].reshape(2 * count, 2 * BLOCK).astype(f32)
    own_re, own_im = own[:, :BLOCK], own[:, BLOCK:]
    grad_re, grad_im = spectra[:, :BLOCK], spectra[:, BLOCK:]
    lag = jnp.concatenate([own_re * grad_re + own_im * grad_im, own_re * grad_im - own_im * grad_re], 1)
    result = backward(lag, back_second_ref, back_first_ref, cosine, sine)
    both = []
    for half in range(2):
        lanes = slice(half * BLOCK, (half + 1) * BLOCK)
        both.append(jnp.concatenate([result[i * LANE8 : (i + 1) * LANE8, lanes] for i in range(BLOCKS)], 1))
    out_ref[0] = jnp.concatenate(both, 0).astype(bf16)


def read_out_kernel(place_ref, rows_hbm, marks_hbm, *rest):
    devices = X * CORES
    weight_hbms = rest[:devices]
    out_ref, weight, rows_all, chunk_all, weight_sems, sems = rest[devices:]
    slots, inner, width = weight.shape
    trials = BLOCK // TRIAL
    top = inner // 2
    take = lambda number, group, slot: [
        (
            pl.ds(2 * CHANS + half * width, width),
            weight.at[group * 2 + slot, pl.ds(half * top, top), :],
            weight_sems.at[number * 2 + half],
        )
        for half in range(2)
    ]
    first = [pltpu.make_async_copy(rows_hbm, rows_all, sems.at[0]), pltpu.make_async_copy(marks_hbm, chunk_all, sems.at[1])]
    loads = weight_copies(place_ref, weight_hbms, take)
    start_all(first)
    start_all(loads)
    wait_all(first)
    places = [block_of(place_ref, 0, index) - place_ref[0] * Y for index in range(Y)]
    rows = jnp.concatenate([rows_all[:, block, :, :].reshape(inner, BLOCK).T for block in places], 0)
    marks = chunk_all[...].astype(f32).reshape(Y * trials, chunk_all.shape[2])
    marks = jnp.concatenate([marks] * (inner // width), 1)
    marks = jnp.broadcast_to(marks[:, None, :], (Y * trials, TRIAL, inner)).reshape(Y * BLOCK, inner).astype(bf16)
    nothing = jnp.zeros_like(rows)
    total = jnp.zeros((Y * BLOCK, width), f32)
    for number in range(0, devices, 2):
        for load in loads[number * 4 : number * 4 + 8]:
            load.wait()
        for offset in range(2):
            core = place_ref[3] if number + offset < X else 1 - place_ref[3]
            group = lax.rem(place_ref[2] + (X_STEPS[(number + offset) % X] + X), X) * CORES + core
            wide = []
            for slot in range(2):
                mark = (group * 2 + slot).astype(f32).astype(bf16)
                wide.append(jnp.where(marks == mark, rows, nothing))
            pair = weight[pl.ds(group * 2, 2)].reshape(2 * inner, width)
            total = total + jnp.dot(jnp.concatenate(wide, 1), pair, preferred_element_type=f32)
    for index, block in enumerate(places):
        out_ref[block] = total[index * BLOCK : (index + 1) * BLOCK].astype(bf16)


def along_y(value, step):
    return lax.ppermute(value, "seq", [(z * Y + y, z * Y + (y + step) % Y) for z in range(Z) for y in range(Y)])


def along_z(value, step):
    return lax.ppermute(value, "seq", [(z * Y + y, (z + step) % Z * Y + y) for z in range(Z) for y in range(Y)])


def along_x(value, step):
    pairs = [(x * CORES + c, (x + step) % X * CORES + c) for x in range(X) for c in range(CORES)]
    return lax.ppermute(value, "grp", pairs)


def other_core(value):
    return lax.ppermute(value, "grp", [(group, group ^ 1) for group in range(X * CORES)])


def whole(count):
    return [pl.BlockSpec(memory_space=pltpu.VMEM)] * count


def local(spikes, session_of_bin, session_slot, readin_weight, short_kernel, long_filter, skip_gain, readout_weight, out_grad):
    in_chans = spikes.shape[2]
    model_width = short_kernel.shape[1]
    place = lax.axis_index("seq")
    group = lax.axis_index("grp")
    scalar = pl.BlockSpec(memory_space=pltpu.SMEM)
    hbm = pl.BlockSpec(memory_space=pltpu.HBM)
    z_groups = [[z * Y + y for z in range(Z)] for y in range(Y)]
    y_groups = [[z * Y + y for y in range(Y)] for z in range(Z)]
    coords = jnp.stack([place // Y, place % Y, group // CORES, group % CORES]).astype(jnp.int32)
    first, second, back_second, back_first, twists = transform_tables()
    params = pltpu.CompilerParams(vmem_limit_bytes=60 << 20)
    spectrum_shape = jax.ShapeDtypeStruct((GROUPS, BLOCKS * LANE8, 2 * BLOCK), bf16)
    plane = (BLOCKS, CHANS, BLOCK)
    work = 2 * GROUPS * (512 * 256 * 128 + 256 * 256 * 256)
    pair = 2 * LANE8
    same = lambda table: pl.BlockSpec(table.shape, lambda i, rank=table.ndim: (0,) * rank)

    sessions = session_of_bin[0, ::TRIAL]
    matches = sessions[:, None] == jnp.arange(session_slot.shape[0], dtype=jnp.int32)[None, :]
    slots = jnp.sum(jnp.where(matches, session_slot[None, :], 0), axis=1)
    marks = jnp.broadcast_to(slots.astype(bf16)[:, None], (slots.shape[0], in_chans))
    block = jnp.concatenate([spikes[0], marks], 0)
    block, readin_weight, readout_weight = lax.optimization_barrier((block, readin_weight, readout_weight))
    chunk = jnp.stack([block, along_y(block, 1), along_y(block, -1), along_y(block, 2)])
    own_marks = chunk[:, BLOCK:, :]
    right, left = along_z(chunk, 1), along_z(chunk, -1)
    chunks = [chunk, right, left]

    pieces = [lax.dynamic_slice_in_dim(readin_weight, start + place * CHANS, CHANS, 2) for start in (0, model_width)]
    split = readout_weight.reshape(2, 2, Z // 2, Y, CHANS, in_chans)
    split = lax.dynamic_index_in_dim(split, place % Y, 3, keepdims=False).reshape(2, 2, Z // 2 * CHANS, in_chans)
    own = jnp.concatenate(pieces + [split[:, 0], split[:, 1]], 2)
    own_right, own_left = along_x(own, 1), along_x(own, -1)
    own_other = other_core(own)

    filter_spectrum = pl.pallas_call(
        filter_kernel,
        out_shape=spectrum_shape,
        grid=(GROUPS // 2,),
        in_specs=[pl.BlockSpec((pair, LENGTH), lambda i: (i, 0))] + [same(table) for table in (first, second, twists)],
        out_specs=pl.BlockSpec((2,) + spectrum_shape.shape[1:], lambda i: (i, 0, 0)),
        compiler_params=params,
        cost_estimate=pl.CostEstimate(flops=work, bytes_accessed=4 << 20, transcendentals=0),
        name="filter_transform",
    )(long_filter, first, second, twists)

    right, left, filter_spectrum, own_marks = lax.optimization_barrier((right, left, filter_spectrum, own_marks))
    right, left = along_z(right, 1), along_z(left, -1)
    chunks += [right, left]
    ready = (right, left, own_right, own_left, own_other)
    right, left, own_right, own_left, own_other = lax.optimization_barrier(ready)
    right, left = along_z(right, 1), along_z(left, -1)
    chunks += [right, left]
    far = along_x(own_right, 1)
    right_other, left_other = other_core(own_right), other_core(own_left)
    taps = lax.dynamic_slice_in_dim(short_kernel, place * CHANS, CHANS, 1)
    taps = jnp.broadcast_to(taps[:, :, None], (short_kernel.shape[0], CHANS, BLOCK))
    gains = jnp.broadcast_to(skip_gain[:, None], (CHANS, BLOCK))
    right, left, far, right_other, left_other = lax.optimization_barrier((right, left, far, right_other, left_other))
    far_other = other_core(far)
    weights = [own, own_right, own_left, far, own_other, right_other, left_other, far_other]
    turned = out_grad[0].T.reshape(BLOCKS, CHANS, BLOCK)
    ready = (along_z(right, 1), taps, gains, coords, turned, weights[-1])
    right, taps, gains, coords, turned, weights[-1] = lax.optimization_barrier(ready)
    chunks.append(right)
    grads = lax.all_to_all(turned, "seq", split_axis=0, concat_axis=0, tiled=True)

    tables = (first, second, back_second, back_first)
    slot_count = session_slot.shape[0]
    gated, gates, spectrum = pl.pallas_call(
        forward_kernel,
        out_shape=(
            jax.ShapeDtypeStruct(plane, bf16),
            jax.ShapeDtypeStruct(plane, bf16),
            spectrum_shape,
        ),
        in_specs=[scalar] + whole(3) + [hbm] * (1 + X * CORES + Z + 4),
        out_specs=tuple(whole(3)),
        scratch_shapes=[
            pltpu.VMEM((BLOCKS, 2 * CHANS, BLOCK), bf16),
            pltpu.VMEM((BLOCKS,) + chunk.shape[1:], bf16),
            pltpu.VMEM((slot_count // 2, in_chans, 4 * CHANS), bf16),
            pltpu.VMEM(spectrum_shape.shape, bf16),
        ]
        + [pltpu.VMEM(table.shape, bf16) for table in tables]
        + [pltpu.SemaphoreType.DMA((count,)) for count in (slot_count, Z, 5)],
        compiler_params=params,
        cost_estimate=pl.CostEstimate(flops=4 * work, bytes_accessed=8 << 20, transcendentals=0),
        name="long_convolution",
    )(coords, taps, gains, twists, filter_spectrum, *weights, *chunks, *tables)

    gated = gated.reshape(Z, Y, CHANS, BLOCK)
    arrived = lax.all_to_all(gated, "seq", split_axis=0, concat_axis=0, tiled=True, axis_index_groups=z_groups)
    half = CHANS // CORES
    fixed = lambda table: pl.BlockSpec(table.shape, lambda i, place, rank=table.ndim: (0,) * rank)
    steps = half // pair
    halves = pl.pallas_call(
        gradient_kernel,
        out_shape=jax.ShapeDtypeStruct((CORES, half, LENGTH), bf16),
        grid_spec=pltpu.PrefetchScalarGridSpec(
            num_scalar_prefetch=1,
            grid=(GROUPS // 2,),
            in_specs=[pl.BlockSpec((BLOCKS, pair, BLOCK), lambda i, place: (0, i, 0))] * 2
            + [pl.BlockSpec((2,) + spectrum_shape.shape[1:], lambda i, place: (i, 0, 0))]
            + [fixed(table) for table in tables + (twists,)],
            out_specs=pl.BlockSpec((1, pair, LENGTH), lambda i, place: (lax.rem(i // steps + place[3], 2), i % steps, 0)),
        ),
        compiler_params=params,
        cost_estimate=pl.CostEstimate(flops=2 * work, bytes_accessed=4 << 20, transcendentals=0),
        name="filter_gradient",
    )(coords, grads, gates, spectrum, *tables, twists)
    came = other_core(halves[1])
    plus = lambda *terms: sum(term.astype(f32) for term in terms).astype(bf16)
    came, arrived = lax.optimization_barrier((came, arrived))
    total = plus(halves[0], came)
    cames = [along_x(total, step) for step in (1, -1, 2)]
    partial = pl.pallas_call(
        read_out_kernel,
        out_shape=jax.ShapeDtypeStruct((Y, BLOCK, in_chans), bf16),
        in_specs=[scalar] + [hbm] * (2 + X * CORES),
        out_specs=whole(1)[0],
        scratch_shapes=[
            pltpu.VMEM((slot_count, Z * CHANS, in_chans), bf16),
            pltpu.VMEM((Z, Y, CHANS, BLOCK), bf16),
            pltpu.VMEM((Y, BLOCK // TRIAL, in_chans), bf16),
        ]
        + [pltpu.SemaphoreType.DMA((count,)) for count in (2 * slot_count, 2)],
        compiler_params=params,
        cost_estimate=pl.CostEstimate(flops=2 * 512 * 512 * 4096, bytes_accessed=6 << 20, transcendentals=0),
        name="read_out",
    )(coords, arrived, own_marks, *weights)
    cames, partial = lax.optimization_barrier((cames, partial))
    total = plus(total, *cames)
    theirs = other_core(total)
    lower = coords[3] == 0
    filter_grad = jnp.concatenate([jnp.where(lower, total, theirs), jnp.where(lower, theirs, total)], 0).astype(f32)
    pieces = lax.all_to_all(partial, "seq", split_axis=0, concat_axis=0, tiled=True, axis_index_groups=y_groups)
    denoised = jnp.sum(pieces.astype(f32), 0).astype(bf16)
    return denoised[None], filter_grad


def solution(mesh):
    placed = (
        P("grp", "seq", None),
        P("grp", "seq"),
        P(),
        P("grp", None, None),
        P(),
        P("seq", None),
        P("seq"),
        P("grp", None, None),
        P("grp", "seq", None),
    )
    return jax.shard_map(
        local,
        mesh=mesh,
        in_specs=placed,
        out_specs=(P("grp", "seq", None), P("seq", None)),
        check_vma=False,
    )
```

```python
import jax
import jax.numpy as jnp
import numpy as np
from jax import lax
from jax.experimental import pallas as pl
from jax.experimental.pallas import tpu as pltpu
from jax.sharding import PartitionSpec as P

BLOCK = 128
TRIAL = 16
Z = 8
Y = 4
BLOCKS = Z * Y
CHANS = 64
LANE8 = 8
GROUPS = CHANS // LANE8
LENGTH = BLOCKS * BLOCK
f32 = jnp.float32
bf16 = jnp.bfloat16


def transform_tables():
    slow = np.arange(BLOCKS)
    fast = np.arange(BLOCK)
    first = np.exp(-2j * np.pi * (np.outer(slow, slow) / BLOCKS + slow[None, :] / (4.0 * BLOCKS)))
    twist = np.exp(-2j * np.pi * (slow[:, None] + 0.25) * fast[None, :] / LENGTH)
    second = np.exp(-2j * np.pi * np.outer(fast, fast) / BLOCK)
    eye = np.eye(LANE8)
    spread_first = np.concatenate([np.kron(first.real, eye), np.kron(first.imag, eye)], 0)
    forward_second = np.block([[second.real, second.imag], [-second.imag, second.real]])
    back = second.conj()
    back_second = np.block([[back.real, back.imag], [-back.imag, back.real]])
    back_first = first.conj().T / LENGTH
    spread_back = np.concatenate([np.kron(back_first.real, eye), np.kron(-back_first.imag, eye)], 1)
    as_bf16 = lambda table: jnp.asarray(table.astype(np.float32), bf16)
    twists = np.stack([twist.real, twist.imag]).astype(np.float32)
    return (
        as_bf16(spread_first),
        as_bf16(forward_second),
        as_bf16(back_second),
        as_bf16(spread_back),
        jnp.asarray(twists),
    )


def twists_of(twist_ref):
    shape = (BLOCKS, LANE8, BLOCK)
    cosine = jnp.broadcast_to(twist_ref[0][:, None, :], shape).reshape(BLOCKS * LANE8, BLOCK)
    sine = jnp.broadcast_to(twist_ref[1][:, None, :], shape).reshape(BLOCKS * LANE8, BLOCK)
    return cosine, sine


def forward(low, high, first_ref, second_ref, cosine, sine):
    rows = BLOCKS * LANE8
    signals = jnp.concatenate([low, high], 1).astype(bf16)
    part = jnp.dot(first_ref[...], signals, preferred_element_type=f32)
    turned = []
    for lanes in (slice(0, BLOCK), slice(BLOCK, 2 * BLOCK)):
        real, imag = part[:rows, lanes], part[rows:, lanes]
        turned.append(jnp.concatenate([real * cosine - imag * sine, real * sine + imag * cosine], 1))
    return jnp.dot(jnp.concatenate(turned, 0).astype(bf16), second_ref[...], preferred_element_type=f32)


def backward(spectra, back_second_ref, back_first_ref, cosine, sine):
    rows = BLOCKS * LANE8
    part = jnp.dot(spectra.astype(bf16), back_second_ref[...], preferred_element_type=f32)
    turned = []
    for start in (0, rows):
        real, imag = part[start : start + rows, :BLOCK], part[start : start + rows, BLOCK:]
        turned.append(jnp.concatenate([real * cosine + imag * sine, imag * cosine - real * sine], 0))
    return jnp.dot(back_first_ref[...], jnp.concatenate(turned, 1).astype(bf16), preferred_element_type=f32)


def filter_kernel(filter_ref, first_ref, second_ref, twist_ref, spectrum_ref):
    cosine, sine = twists_of(twist_ref)
    rows = BLOCKS * LANE8
    signals = []
    for start in (0, LANE8):
        pieces = [filter_ref[start : start + LANE8, i * BLOCK : (i + 1) * BLOCK] for i in range(BLOCKS)]
        signals.append(jnp.concatenate(pieces, 0))
    spectra = forward(*signals, first_ref, second_ref, cosine, sine)
    spectrum_ref[...] = spectra.astype(bf16).reshape(2, rows, 2 * BLOCK)


def start_all(copies):
    for copy in copies:
        copy.start()


def wait_all(copies):
    for copy in copies:
        copy.wait()


def weight_copies(weight_hbm, weight, sems):
    copies = []
    for slot in range(weight_hbm.shape[0]):
        lanes = pl.ds(slot % 2 * 2 * CHANS, 2 * CHANS)
        copies.append(pltpu.make_async_copy(weight_hbm.at[slot], weight.at[slot // 2, :, lanes], sems.at[slot]))
    return copies


def spread(rows, marks, count):
    trials, width = marks.shape
    marks = jnp.broadcast_to(marks[:, None, :], (trials, TRIAL, width)).reshape(trials * TRIAL, width).astype(bf16)
    nothing = jnp.zeros_like(rows)
    return jnp.concatenate([jnp.where(marks == number, rows, nothing) for number in range(count)], 1)


def project(rows_ref, start, blocks, weight):
    width = 2 * CHANS
    in_chans = rows_ref.shape[2]
    rows = rows_ref[pl.ds(start, blocks), :BLOCK, :].reshape(blocks * BLOCK, in_chans)
    marks = rows_ref[pl.ds(start, blocks), BLOCK:, :].astype(f32).reshape(blocks * BLOCK // TRIAL, in_chans)
    wide = spread(rows, jnp.floor(marks * 0.5), weight.shape[0])
    product = jnp.dot(wide, weight[...].reshape(-1, 2 * width), preferred_element_type=f32)
    odd = (marks - 2 * jnp.floor(marks * 0.5))[:, :width]
    trials = odd.shape[0]
    odd = jnp.broadcast_to(odd[:, None, :], (trials, TRIAL, width)).reshape(trials * TRIAL, width)
    chosen = jnp.where(odd > 0.5, product[:, width:], product[:, :width])
    return [chosen[i * BLOCK : (i + 1) * BLOCK].T.astype(bf16) for i in range(blocks)]


def block_of(place_ref, z_step, y_index):
    y_step = jnp.where(y_index < 2, Y - y_index, y_index - 1)
    return lax.rem(place_ref[0] + z_step, Z) * Y + lax.rem(place_ref[1] + y_step, Y)


def z_step_of(index):
    return jnp.where(index % 2 == 1, Z - (index + 1) // 2, index // 2)


def read_in_kernel(weight_hbm, *rest):
    chunk_hbms = rest[:-5]
    out_ref, rows, weight, weight_sems, sems = rest[-5:]
    loads = weight_copies(weight_hbm, weight, weight_sems)
    for index, chunk in enumerate(chunk_hbms):
        loads.append(pltpu.make_async_copy(chunk, rows.at[pl.ds(index * Y, Y)], sems.at[index]))
    start_all(loads)
    wait_all(loads)

    def step(index, carry):
        blocks = project(rows, index * Y, Y, weight)
        for y_index in range(Y):
            out_ref[index * Y + y_index] = blocks[y_index]
        return carry

    lax.fori_loop(0, len(chunk_hbms), step, 0)


def forward_kernel(place_ref, taps_ref, gain_ref, twist_ref, filter_hbm, weight_hbm, early_hbm, *rest):
    late = Z - early_hbm.shape[0] // Y
    chunk_hbms = rest[:late]
    table_hbms = rest[late : late + 4]
    gated_ref, gate_ref, spectrum_ref, both, rows, weight, spectra, *rest = rest[late + 4 :]
    tables = rest[:4]
    weight_sems, row_sems, early_sems, sems = rest[4:]
    loads = weight_copies(weight_hbm, weight, weight_sems)
    for index, chunk in enumerate(chunk_hbms):
        loads.append(pltpu.make_async_copy(chunk, rows.at[pl.ds(index * Y, Y)], row_sems.at[index]))
    others = []
    for index in range(early_hbm.shape[0]):
        target = both.at[block_of(place_ref, z_step_of(index // Y), index % Y)]
        others.append(pltpu.make_async_copy(early_hbm.at[index], target, early_sems.at[index]))
    pairs = [(filter_hbm, spectra)] + list(zip(table_hbms, tables))
    others += [pltpu.make_async_copy(source, target, sems.at[index]) for index, (source, target) in enumerate(pairs)]
    start_all(loads)
    start_all(others)
    wait_all(loads)

    def read_in(index, carry):
        blocks = project(rows, index * Y, Y, weight)
        for y_index in range(Y):
            both[block_of(place_ref, z_step_of(index + Z - late), y_index)] = blocks[y_index]
        return carry

    lax.fori_loop(0, late, read_in, 0)
    cosine, sine = twists_of(twist_ref)
    lane = lax.broadcasted_iota(jnp.int32, (BLOCKS, LANE8, BLOCK), 2)
    count = BLOCKS * LANE8
    cube = (BLOCKS, LANE8, BLOCK)
    wait_all(others)
    first_ref, second_ref, back_second_ref, back_first_ref = tables

    def short(value, group):
        taps = taps_ref[:, pl.ds(pl.multiple_of(group * LANE8, LANE8), LANE8), :]
        total = taps[0][None] * value
        for shift in (1, 2):
            rolled = pltpu.roll(value.reshape(count, BLOCK), shift, 1).reshape(cube)
            before = jnp.concatenate([jnp.zeros((1, LANE8, BLOCK), f32), rolled[:-1]], 0)
            total = total + taps[shift][None] * jnp.where(lane < shift, before, rolled)
        return total.astype(bf16).astype(f32).reshape(count, BLOCK)

    def step(pair, carry):
        here = pl.ds(pl.multiple_of(pair * 2 * LANE8, 2 * LANE8), 2 * LANE8)
        there = pl.ds(pl.multiple_of(CHANS + pair * 2 * LANE8, 2 * LANE8), 2 * LANE8)
        value = both[:, here, :].astype(f32)
        gate = both[:, there, :]
        signals = [short(value[:, i * LANE8 : (i + 1) * LANE8], pair * 2 + i) for i in range(2)]
        own = forward(*signals, first_ref, second_ref, cosine, sine)
        spectrum_ref[pl.ds(pair * 2, 2)] = own.reshape(2, count, 2 * BLOCK).astype(bf16)
        weight = spectra[pl.ds(pair * 2, 2)].reshape(2 * count, 2 * BLOCK).astype(f32)
        own_re, own_im = own[:, :BLOCK], own[:, BLOCK:]
        filter_re, filter_im = weight[:, :BLOCK], weight[:, BLOCK:]
        mix = jnp.concatenate([own_re * filter_re - own_im * filter_im, own_re * filter_im + own_im * filter_re], 1)
        result = backward(mix, back_second_ref, back_first_ref, cosine, sine)
        signal = jnp.concatenate([piece.reshape(cube) for piece in signals], 1)
        long_part = jnp.concatenate([result[:, i * BLOCK : (i + 1) * BLOCK].reshape(cube) for i in range(2)], 1)
        mixed = (long_part + gain_ref[here, :][None] * signal).astype(bf16).astype(f32)
        gated_ref[:, here, :] = (gate.astype(f32) * mixed).astype(bf16)
        gate_ref[:, here, :] = gate
        return carry

    lax.fori_loop(0, GROUPS // 2, step, 0)


def gradient_kernel(grad_ref, gate_ref, spectrum_ref, first_ref, second_ref, back_second_ref, back_first_ref, twist_ref, out_ref):
    cosine, sine = twists_of(twist_ref)
    count = BLOCKS * LANE8
    products = (grad_ref[...].astype(f32) * gate_ref[...].astype(f32)).astype(bf16).astype(f32)
    signals = [products[:, i * LANE8 : (i + 1) * LANE8].reshape(count, BLOCK) for i in range(2)]
    spectra = forward(*signals, first_ref, second_ref, cosine, sine)
    own = spectrum_ref[...].reshape(2 * count, 2 * BLOCK).astype(f32)
    own_re, own_im = own[:, :BLOCK], own[:, BLOCK:]
    grad_re, grad_im = spectra[:, :BLOCK], spectra[:, BLOCK:]
    lag = jnp.concatenate([own_re * grad_re + own_im * grad_im, own_re * grad_im - own_im * grad_re], 1)
    result = backward(lag, back_second_ref, back_first_ref, cosine, sine)
    both = []
    for half in range(2):
        lanes = slice(half * BLOCK, (half + 1) * BLOCK)
        both.append(jnp.concatenate([result[i * LANE8 : (i + 1) * LANE8, lanes] for i in range(BLOCKS)], 1))
    out_ref[...] = jnp.concatenate(both, 0).astype(bf16)


def read_out_kernel(place_ref, rows_hbm, marks_hbm, weight_hbm, out_ref, weight, rows_all, chunk_all, weight_sems, sems):
    slots, inner, width = weight.shape
    trials = BLOCK // TRIAL
    first = [pltpu.make_async_copy(rows_hbm, rows_all, sems.at[0]), pltpu.make_async_copy(marks_hbm, chunk_all, sems.at[1])]
    loads = [pltpu.make_async_copy(weight_hbm.at[slot], weight.at[slot], weight_sems.at[slot]) for slot in range(slots)]
    start_all(first)
    start_all(loads)
    wait_all(first)
    places = [block_of(place_ref, 0, index) - place_ref[0] * Y for index in range(Y)]
    rows = jnp.concatenate([rows_all[:, block, :, :].reshape(inner, BLOCK).T for block in places], 0)
    marks = chunk_all[...].astype(f32).reshape(Y * trials, chunk_all.shape[2])
    marks = jnp.concatenate([marks] * (inner // width), 1)
    total = jnp.zeros((Y * BLOCK, width), f32)
    part = slots // 2
    for start in range(0, slots, part):
        wait_all(loads[start : start + part])
        wide = spread(rows, marks - start, part)
        total = total + jnp.dot(wide, weight[start : start + part].reshape(part * inner, width), preferred_element_type=f32)
    for index, block in enumerate(places):
        out_ref[block] = total[index * BLOCK : (index + 1) * BLOCK].astype(bf16)


def sum_kernel(parts_ref, out_ref):
    total = parts_ref[0].astype(f32)
    for index in range(1, parts_ref.shape[0]):
        total = total + parts_ref[index].astype(f32)
    out_ref[...] = total


def along_y(value, step):
    return lax.ppermute(value, "seq", [(z * Y + y, z * Y + (y + step) % Y) for z in range(Z) for y in range(Y)])


def along_z(value, step):
    return lax.ppermute(value, "seq", [(z * Y + y, (z + step) % Z * Y + y) for z in range(Z) for y in range(Y)])


def whole(count):
    return [pl.BlockSpec(memory_space=pltpu.VMEM)] * count


def local(spikes, session_of_bin, session_slot, readin_weight, short_kernel, long_filter, skip_gain, readout_weight, out_grad):
    in_chans = spikes.shape[2]
    model_width = short_kernel.shape[1]
    place = lax.axis_index("seq")
    scalar = pl.BlockSpec(memory_space=pltpu.SMEM)
    hbm = pl.BlockSpec(memory_space=pltpu.HBM)
    z_groups = [[z * Y + y for z in range(Z)] for y in range(Y)]
    y_groups = [[z * Y + y for y in range(Y)] for z in range(Z)]
    coords = jnp.stack([place // Y, place % Y]).astype(jnp.int32)
    first, second, back_second, back_first, twists = transform_tables()
    params = pltpu.CompilerParams(vmem_limit_bytes=60 << 20)
    spectrum_shape = jax.ShapeDtypeStruct((GROUPS, BLOCKS * LANE8, 2 * BLOCK), bf16)
    plane = (BLOCKS, CHANS, BLOCK)
    work = 2 * GROUPS * (512 * 256 * 128 + 256 * 256 * 256)
    pair = 2 * LANE8
    same = lambda table: pl.BlockSpec(table.shape, lambda i, rank=table.ndim: (0,) * rank)

    sessions = session_of_bin[0, ::TRIAL]
    matches = sessions[:, None] == jnp.arange(session_slot.shape[0], dtype=jnp.int32)[None, :]
    slots = jnp.sum(jnp.where(matches, session_slot[None, :], 0), axis=1)
    marks = jnp.broadcast_to(slots.astype(bf16)[:, None], (slots.shape[0], in_chans))
    block = jnp.concatenate([spikes[0], marks], 0)
    chunk = jnp.stack([block, along_y(block, 1), along_y(block, -1), along_y(block, 2)])
    own_marks = chunk[:, BLOCK:, :]
    right, left = along_z(chunk, 1), along_z(chunk, -1)
    chunks = [chunk, right, left]

    pieces = [lax.dynamic_slice_in_dim(readin_weight, start + place * CHANS, CHANS, 2) for start in (0, model_width)]
    in_weights = lax.all_gather(jnp.concatenate(pieces, 2), "grp", axis=0, tiled=True)
    split = readout_weight.reshape(2, Z, Y, CHANS, in_chans)
    split = lax.dynamic_index_in_dim(split, place % Y, 2, keepdims=False).reshape(2, Z * CHANS, in_chans)
    out_weights = lax.all_gather(split, "grp", axis=0, tiled=True)

    filter_spectrum = pl.pallas_call(
        filter_kernel,
        out_shape=spectrum_shape,
        grid=(GROUPS // 2,),
        in_specs=[pl.BlockSpec((pair, LENGTH), lambda i: (i, 0))] + [same(table) for table in (first, second, twists)],
        out_specs=pl.BlockSpec((2,) + spectrum_shape.shape[1:], lambda i: (i, 0, 0)),
        compiler_params=params,
        cost_estimate=pl.CostEstimate(flops=work, bytes_accessed=4 << 20, transcendentals=0),
        name="filter_transform",
    )(long_filter, first, second, twists)

    right, left, filter_spectrum, own_marks = lax.optimization_barrier((right, left, filter_spectrum, own_marks))
    right, left = along_z(right, 1), along_z(left, -1)
    chunks += [right, left]
    turned = out_grad[0].T.reshape(BLOCKS, CHANS, BLOCK)
    taps = lax.dynamic_slice_in_dim(short_kernel, place * CHANS, CHANS, 1)
    taps = jnp.broadcast_to(taps[:, :, None], (short_kernel.shape[0], CHANS, BLOCK))
    gains = jnp.broadcast_to(skip_gain[:, None], (CHANS, BLOCK))
    ready = (right, left, taps, gains, coords, turned)
    right, left, taps, gains, coords, turned = lax.optimization_barrier(ready)
    right, left = along_z(right, 1), along_z(left, -1)
    slot_count = session_slot.shape[0]
    width = 2 * CHANS
    early_blocks = len(chunks) * Y
    early = pl.pallas_call(
        read_in_kernel,
        out_shape=jax.ShapeDtypeStruct((early_blocks, width, BLOCK), bf16),
        in_specs=[hbm] * (1 + len(chunks)),
        out_specs=whole(1)[0],
        scratch_shapes=[
            pltpu.VMEM((early_blocks,) + chunk.shape[1:], bf16),
            pltpu.VMEM((slot_count // 2, in_chans, 2 * width), bf16),
            pltpu.SemaphoreType.DMA((slot_count,)),
            pltpu.SemaphoreType.DMA((len(chunks),)),
        ],
        compiler_params=params,
        cost_estimate=pl.CostEstimate(flops=work, bytes_accessed=4 << 20, transcendentals=0),
        name="read_in",
    )(in_weights, *chunks)
    right, left, early = lax.optimization_barrier((right, left, early))
    late = [right, left, along_z(right, 1)]
    late[2], turned = lax.optimization_barrier((late[2], turned))
    grads = lax.all_to_all(turned, "seq", split_axis=0, concat_axis=0, tiled=True)

    tables = (first, second, back_second, back_first)
    gated, gates, spectrum = pl.pallas_call(
        forward_kernel,
        out_shape=(
            jax.ShapeDtypeStruct(plane, bf16),
            jax.ShapeDtypeStruct(plane, bf16),
            spectrum_shape,
        ),
        in_specs=[scalar] + whole(3) + [hbm] * (3 + len(late) + 4),
        out_specs=tuple(whole(3)),
        scratch_shapes=[
            pltpu.VMEM((BLOCKS, 2 * CHANS, BLOCK), bf16),
            pltpu.VMEM((len(late) * Y,) + chunk.shape[1:], bf16),
            pltpu.VMEM((slot_count // 2, in_chans, 4 * CHANS), bf16),
            pltpu.VMEM(spectrum_shape.shape, bf16),
        ]
        + [pltpu.VMEM(table.shape, bf16) for table in tables]
        + [pltpu.SemaphoreType.DMA((count,)) for count in (slot_count, len(late), early_blocks, 5)],
        compiler_params=params,
        cost_estimate=pl.CostEstimate(flops=4 * work, bytes_accessed=8 << 20, transcendentals=0),
        name="long_convolution",
    )(coords, taps, gains, twists, filter_spectrum, in_weights, early, *late, *tables)

    gated = gated.reshape(Z, Y, CHANS, BLOCK)
    arrived = lax.all_to_all(gated, "seq", split_axis=0, concat_axis=0, tiled=True, axis_index_groups=z_groups)
    own_grad = pl.pallas_call(
        gradient_kernel,
        out_shape=jax.ShapeDtypeStruct((CHANS, LENGTH), bf16),
        grid=(GROUPS // 2,),
        in_specs=[pl.BlockSpec((BLOCKS, pair, BLOCK), lambda i: (0, i, 0))] * 2
        + [pl.BlockSpec((2,) + spectrum_shape.shape[1:], lambda i: (i, 0, 0))]
        + [same(table) for table in tables + (twists,)],
        out_specs=pl.BlockSpec((pair, LENGTH), lambda i: (i, 0)),
        compiler_params=params,
        cost_estimate=pl.CostEstimate(flops=2 * work, bytes_accessed=4 << 20, transcendentals=0),
        name="filter_gradient",
    )(grads, gates, spectrum, *tables, twists)
    all_grads = lax.all_gather(own_grad, "grp", axis=0, tiled=False)
    lanes = LENGTH // 8
    filter_grad = pl.pallas_call(
        sum_kernel,
        out_shape=jax.ShapeDtypeStruct((CHANS, LENGTH), f32),
        grid=(LENGTH // lanes,),
        in_specs=[pl.BlockSpec((all_grads.shape[0], CHANS, lanes), lambda i: (0, 0, i))],
        out_specs=pl.BlockSpec((CHANS, lanes), lambda i: (0, i)),
        compiler_params=params,
        cost_estimate=pl.CostEstimate(flops=all_grads.size, bytes_accessed=5 << 20, transcendentals=0),
        name="sum_gradients",
    )(all_grads)
    partial = pl.pallas_call(
        read_out_kernel,
        out_shape=jax.ShapeDtypeStruct((Y, BLOCK, in_chans), bf16),
        in_specs=[scalar] + [hbm] * 3,
        out_specs=whole(1)[0],
        scratch_shapes=[
            pltpu.VMEM(out_weights.shape, bf16),
            pltpu.VMEM((Z, Y, CHANS, BLOCK), bf16),
            pltpu.VMEM((Y, BLOCK // TRIAL, in_chans), bf16),
        ]
        + [pltpu.SemaphoreType.DMA((count,)) for count in (slot_count, 2)],
        compiler_params=params,
        cost_estimate=pl.CostEstimate(flops=2 * 512 * 512 * 4096, bytes_accessed=6 << 20, transcendentals=0),
        name="read_out",
    )(coords, arrived, own_marks, out_weights)
    pieces = lax.all_to_all(partial, "seq", split_axis=0, concat_axis=0, tiled=True, axis_index_groups=y_groups)
    denoised = jnp.sum(pieces.astype(f32), 0).astype(bf16)
    return denoised[None], filter_grad


def solution(mesh):
    placed = (
        P("grp", "seq", None),
        P("grp", "seq"),
        P(),
        P("grp", None, None),
        P(),
        P("seq", None),
        P("seq"),
        P("grp", None, None),
        P("grp", "seq", None),
    )
    return jax.shard_map(
        local,
        mesh=mesh,
        in_specs=placed,
        out_specs=(P("grp", "seq", None), P("seq", None)),
        check_vma=False,
    )
```

```python
import jax
import jax.numpy as jnp
import numpy as np
from jax import lax
from jax.experimental import pallas as pl
from jax.experimental.pallas import tpu as pltpu
from jax.sharding import PartitionSpec as P

BLOCK = 128
TRIAL = 16
Z = 8
Y = 4
BLOCKS = Z * Y
CHANS = 64
LANE8 = 8
GROUPS = CHANS // LANE8
LENGTH = BLOCKS * BLOCK
f32 = jnp.float32
bf16 = jnp.bfloat16


def transform_tables():
    slow = np.arange(BLOCKS)
    fast = np.arange(BLOCK)
    first = np.exp(-2j * np.pi * (np.outer(slow, slow) / BLOCKS + slow[None, :] / (4.0 * BLOCKS)))
    twist = np.exp(-2j * np.pi * (slow[:, None] + 0.25) * fast[None, :] / LENGTH)
    second = np.exp(-2j * np.pi * np.outer(fast, fast) / BLOCK)
    eye = np.eye(LANE8)
    spread_first = np.concatenate([np.kron(first.real, eye), np.kron(first.imag, eye)], 0)
    forward_second = np.block([[second.real, second.imag], [-second.imag, second.real]])
    back = second.conj()
    back_second = np.block([[back.real, back.imag], [-back.imag, back.real]])
    back_first = first.conj().T / LENGTH
    spread_back = np.concatenate([np.kron(back_first.real, eye), np.kron(-back_first.imag, eye)], 1)
    as_bf16 = lambda table: jnp.asarray(table.astype(np.float32), bf16)
    twists = np.stack([twist.real, twist.imag]).astype(np.float32)
    return (
        as_bf16(spread_first),
        as_bf16(forward_second),
        as_bf16(back_second),
        as_bf16(spread_back),
        jnp.asarray(twists),
    )


def twists_of(twist_ref):
    shape = (BLOCKS, LANE8, BLOCK)
    cosine = jnp.broadcast_to(twist_ref[0][:, None, :], shape).reshape(BLOCKS * LANE8, BLOCK)
    sine = jnp.broadcast_to(twist_ref[1][:, None, :], shape).reshape(BLOCKS * LANE8, BLOCK)
    return cosine, sine


def forward(low, high, first_ref, second_ref, cosine, sine):
    rows = BLOCKS * LANE8
    signals = jnp.concatenate([low, high], 1).astype(bf16)
    part = jnp.dot(first_ref[...], signals, preferred_element_type=f32)
    turned = []
    for lanes in (slice(0, BLOCK), slice(BLOCK, 2 * BLOCK)):
        real, imag = part[:rows, lanes], part[rows:, lanes]
        turned.append(jnp.concatenate([real * cosine - imag * sine, real * sine + imag * cosine], 1))
    return jnp.dot(jnp.concatenate(turned, 0).astype(bf16), second_ref[...], preferred_element_type=f32)


def backward(spectra, back_second_ref, back_first_ref, cosine, sine):
    rows = BLOCKS * LANE8
    part = jnp.dot(spectra.astype(bf16), back_second_ref[...], preferred_element_type=f32)
    turned = []
    for start in (0, rows):
        real, imag = part[start : start + rows, :BLOCK], part[start : start + rows, BLOCK:]
        turned.append(jnp.concatenate([real * cosine + imag * sine, imag * cosine - real * sine], 0))
    return jnp.dot(back_first_ref[...], jnp.concatenate(turned, 1).astype(bf16), preferred_element_type=f32)


def filter_kernel(filter_ref, first_ref, second_ref, twist_ref, spectrum_ref):
    cosine, sine = twists_of(twist_ref)
    rows = BLOCKS * LANE8
    signals = []
    for start in (0, LANE8):
        pieces = [filter_ref[start : start + LANE8, i * BLOCK : (i + 1) * BLOCK] for i in range(BLOCKS)]
        signals.append(jnp.concatenate(pieces, 0))
    spectra = forward(*signals, first_ref, second_ref, cosine, sine)
    spectrum_ref[...] = spectra.astype(bf16).reshape(2, rows, 2 * BLOCK)


def start_all(copies):
    for copy in copies:
        copy.start()


def wait_all(copies):
    for copy in copies:
        copy.wait()


def weight_copies(weight_hbm, weight, sems):
    copies = []
    for slot in range(weight_hbm.shape[0]):
        lanes = pl.ds(slot % 2 * 2 * CHANS, 2 * CHANS)
        copies.append(pltpu.make_async_copy(weight_hbm.at[slot], weight.at[slot // 2, :, lanes], sems.at[slot]))
    return copies


def spread(rows, marks, count):
    trials, width = marks.shape
    marks = jnp.broadcast_to(marks[:, None, :], (trials, TRIAL, width)).reshape(trials * TRIAL, width).astype(bf16)
    nothing = jnp.zeros_like(rows)
    return jnp.concatenate([jnp.where(marks == number, rows, nothing) for number in range(count)], 1)


def project(rows_ref, start, blocks, weight):
    width = 2 * CHANS
    in_chans = rows_ref.shape[2]
    rows = rows_ref[pl.ds(start, blocks), :BLOCK, :].reshape(blocks * BLOCK, in_chans)
    marks = rows_ref[pl.ds(start, blocks), BLOCK:, :].astype(f32).reshape(blocks * BLOCK // TRIAL, in_chans)
    wide = spread(rows, jnp.floor(marks * 0.5), weight.shape[0])
    product = jnp.dot(wide, weight[...].reshape(-1, 2 * width), preferred_element_type=f32)
    odd = (marks - 2 * jnp.floor(marks * 0.5))[:, :width]
    trials = odd.shape[0]
    odd = jnp.broadcast_to(odd[:, None, :], (trials, TRIAL, width)).reshape(trials * TRIAL, width)
    chosen = jnp.where(odd > 0.5, product[:, width:], product[:, :width])
    return [chosen[i * BLOCK : (i + 1) * BLOCK].T.astype(bf16) for i in range(blocks)]


def block_of(place_ref, z_step, y_index):
    y_step = jnp.where(y_index < 2, Y - y_index, y_index - 1)
    return lax.rem(place_ref[0] + z_step, Z) * Y + lax.rem(place_ref[1] + y_step, Y)


def z_step_of(index):
    return jnp.where(index % 2 == 1, Z - (index + 1) // 2, index // 2)


def read_in_kernel(weight_hbm, *rest):
    chunk_hbms = rest[:-5]
    out_ref, rows, weight, weight_sems, sems = rest[-5:]
    loads = weight_copies(weight_hbm, weight, weight_sems)
    for index, chunk in enumerate(chunk_hbms):
        loads.append(pltpu.make_async_copy(chunk, rows.at[pl.ds(index * Y, Y)], sems.at[index]))
    start_all(loads)
    wait_all(loads)

    def step(index, carry):
        blocks = project(rows, index * Y, Y, weight)
        for y_index in range(Y):
            out_ref[index * Y + y_index] = blocks[y_index]
        return carry

    lax.fori_loop(0, len(chunk_hbms), step, 0)


def forward_kernel(place_ref, taps_ref, gain_ref, twist_ref, filter_hbm, weight_hbm, early_hbm, *rest):
    late = Z - early_hbm.shape[0] // Y
    chunk_hbms = rest[:late]
    table_hbms = rest[late : late + 4]
    gated_ref, gate_ref, spectrum_ref, both, rows, weight, spectra, *rest = rest[late + 4 :]
    tables = rest[:4]
    weight_sems, row_sems, early_sems, sems = rest[4:]
    loads = weight_copies(weight_hbm, weight, weight_sems)
    for index, chunk in enumerate(chunk_hbms):
        loads.append(pltpu.make_async_copy(chunk, rows.at[pl.ds(index * Y, Y)], row_sems.at[index]))
    others = []
    for index in range(early_hbm.shape[0]):
        target = both.at[block_of(place_ref, z_step_of(index // Y), index % Y)]
        others.append(pltpu.make_async_copy(early_hbm.at[index], target, early_sems.at[index]))
    pairs = [(filter_hbm, spectra)] + list(zip(table_hbms, tables))
    others += [pltpu.make_async_copy(source, target, sems.at[index]) for index, (source, target) in enumerate(pairs)]
    start_all(loads)
    start_all(others)
    wait_all(loads)

    def read_in(index, carry):
        blocks = project(rows, index * Y, Y, weight)
        for y_index in range(Y):
            both[block_of(place_ref, z_step_of(index + Z - late), y_index)] = blocks[y_index]
        return carry

    lax.fori_loop(0, late, read_in, 0)
    cosine, sine = twists_of(twist_ref)
    lane = lax.broadcasted_iota(jnp.int32, (BLOCKS, LANE8, BLOCK), 2)
    count = BLOCKS * LANE8
    cube = (BLOCKS, LANE8, BLOCK)
    wait_all(others)
    first_ref, second_ref, back_second_ref, back_first_ref = tables

    def short(value, group):
        taps = taps_ref[:, pl.ds(pl.multiple_of(group * LANE8, LANE8), LANE8), :]
        total = taps[0][None] * value
        for shift in (1, 2):
            rolled = pltpu.roll(value.reshape(count, BLOCK), shift, 1).reshape(cube)
            before = jnp.concatenate([jnp.zeros((1, LANE8, BLOCK), f32), rolled[:-1]], 0)
            total = total + taps[shift][None] * jnp.where(lane < shift, before, rolled)
        return total.astype(bf16).astype(f32).reshape(count, BLOCK)

    def step(pair, carry):
        here = pl.ds(pl.multiple_of(pair * 2 * LANE8, 2 * LANE8), 2 * LANE8)
        there = pl.ds(pl.multiple_of(CHANS + pair * 2 * LANE8, 2 * LANE8), 2 * LANE8)
        value = both[:, here, :].astype(f32)
        gate = both[:, there, :]
        signals = [short(value[:, i * LANE8 : (i + 1) * LANE8], pair * 2 + i) for i in range(2)]
        own = forward(*signals, first_ref, second_ref, cosine, sine)
        spectrum_ref[pl.ds(pair * 2, 2)] = own.reshape(2, count, 2 * BLOCK).astype(bf16)
        weight = spectra[pl.ds(pair * 2, 2)].reshape(2 * count, 2 * BLOCK).astype(f32)
        own_re, own_im = own[:, :BLOCK], own[:, BLOCK:]
        filter_re, filter_im = weight[:, :BLOCK], weight[:, BLOCK:]
        mix = jnp.concatenate([own_re * filter_re - own_im * filter_im, own_re * filter_im + own_im * filter_re], 1)
        result = backward(mix, back_second_ref, back_first_ref, cosine, sine)
        signal = jnp.concatenate([piece.reshape(cube) for piece in signals], 1)
        long_part = jnp.concatenate([result[:, i * BLOCK : (i + 1) * BLOCK].reshape(cube) for i in range(2)], 1)
        mixed = (long_part + gain_ref[here, :][None] * signal).astype(bf16).astype(f32)
        gated_ref[:, here, :] = (gate.astype(f32) * mixed).astype(bf16)
        gate_ref[:, here, :] = gate
        return carry

    lax.fori_loop(0, GROUPS // 2, step, 0, unroll=2)


def gradient_kernel(grad_ref, gate_ref, spectrum_ref, first_ref, second_ref, back_second_ref, back_first_ref, twist_ref, out_ref):
    cosine, sine = twists_of(twist_ref)
    count = BLOCKS * LANE8
    pair = 2 * LANE8
    for start in range(0, grad_ref.shape[1], pair):
        here = slice(start, start + pair)
        products = (grad_ref[:, here, :].astype(f32) * gate_ref[:, here, :].astype(f32)).astype(bf16).astype(f32)
        signals = [products[:, i * LANE8 : (i + 1) * LANE8].reshape(count, BLOCK) for i in range(2)]
        spectra = forward(*signals, first_ref, second_ref, cosine, sine)
        own = spectrum_ref[start // LANE8 : start // LANE8 + 2].reshape(2 * count, 2 * BLOCK).astype(f32)
        own_re, own_im = own[:, :BLOCK], own[:, BLOCK:]
        grad_re, grad_im = spectra[:, :BLOCK], spectra[:, BLOCK:]
        lag = jnp.concatenate([own_re * grad_re + own_im * grad_im, own_re * grad_im - own_im * grad_re], 1)
        result = backward(lag, back_second_ref, back_first_ref, cosine, sine)
        both = []
        for half in range(2):
            lanes = slice(half * BLOCK, (half + 1) * BLOCK)
            both.append(jnp.concatenate([result[i * LANE8 : (i + 1) * LANE8, lanes] for i in range(BLOCKS)], 1))
        out_ref[here, :] = jnp.concatenate(both, 0).astype(bf16)


def read_out_kernel(place_ref, rows_hbm, marks_hbm, weight_hbm, out_ref, weight, rows_all, chunk_all, weight_sems, sems):
    slots, inner, width = weight.shape
    trials = BLOCK // TRIAL
    first = [pltpu.make_async_copy(rows_hbm, rows_all, sems.at[0]), pltpu.make_async_copy(marks_hbm, chunk_all, sems.at[1])]
    loads = [pltpu.make_async_copy(weight_hbm.at[slot], weight.at[slot], weight_sems.at[slot]) for slot in range(slots)]
    start_all(first)
    start_all(loads)
    wait_all(first)
    places = [block_of(place_ref, 0, index) - place_ref[0] * Y for index in range(Y)]
    rows = jnp.concatenate([rows_all[:, block, :, :].reshape(inner, BLOCK).T for block in places], 0)
    marks = chunk_all[...].astype(f32).reshape(Y * trials, chunk_all.shape[2])
    marks = jnp.concatenate([marks] * (inner // width), 1)
    total = jnp.zeros((Y * BLOCK, width), f32)
    part = slots // 4
    for start in range(0, slots, part):
        wait_all(loads[start : start + part])
        wide = spread(rows, marks - start, part)
        total = total + jnp.dot(wide, weight[start : start + part].reshape(part * inner, width), preferred_element_type=f32)
    for index, block in enumerate(places):
        out_ref[block] = total[index * BLOCK : (index + 1) * BLOCK].astype(bf16)


def sum_kernel(parts_ref, pick_ref, out_ref):
    count, rows, lanes = parts_ref.shape
    out_ref[...] = jnp.dot(pick_ref[...], parts_ref[...].reshape(count * rows, lanes), preferred_element_type=f32)


def along_y(value, step):
    return lax.ppermute(value, "seq", [(z * Y + y, z * Y + (y + step) % Y) for z in range(Z) for y in range(Y)])


def along_z(value, step):
    return lax.ppermute(value, "seq", [(z * Y + y, (z + step) % Z * Y + y) for z in range(Z) for y in range(Y)])


def whole(count):
    return [pl.BlockSpec(memory_space=pltpu.VMEM)] * count


def local(spikes, session_of_bin, session_slot, readin_weight, short_kernel, long_filter, skip_gain, readout_weight, out_grad):
    in_chans = spikes.shape[2]
    model_width = short_kernel.shape[1]
    place = lax.axis_index("seq")
    scalar = pl.BlockSpec(memory_space=pltpu.SMEM)
    hbm = pl.BlockSpec(memory_space=pltpu.HBM)
    z_groups = [[z * Y + y for z in range(Z)] for y in range(Y)]
    y_groups = [[z * Y + y for y in range(Y)] for z in range(Z)]
    coords = jnp.stack([place // Y, place % Y]).astype(jnp.int32)
    first, second, back_second, back_first, twists = transform_tables()
    params = pltpu.CompilerParams(vmem_limit_bytes=60 << 20)
    spectrum_shape = jax.ShapeDtypeStruct((GROUPS, BLOCKS * LANE8, 2 * BLOCK), bf16)
    plane = (BLOCKS, CHANS, BLOCK)
    work = 2 * GROUPS * (512 * 256 * 128 + 256 * 256 * 256)
    pair = 2 * LANE8
    same = lambda table: pl.BlockSpec(table.shape, lambda i, rank=table.ndim: (0,) * rank)

    sessions = session_of_bin[0, ::TRIAL]
    matches = sessions[:, None] == jnp.arange(session_slot.shape[0], dtype=jnp.int32)[None, :]
    slots = jnp.sum(jnp.where(matches, session_slot[None, :], 0), axis=1)
    marks = jnp.broadcast_to(slots.astype(bf16)[:, None], (slots.shape[0], in_chans))
    block = jnp.concatenate([spikes[0], marks], 0)
    chunk = jnp.stack([block, along_y(block, 1), along_y(block, -1), along_y(block, 2)])
    chunk, readout_weight = lax.optimization_barrier((chunk, readout_weight))
    own_marks = chunk[:, BLOCK:, :]
    right, left = along_z(chunk, 1), along_z(chunk, -1)
    chunks = [chunk, right, left]

    pieces = [lax.dynamic_slice_in_dim(readin_weight, start + place * CHANS, CHANS, 2) for start in (0, model_width)]
    in_weights = lax.all_gather(jnp.concatenate(pieces, 2), "grp", axis=0, tiled=True)
    split = readout_weight.reshape(2, Z, Y, CHANS, in_chans)
    split = lax.dynamic_index_in_dim(split, place % Y, 2, keepdims=False).reshape(2, Z * CHANS, in_chans)
    out_weights = lax.all_gather(split, "grp", axis=0, tiled=True)

    filter_spectrum = pl.pallas_call(
        filter_kernel,
        out_shape=spectrum_shape,
        grid=(GROUPS // 2,),
        in_specs=[pl.BlockSpec((pair, LENGTH), lambda i: (i, 0))] + [same(table) for table in (first, second, twists)],
        out_specs=pl.BlockSpec((2,) + spectrum_shape.shape[1:], lambda i: (i, 0, 0)),
        compiler_params=params,
        cost_estimate=pl.CostEstimate(flops=work, bytes_accessed=4 << 20, transcendentals=0),
        name="filter_transform",
    )(long_filter, first, second, twists)

    right, left, filter_spectrum, own_marks = lax.optimization_barrier((right, left, filter_spectrum, own_marks))
    right, left = along_z(right, 1), along_z(left, -1)
    chunks += [right, left]
    turned = out_grad[0].T.reshape(BLOCKS, CHANS, BLOCK)
    taps = lax.dynamic_slice_in_dim(short_kernel, place * CHANS, CHANS, 1)
    taps = jnp.broadcast_to(taps[:, :, None], (short_kernel.shape[0], CHANS, BLOCK))
    gains = jnp.broadcast_to(skip_gain[:, None], (CHANS, BLOCK))
    ready = (right, left, taps, gains, coords, turned)
    right, left, taps, gains, coords, turned = lax.optimization_barrier(ready)
    right, left = along_z(right, 1), along_z(left, -1)
    slot_count = session_slot.shape[0]
    width = 2 * CHANS
    early_blocks = len(chunks) * Y
    early = pl.pallas_call(
        read_in_kernel,
        out_shape=jax.ShapeDtypeStruct((early_blocks, width, BLOCK), bf16),
        in_specs=[hbm] * (1 + len(chunks)),
        out_specs=whole(1)[0],
        scratch_shapes=[
            pltpu.VMEM((early_blocks,) + chunk.shape[1:], bf16),
            pltpu.VMEM((slot_count // 2, in_chans, 2 * width), bf16),
            pltpu.SemaphoreType.DMA((slot_count,)),
            pltpu.SemaphoreType.DMA((len(chunks),)),
        ],
        compiler_params=params,
        cost_estimate=pl.CostEstimate(flops=work, bytes_accessed=4 << 20, transcendentals=0),
        name="read_in",
    )(in_weights, *chunks)
    right, left, early = lax.optimization_barrier((right, left, early))
    late = [right, left, along_z(right, 1)]
    late[2], turned = lax.optimization_barrier((late[2], turned))
    grads = lax.all_to_all(turned, "seq", split_axis=0, concat_axis=0, tiled=True)

    tables = (first, second, back_second, back_first)
    gated, gates, spectrum = pl.pallas_call(
        forward_kernel,
        out_shape=(
            jax.ShapeDtypeStruct(plane, bf16),
            jax.ShapeDtypeStruct(plane, bf16),
            spectrum_shape,
        ),
        in_specs=[scalar] + whole(3) + [hbm] * (3 + len(late) + 4),
        out_specs=tuple(whole(3)),
        scratch_shapes=[
            pltpu.VMEM((BLOCKS, 2 * CHANS, BLOCK), bf16),
            pltpu.VMEM((len(late) * Y,) + chunk.shape[1:], bf16),
            pltpu.VMEM((slot_count // 2, in_chans, 4 * CHANS), bf16),
            pltpu.VMEM(spectrum_shape.shape, bf16),
        ]
        + [pltpu.VMEM(table.shape, bf16) for table in tables]
        + [pltpu.SemaphoreType.DMA((count,)) for count in (slot_count, len(late), early_blocks, 5)],
        compiler_params=params,
        cost_estimate=pl.CostEstimate(flops=4 * work, bytes_accessed=8 << 20, transcendentals=0),
        name="long_convolution",
    )(coords, taps, gains, twists, filter_spectrum, in_weights, early, *late, *tables)

    gated = gated.reshape(Z, Y, CHANS, BLOCK)
    arrived = lax.all_to_all(gated, "seq", split_axis=0, concat_axis=0, tiled=True, axis_index_groups=z_groups)
    own_grad = pl.pallas_call(
        gradient_kernel,
        out_shape=jax.ShapeDtypeStruct((CHANS, LENGTH), bf16),
        grid=(GROUPS // 4,),
        in_specs=[pl.BlockSpec((BLOCKS, 2 * pair, BLOCK), lambda i: (0, i, 0))] * 2
        + [pl.BlockSpec((4,) + spectrum_shape.shape[1:], lambda i: (i, 0, 0))]
        + [same(table) for table in tables + (twists,)],
        out_specs=pl.BlockSpec((2 * pair, LENGTH), lambda i: (i, 0)),
        compiler_params=params,
        cost_estimate=pl.CostEstimate(flops=2 * work, bytes_accessed=4 << 20, transcendentals=0),
        name="filter_gradient",
    )(grads, gates, spectrum, *tables, twists)
    all_grads = lax.all_gather(own_grad, "grp", axis=0, tiled=False)
    devices = all_grads.shape[0]
    picks = jnp.asarray(np.tile(np.eye(pair, dtype=np.float32), (1, devices)), bf16)
    filter_grad = pl.pallas_call(
        sum_kernel,
        out_shape=jax.ShapeDtypeStruct((CHANS, LENGTH), f32),
        grid=(CHANS // pair,),
        in_specs=[pl.BlockSpec((devices, pair, LENGTH), lambda i: (0, i, 0)), same(picks)],
        out_specs=pl.BlockSpec((pair, LENGTH), lambda i: (i, 0)),
        compiler_params=params,
        cost_estimate=pl.CostEstimate(flops=all_grads.size, bytes_accessed=5 << 20, transcendentals=0),
        name="sum_gradients",
    )(all_grads, picks)
    partial = pl.pallas_call(
        read_out_kernel,
        out_shape=jax.ShapeDtypeStruct((Y, BLOCK, in_chans), bf16),
        in_specs=[scalar] + [hbm] * 3,
        out_specs=whole(1)[0],
        scratch_shapes=[
            pltpu.VMEM(out_weights.shape, bf16),
            pltpu.VMEM((Z, Y, CHANS, BLOCK), bf16),
            pltpu.VMEM((Y, BLOCK // TRIAL, in_chans), bf16),
        ]
        + [pltpu.SemaphoreType.DMA((count,)) for count in (slot_count, 2)],
        compiler_params=params,
        cost_estimate=pl.CostEstimate(flops=2 * 512 * 512 * 4096, bytes_accessed=6 << 20, transcendentals=0),
        name="read_out",
    )(coords, arrived, own_marks, out_weights)
    pieces = lax.all_to_all(partial, "seq", split_axis=0, concat_axis=0, tiled=True, axis_index_groups=y_groups)
    denoised = jnp.sum(pieces.astype(f32), 0).astype(bf16)
    return denoised[None], filter_grad


def solution(mesh):
    placed = (
        P("grp", "seq", None),
        P("grp", "seq"),
        P(),
        P("grp", None, None),
        P(),
        P("seq", None),
        P("seq"),
        P("grp", None, None),
        P("grp", "seq", None),
    )
    return jax.shard_map(
        local,
        mesh=mesh,
        in_specs=placed,
        out_specs=(P("grp", "seq", None), P("seq", None)),
        check_vma=False,
    )
```

```python
import jax
import jax.numpy as jnp
import numpy as np
from jax import lax
from jax.experimental import pallas as pl
from jax.experimental.pallas import tpu as pltpu
from jax.sharding import PartitionSpec as P

BLOCK = 128
TRIAL = 16
Z = 8
Y = 4
BLOCKS = Z * Y
CHANS = 64
LANE8 = 8
GROUPS = CHANS // LANE8
LENGTH = BLOCKS * BLOCK
f32 = jnp.float32
bf16 = jnp.bfloat16


def transform_tables():
    slow = np.arange(BLOCKS)
    fast = np.arange(BLOCK)
    first = np.exp(-2j * np.pi * (np.outer(slow, slow) / BLOCKS + slow[None, :] / (4.0 * BLOCKS)))
    twist = np.exp(-2j * np.pi * (slow[:, None] + 0.25) * fast[None, :] / LENGTH)
    second = np.exp(-2j * np.pi * np.outer(fast, fast) / BLOCK)
    eye = np.eye(LANE8)
    spread_first = np.concatenate([np.kron(first.real, eye), np.kron(first.imag, eye)], 0)
    forward_second = np.block([[second.real, second.imag], [-second.imag, second.real]])
    back = second.conj()
    back_second = np.block([[back.real, back.imag], [-back.imag, back.real]])
    back_first = first.conj().T / LENGTH
    spread_back = np.concatenate([np.kron(back_first.real, eye), np.kron(-back_first.imag, eye)], 1)
    as_bf16 = lambda table: jnp.asarray(table.astype(np.float32), bf16)
    twists = np.stack([twist.real, twist.imag]).astype(np.float32)
    return (
        as_bf16(spread_first),
        as_bf16(forward_second),
        as_bf16(back_second),
        as_bf16(spread_back),
        jnp.asarray(twists),
    )


def twists_of(twist_ref):
    shape = (BLOCKS, LANE8, BLOCK)
    cosine = jnp.broadcast_to(twist_ref[0][:, None, :], shape).reshape(BLOCKS * LANE8, BLOCK)
    sine = jnp.broadcast_to(twist_ref[1][:, None, :], shape).reshape(BLOCKS * LANE8, BLOCK)
    return cosine, sine


def forward(low, high, first_ref, second_ref, cosine, sine):
    rows = BLOCKS * LANE8
    signals = jnp.concatenate([low, high], 1).astype(bf16)
    part = jnp.dot(first_ref[...], signals, preferred_element_type=f32)
    turned = []
    for lanes in (slice(0, BLOCK), slice(BLOCK, 2 * BLOCK)):
        real, imag = part[:rows, lanes], part[rows:, lanes]
        turned.append(jnp.concatenate([real * cosine - imag * sine, real * sine + imag * cosine], 1))
    return jnp.dot(jnp.concatenate(turned, 0).astype(bf16), second_ref[...], preferred_element_type=f32)


def backward(spectra, back_second_ref, back_first_ref, cosine, sine):
    rows = BLOCKS * LANE8
    part = jnp.dot(spectra.astype(bf16), back_second_ref[...], preferred_element_type=f32)
    turned = []
    for start in (0, rows):
        real, imag = part[start : start + rows, :BLOCK], part[start : start + rows, BLOCK:]
        turned.append(jnp.concatenate([real * cosine + imag * sine, imag * cosine - real * sine], 0))
    return jnp.dot(back_first_ref[...], jnp.concatenate(turned, 1).astype(bf16), preferred_element_type=f32)


def filter_kernel(filter_ref, first_ref, second_ref, twist_ref, spectrum_ref):
    cosine, sine = twists_of(twist_ref)
    rows = BLOCKS * LANE8
    signals = []
    for start in (0, LANE8):
        pieces = [filter_ref[start : start + LANE8, i * BLOCK : (i + 1) * BLOCK] for i in range(BLOCKS)]
        signals.append(jnp.concatenate(pieces, 0))
    spectra = forward(*signals, first_ref, second_ref, cosine, sine)
    spectrum_ref[...] = spectra.astype(bf16).reshape(2, rows, 2 * BLOCK)


def start_all(copies):
    for copy in copies:
        copy.start()


def wait_all(copies):
    for copy in copies:
        copy.wait()


def weight_copies(weight_hbm, weight, sems):
    copies = []
    for slot in range(weight_hbm.shape[0]):
        lanes = pl.ds(slot % 2 * 2 * CHANS, 2 * CHANS)
        copies.append(pltpu.make_async_copy(weight_hbm.at[slot], weight.at[slot // 2, :, lanes], sems.at[slot]))
    return copies


def spread(rows, marks, count):
    trials, width = marks.shape
    marks = jnp.broadcast_to(marks[:, None, :], (trials, TRIAL, width)).reshape(trials * TRIAL, width).astype(bf16)
    nothing = jnp.zeros_like(rows)
    return jnp.concatenate([jnp.where(marks == number, rows, nothing) for number in range(count)], 1)


def project(rows_ref, start, blocks, weight):
    width = 2 * CHANS
    in_chans = rows_ref.shape[2]
    rows = rows_ref[pl.ds(start, blocks), :BLOCK, :].reshape(blocks * BLOCK, in_chans)
    marks = rows_ref[pl.ds(start, blocks), BLOCK:, :].astype(f32).reshape(blocks * BLOCK // TRIAL, in_chans)
    wide = spread(rows, jnp.floor(marks * 0.5), weight.shape[0])
    product = jnp.dot(wide, weight[...].reshape(-1, 2 * width), preferred_element_type=f32)
    odd = (marks - 2 * jnp.floor(marks * 0.5))[:, :width]
    trials = odd.shape[0]
    odd = jnp.broadcast_to(odd[:, None, :], (trials, TRIAL, width)).reshape(trials * TRIAL, width)
    chosen = jnp.where(odd > 0.5, product[:, width:], product[:, :width])
    return [chosen[i * BLOCK : (i + 1) * BLOCK].T.astype(bf16) for i in range(blocks)]


def block_of(place_ref, z_step, y_index):
    y_step = jnp.where(y_index < 2, Y - y_index, y_index - 1)
    return lax.rem(place_ref[0] + z_step, Z) * Y + lax.rem(place_ref[1] + y_step, Y)


def z_step_of(index):
    return jnp.where(index % 2 == 1, Z - (index + 1) // 2, index // 2)


def read_in_kernel(weight_hbm, *rest):
    chunk_hbms = rest[:-5]
    out_ref, rows, weight, weight_sems, sems = rest[-5:]
    loads = weight_copies(weight_hbm, weight, weight_sems)
    for index, chunk in enumerate(chunk_hbms):
        loads.append(pltpu.make_async_copy(chunk, rows.at[pl.ds(index * Y, Y)], sems.at[index]))
    start_all(loads)
    wait_all(loads)

    def step(index, carry):
        blocks = project(rows, index * Y, Y, weight)
        for y_index in range(Y):
            out_ref[index * Y + y_index] = blocks[y_index]
        return carry

    lax.fori_loop(0, len(chunk_hbms), step, 0)


def forward_kernel(place_ref, taps_ref, gain_ref, twist_ref, filter_hbm, weight_hbm, early_hbm, *rest):
    late = Z - early_hbm.shape[0] // Y
    chunk_hbms = rest[:late]
    table_hbms = rest[late : late + 4]
    gated_ref, gate_ref, spectrum_ref, both, rows, weight, spectra, *rest = rest[late + 4 :]
    tables = rest[:4]
    weight_sems, row_sems, early_sems, sems = rest[4:]
    loads = weight_copies(weight_hbm, weight, weight_sems)
    for index, chunk in enumerate(chunk_hbms):
        loads.append(pltpu.make_async_copy(chunk, rows.at[pl.ds(index * Y, Y)], row_sems.at[index]))
    others = []
    for index in range(early_hbm.shape[0]):
        target = both.at[block_of(place_ref, z_step_of(index // Y), index % Y)]
        others.append(pltpu.make_async_copy(early_hbm.at[index], target, early_sems.at[index]))
    pairs = [(filter_hbm, spectra)] + list(zip(table_hbms, tables))
    others += [pltpu.make_async_copy(source, target, sems.at[index]) for index, (source, target) in enumerate(pairs)]
    start_all(loads)
    start_all(others)
    wait_all(loads)

    def read_in(index, carry):
        blocks = project(rows, index * Y, Y, weight)
        for y_index in range(Y):
            both[block_of(place_ref, z_step_of(index + Z - late), y_index)] = blocks[y_index]
        return carry

    lax.fori_loop(0, late, read_in, 0)
    cosine, sine = twists_of(twist_ref)
    lane = lax.broadcasted_iota(jnp.int32, (BLOCKS, LANE8, BLOCK), 2)
    count = BLOCKS * LANE8
    cube = (BLOCKS, LANE8, BLOCK)
    wait_all(others)
    first_ref, second_ref, back_second_ref, back_first_ref = tables

    def short(value, group):
        taps = taps_ref[:, pl.ds(pl.multiple_of(group * LANE8, LANE8), LANE8), :]
        total = taps[0][None] * value
        for shift in (1, 2):
            rolled = pltpu.roll(value.reshape(count, BLOCK), shift, 1).reshape(cube)
            before = jnp.concatenate([jnp.zeros((1, LANE8, BLOCK), f32), rolled[:-1]], 0)
            total = total + taps[shift][None] * jnp.where(lane < shift, before, rolled)
        return total.astype(bf16).astype(f32).reshape(count, BLOCK)

    def step(pair, carry):
        here = pl.ds(pl.multiple_of(pair * 2 * LANE8, 2 * LANE8), 2 * LANE8)
        there = pl.ds(pl.multiple_of(CHANS + pair * 2 * LANE8, 2 * LANE8), 2 * LANE8)
        value = both[:, here, :].astype(f32)
        gate = both[:, there, :]
        signals = [short(value[:, i * LANE8 : (i + 1) * LANE8], pair * 2 + i) for i in range(2)]
        own = forward(*signals, first_ref, second_ref, cosine, sine)
        spectrum_ref[pl.ds(pair * 2, 2)] = own.reshape(2, count, 2 * BLOCK).astype(bf16)
        weight = spectra[pl.ds(pair * 2, 2)].reshape(2 * count, 2 * BLOCK).astype(f32)
        own_re, own_im = own[:, :BLOCK], own[:, BLOCK:]
        filter_re, filter_im = weight[:, :BLOCK], weight[:, BLOCK:]
        mix = jnp.concatenate([own_re * filter_re - own_im * filter_im, own_re * filter_im + own_im * filter_re], 1)
        result = backward(mix, back_second_ref, back_first_ref, cosine, sine)
        signal = jnp.concatenate([piece.reshape(cube) for piece in signals], 1)
        long_part = jnp.concatenate([result[:, i * BLOCK : (i + 1) * BLOCK].reshape(cube) for i in range(2)], 1)
        mixed = (long_part + gain_ref[here, :][None] * signal).astype(bf16).astype(f32)
        gated_ref[:, here, :] = (gate.astype(f32) * mixed).astype(bf16)
        gate_ref[:, here, :] = gate
        return carry

    lax.fori_loop(0, GROUPS // 2, step, 0, unroll=2)


def gradient_kernel(grad_ref, gate_ref, spectrum_ref, first_ref, second_ref, back_second_ref, back_first_ref, twist_ref, out_ref):
    cosine, sine = twists_of(twist_ref)
    count = BLOCKS * LANE8
    pair = 2 * LANE8
    for start in range(0, grad_ref.shape[1], pair):
        here = slice(start, start + pair)
        products = (grad_ref[:, here, :].astype(f32) * gate_ref[:, here, :].astype(f32)).astype(bf16).astype(f32)
        signals = [products[:, i * LANE8 : (i + 1) * LANE8].reshape(count, BLOCK) for i in range(2)]
        spectra = forward(*signals, first_ref, second_ref, cosine, sine)
        own = spectrum_ref[start // LANE8 : start // LANE8 + 2].reshape(2 * count, 2 * BLOCK).astype(f32)
        own_re, own_im = own[:, :BLOCK], own[:, BLOCK:]
        grad_re, grad_im = spectra[:, :BLOCK], spectra[:, BLOCK:]
        lag = jnp.concatenate([own_re * grad_re + own_im * grad_im, own_re * grad_im - own_im * grad_re], 1)
        result = backward(lag, back_second_ref, back_first_ref, cosine, sine)
        both = []
        for half in range(2):
            lanes = slice(half * BLOCK, (half + 1) * BLOCK)
            both.append(jnp.concatenate([result[i * LANE8 : (i + 1) * LANE8, lanes] for i in range(BLOCKS)], 1))
        out_ref[here, :] = jnp.concatenate(both, 0).astype(bf16)


def read_out_kernel(place_ref, rows_hbm, marks_hbm, weight_hbm, out_ref, weight, rows_all, chunk_all, weight_sems, sems):
    slots, inner, width = weight.shape
    trials = BLOCK // TRIAL
    first = [pltpu.make_async_copy(rows_hbm, rows_all, sems.at[0]), pltpu.make_async_copy(marks_hbm, chunk_all, sems.at[1])]
    loads = [pltpu.make_async_copy(weight_hbm.at[slot], weight.at[slot], weight_sems.at[slot]) for slot in range(slots)]
    start_all(first)
    start_all(loads)
    wait_all(first)
    places = [block_of(place_ref, 0, index) - place_ref[0] * Y for index in range(Y)]
    rows = jnp.concatenate([rows_all[:, block, :, :].reshape(inner, BLOCK).T for block in places], 0)
    marks = chunk_all[...].astype(f32).reshape(Y * trials, width)
    marks = jnp.broadcast_to(marks[:, None, :], (Y * trials, TRIAL, width)).reshape(Y * BLOCK, width)
    wait_all(loads)
    total = jnp.zeros((Y * BLOCK, width), f32)
    for slot in range(slots):
        product = jnp.dot(rows, weight[slot], preferred_element_type=f32)
        total = jnp.where(marks == slot, product, total)
    for index, block in enumerate(places):
        out_ref[block] = total[index * BLOCK : (index + 1) * BLOCK].astype(bf16)


def sum_kernel(parts_hbm, out_hbm, parts, total, in_sems, out_sems):
    count, rows, _ = parts.shape
    step = 2 * LANE8
    loads = []
    stores = []
    for index in range(rows // step):
        here = pl.ds(index * step, step)
        for part in range(count):
            load = pltpu.make_async_copy(parts_hbm.at[part, here, :], parts.at[part, here, :], in_sems.at[index, part])
            loads.append(load)
        stores.append(pltpu.make_async_copy(total.at[here, :], out_hbm.at[here, :], out_sems.at[index]))
    start_all(loads)
    for index in range(rows // step):
        wait_all(loads[index * count : (index + 1) * count])
        here = slice(index * step, (index + 1) * step)
        running = parts[0, here, :].astype(f32)
        for part in range(1, count):
            running = running + parts[part, here, :].astype(f32)
        total[here, :] = running
        stores[index].start()
    wait_all(stores)


def prepare_kernel(place_ref, session_ref, slot_ref, spikes_ref, weight_hbm, block_ref, own_ref, value, gate, sems):
    place = place_ref[0]
    half = weight_hbm.shape[2] // 2
    window = pl.multiple_of(place // 2 * 2 * CHANS, 2 * CHANS)
    loads = [
        pltpu.make_async_copy(weight_hbm.at[:, :, pl.ds(window, 2 * CHANS)], value, sems.at[0]),
        pltpu.make_async_copy(weight_hbm.at[:, :, pl.ds(half + window, 2 * CHANS)], gate, sems.at[1]),
    ]
    start_all(loads)
    trials = BLOCK // TRIAL
    width = block_ref.shape[1]
    row = lax.broadcasted_iota(jnp.int32, (trials, width), 0)
    marks = jnp.zeros((trials, width), jnp.int32)
    for trial in range(trials):
        marks = jnp.where(row == trial, slot_ref[session_ref[0, trial * TRIAL]], marks)
    block_ref[:BLOCK, :] = spikes_ref[0]
    block_ref[BLOCK:, :] = marks.astype(f32).astype(bf16)
    wait_all(loads)
    slots, inner, lanes = own_ref.shape
    odd = place % 2
    low = pltpu.roll(value[...].astype(f32).reshape(slots * inner, lanes), odd * CHANS, 1)
    high = pltpu.roll(gate[...].astype(f32).reshape(slots * inner, lanes), (1 - odd) * CHANS, 1)
    lane = lax.broadcasted_iota(jnp.int32, (slots * inner, lanes), 1)
    own_ref[...] = jnp.where(lane < CHANS, low, high).astype(bf16).reshape(slots, inner, lanes)


def along_y(value, step):
    return lax.ppermute(value, "seq", [(z * Y + y, z * Y + (y + step) % Y) for z in range(Z) for y in range(Y)])


def along_z(value, step):
    return lax.ppermute(value, "seq", [(z * Y + y, (z + step) % Z * Y + y) for z in range(Z) for y in range(Y)])


def whole(count):
    return [pl.BlockSpec(memory_space=pltpu.VMEM)] * count


def local(spikes, session_of_bin, session_slot, readin_weight, short_kernel, long_filter, skip_gain, readout_weight, out_grad):
    in_chans = spikes.shape[2]
    place = lax.axis_index("seq")
    scalar = pl.BlockSpec(memory_space=pltpu.SMEM)
    hbm = pl.BlockSpec(memory_space=pltpu.HBM)
    z_groups = [[z * Y + y for z in range(Z)] for y in range(Y)]
    y_groups = [[z * Y + y for y in range(Y)] for z in range(Z)]
    coords = jnp.stack([place // Y, place % Y]).astype(jnp.int32)
    first, second, back_second, back_first, twists = transform_tables()
    params = pltpu.CompilerParams(vmem_limit_bytes=60 << 20)
    spectrum_shape = jax.ShapeDtypeStruct((GROUPS, BLOCKS * LANE8, 2 * BLOCK), bf16)
    plane = (BLOCKS, CHANS, BLOCK)
    work = 2 * GROUPS * (512 * 256 * 128 + 256 * 256 * 256)
    pair = 2 * LANE8
    same = lambda table: pl.BlockSpec(table.shape, lambda i, rank=table.ndim: (0,) * rank)

    own_shape = (2, in_chans, 2 * CHANS)
    block, own_weights = pl.pallas_call(
        prepare_kernel,
        out_shape=(jax.ShapeDtypeStruct((BLOCK + BLOCK // TRIAL, in_chans), bf16), jax.ShapeDtypeStruct(own_shape, bf16)),
        in_specs=[scalar] * 3 + whole(1) + [hbm],
        out_specs=tuple(whole(2)),
        scratch_shapes=[pltpu.VMEM(own_shape, bf16), pltpu.VMEM(own_shape, bf16), pltpu.SemaphoreType.DMA((2,))],
        compiler_params=params,
        cost_estimate=pl.CostEstimate(flops=1 << 16, bytes_accessed=1 << 19, transcendentals=0),
        name="prepare",
    )(place.astype(jnp.int32)[None], session_of_bin, session_slot, spikes, readin_weight)
    chunk = jnp.stack([block, along_y(block, 1), along_y(block, -1), along_y(block, 2)])
    chunk, readout_weight = lax.optimization_barrier((chunk, readout_weight))
    own_marks = chunk[:, BLOCK:, :]
    right, left = along_z(chunk, 1), along_z(chunk, -1)
    chunks = [chunk, right, left]

    in_weights = lax.all_gather(own_weights, "grp", axis=0, tiled=True)
    split = readout_weight.reshape(2, Z, Y, CHANS, in_chans)
    split = lax.dynamic_index_in_dim(split, place % Y, 2, keepdims=False).reshape(2, Z * CHANS, in_chans)
    out_weights = lax.all_gather(split, "grp", axis=0, tiled=True)

    filter_spectrum = pl.pallas_call(
        filter_kernel,
        out_shape=spectrum_shape,
        grid=(GROUPS // 2,),
        in_specs=[pl.BlockSpec((pair, LENGTH), lambda i: (i, 0))] + [same(table) for table in (first, second, twists)],
        out_specs=pl.BlockSpec((2,) + spectrum_shape.shape[1:], lambda i: (i, 0, 0)),
        compiler_params=params,
        cost_estimate=pl.CostEstimate(flops=work, bytes_accessed=4 << 20, transcendentals=0),
        name="filter_transform",
    )(long_filter, first, second, twists)

    right, left, filter_spectrum, own_marks = lax.optimization_barrier((right, left, filter_spectrum, own_marks))
    right, left = along_z(right, 1), along_z(left, -1)
    chunks += [right, left]
    turned = out_grad[0].T.reshape(BLOCKS, CHANS, BLOCK)
    taps = lax.dynamic_slice_in_dim(short_kernel, place * CHANS, CHANS, 1)
    taps = jnp.broadcast_to(taps[:, :, None], (short_kernel.shape[0], CHANS, BLOCK))
    gains = jnp.broadcast_to(skip_gain[:, None], (CHANS, BLOCK))
    ready = (right, left, taps, gains, coords, turned)
    right, left, taps, gains, coords, turned = lax.optimization_barrier(ready)
    right, left = along_z(right, 1), along_z(left, -1)
    slot_count = session_slot.shape[0]
    width = 2 * CHANS
    early_blocks = len(chunks) * Y
    early = pl.pallas_call(
        read_in_kernel,
        out_shape=jax.ShapeDtypeStruct((early_blocks, width, BLOCK), bf16),
        in_specs=[hbm] * (1 + len(chunks)),
        out_specs=whole(1)[0],
        scratch_shapes=[
            pltpu.VMEM((early_blocks,) + chunk.shape[1:], bf16),
            pltpu.VMEM((slot_count // 2, in_chans, 2 * width), bf16),
            pltpu.SemaphoreType.DMA((slot_count,)),
            pltpu.SemaphoreType.DMA((len(chunks),)),
        ],
        compiler_params=params,
        cost_estimate=pl.CostEstimate(flops=work, bytes_accessed=4 << 20, transcendentals=0),
        name="read_in",
    )(in_weights, *chunks)
    right, left, early = lax.optimization_barrier((right, left, early))
    late = [right, left, along_z(right, 1)]
    late[2], turned = lax.optimization_barrier((late[2], turned))
    grads = lax.all_to_all(turned, "seq", split_axis=0, concat_axis=0, tiled=True)

    tables = (first, second, back_second, back_first)
    gated, gates, spectrum = pl.pallas_call(
        forward_kernel,
        out_shape=(
            jax.ShapeDtypeStruct(plane, bf16),
            jax.ShapeDtypeStruct(plane, bf16),
            spectrum_shape,
        ),
        in_specs=[scalar] + whole(3) + [hbm] * (3 + len(late) + 4),
        out_specs=tuple(whole(3)),
        scratch_shapes=[
            pltpu.VMEM((BLOCKS, 2 * CHANS, BLOCK), bf16),
            pltpu.VMEM((len(late) * Y,) + chunk.shape[1:], bf16),
            pltpu.VMEM((slot_count // 2, in_chans, 4 * CHANS), bf16),
            pltpu.VMEM(spectrum_shape.shape, bf16),
        ]
        + [pltpu.VMEM(table.shape, bf16) for table in tables]
        + [pltpu.SemaphoreType.DMA((count,)) for count in (slot_count, len(late), early_blocks, 5)],
        compiler_params=params,
        cost_estimate=pl.CostEstimate(flops=4 * work, bytes_accessed=8 << 20, transcendentals=0),
        name="long_convolution",
    )(coords, taps, gains, twists, filter_spectrum, in_weights, early, *late, *tables)

    gated = gated.reshape(Z, Y, CHANS, BLOCK)
    arrived = lax.all_to_all(gated, "seq", split_axis=0, concat_axis=0, tiled=True, axis_index_groups=z_groups)
    own_grad = pl.pallas_call(
        gradient_kernel,
        out_shape=jax.ShapeDtypeStruct((CHANS, LENGTH), bf16),
        grid=(GROUPS // 4,),
        in_specs=[pl.BlockSpec((BLOCKS, 2 * pair, BLOCK), lambda i: (0, i, 0))] * 2
        + [pl.BlockSpec((4,) + spectrum_shape.shape[1:], lambda i: (i, 0, 0))]
        + [same(table) for table in tables + (twists,)],
        out_specs=pl.BlockSpec((2 * pair, LENGTH), lambda i: (i, 0)),
        compiler_params=params,
        cost_estimate=pl.CostEstimate(flops=2 * work, bytes_accessed=4 << 20, transcendentals=0),
        name="filter_gradient",
    )(grads, gates, spectrum, *tables, twists)
    all_grads = lax.all_gather(own_grad, "grp", axis=0, tiled=False)
    devices = all_grads.shape[0]
    filter_grad = pl.pallas_call(
        sum_kernel,
        out_shape=jax.ShapeDtypeStruct((CHANS, LENGTH), f32),
        in_specs=[hbm],
        out_specs=hbm,
        scratch_shapes=[
            pltpu.VMEM(all_grads.shape, bf16),
            pltpu.VMEM((CHANS, LENGTH), f32),
            pltpu.SemaphoreType.DMA((CHANS // pair, devices)),
            pltpu.SemaphoreType.DMA((CHANS // pair,)),
        ],
        compiler_params=params,
        cost_estimate=pl.CostEstimate(flops=all_grads.size, bytes_accessed=5 << 20, transcendentals=0),
        name="sum_gradients",
    )(all_grads)
    partial = pl.pallas_call(
        read_out_kernel,
        out_shape=jax.ShapeDtypeStruct((Y, BLOCK, in_chans), bf16),
        in_specs=[scalar] + [hbm] * 3,
        out_specs=whole(1)[0],
        scratch_shapes=[
            pltpu.VMEM(out_weights.shape, bf16),
            pltpu.VMEM((Z, Y, CHANS, BLOCK), bf16),
            pltpu.VMEM((Y, BLOCK // TRIAL, in_chans), bf16),
        ]
        + [pltpu.SemaphoreType.DMA((count,)) for count in (slot_count, 2)],
        compiler_params=params,
        cost_estimate=pl.CostEstimate(flops=2 * 512 * 512 * 4096, bytes_accessed=6 << 20, transcendentals=0),
        name="read_out",
    )(coords, arrived, own_marks, out_weights)
    pieces = lax.all_to_all(partial, "seq", split_axis=0, concat_axis=0, tiled=True, axis_index_groups=y_groups)
    denoised = jnp.sum(pieces.astype(f32), 0).astype(bf16)
    return denoised[None], filter_grad


def solution(mesh):
    placed = (
        P("grp", "seq", None),
        P("grp", "seq"),
        P(),
        P("grp", None, None),
        P(),
        P("seq", None),
        P("seq"),
        P("grp", None, None),
        P("grp", "seq", None),
    )
    return jax.shard_map(
        local,
        mesh=mesh,
        in_specs=placed,
        out_specs=(P("grp", "seq", None), P("seq", None)),
        check_vma=False,
    )
```

```python
import jax
import jax.numpy as jnp
import numpy as np
from jax import lax
from jax.experimental import pallas as pl
from jax.experimental.pallas import tpu as pltpu
from jax.sharding import PartitionSpec as P

BLOCK = 128
TRIAL = 16
Z = 8
Y = 4
BLOCKS = Z * Y
CHANS = 64
LANE8 = 8
GROUPS = CHANS // LANE8
LENGTH = BLOCKS * BLOCK
f32 = jnp.float32
bf16 = jnp.bfloat16


def transform_tables():
    slow = np.arange(BLOCKS)
    fast = np.arange(BLOCK)
    first = np.exp(-2j * np.pi * (np.outer(slow, slow) / BLOCKS + slow[None, :] / (4.0 * BLOCKS)))
    twist = np.exp(-2j * np.pi * (slow[:, None] + 0.25) * fast[None, :] / LENGTH)
    second = np.exp(-2j * np.pi * np.outer(fast, fast) / BLOCK)
    eye = np.eye(LANE8)
    spread_first = np.concatenate([np.kron(first.real, eye), np.kron(first.imag, eye)], 0)
    forward_second = np.block([[second.real, second.imag], [-second.imag, second.real]])
    back = second.conj()
    back_second = np.block([[back.real, back.imag], [-back.imag, back.real]])
    back_first = first.conj().T / LENGTH
    spread_back = np.concatenate([np.kron(back_first.real, eye), np.kron(-back_first.imag, eye)], 1)
    as_bf16 = lambda table: jnp.asarray(table.astype(np.float32), bf16)
    twists = np.stack([twist.real, twist.imag]).astype(np.float32)
    return (
        as_bf16(spread_first),
        as_bf16(forward_second),
        as_bf16(back_second),
        as_bf16(spread_back),
        jnp.asarray(twists),
    )


def twists_of(twist_ref):
    shape = (BLOCKS, LANE8, BLOCK)
    cosine = jnp.broadcast_to(twist_ref[0][:, None, :], shape).reshape(BLOCKS * LANE8, BLOCK)
    sine = jnp.broadcast_to(twist_ref[1][:, None, :], shape).reshape(BLOCKS * LANE8, BLOCK)
    return cosine, sine


def forward(low, high, first_ref, second_ref, cosine, sine):
    rows = BLOCKS * LANE8
    signals = jnp.concatenate([low, high], 1).astype(bf16)
    part = jnp.dot(first_ref[...], signals, preferred_element_type=f32)
    turned = []
    for lanes in (slice(0, BLOCK), slice(BLOCK, 2 * BLOCK)):
        real, imag = part[:rows, lanes], part[rows:, lanes]
        turned.append(jnp.concatenate([real * cosine - imag * sine, real * sine + imag * cosine], 1))
    return jnp.dot(jnp.concatenate(turned, 0).astype(bf16), second_ref[...], preferred_element_type=f32)


def backward(spectra, back_second_ref, back_first_ref, cosine, sine):
    rows = BLOCKS * LANE8
    part = jnp.dot(spectra.astype(bf16), back_second_ref[...], preferred_element_type=f32)
    turned = []
    for start in (0, rows):
        real, imag = part[start : start + rows, :BLOCK], part[start : start + rows, BLOCK:]
        turned.append(jnp.concatenate([real * cosine + imag * sine, imag * cosine - real * sine], 0))
    return jnp.dot(back_first_ref[...], jnp.concatenate(turned, 1).astype(bf16), preferred_element_type=f32)


def filter_kernel(filter_ref, first_ref, second_ref, twist_ref, spectrum_ref):
    cosine, sine = twists_of(twist_ref)
    rows = BLOCKS * LANE8
    signals = []
    for start in (0, LANE8):
        pieces = [filter_ref[start : start + LANE8, i * BLOCK : (i + 1) * BLOCK] for i in range(BLOCKS)]
        signals.append(jnp.concatenate(pieces, 0))
    spectra = forward(*signals, first_ref, second_ref, cosine, sine)
    spectrum_ref[...] = spectra.astype(bf16).reshape(2, rows, 2 * BLOCK)


def start_all(copies):
    for copy in copies:
        copy.start()


def wait_all(copies):
    for copy in copies:
        copy.wait()


def weight_copies(weight_hbm, weight, sems):
    copies = []
    for slot in range(weight_hbm.shape[0]):
        lanes = pl.ds(slot % 2 * 2 * CHANS, 2 * CHANS)
        copies.append(pltpu.make_async_copy(weight_hbm.at[slot], weight.at[slot // 2, :, lanes], sems.at[slot]))
    return copies


def spread(rows, marks, count):
    trials, width = marks.shape
    marks = jnp.broadcast_to(marks[:, None, :], (trials, TRIAL, width)).reshape(trials * TRIAL, width).astype(bf16)
    nothing = jnp.zeros_like(rows)
    return jnp.concatenate([jnp.where(marks == number, rows, nothing) for number in range(count)], 1)


def project(rows_ref, start, blocks, weight):
    width = 2 * CHANS
    in_chans = rows_ref.shape[2]
    rows = rows_ref[pl.ds(start, blocks), :BLOCK, :].reshape(blocks * BLOCK, in_chans)
    marks = rows_ref[pl.ds(start, blocks), BLOCK:, :].astype(f32).reshape(blocks * BLOCK // TRIAL, in_chans)
    wide = spread(rows, jnp.floor(marks * 0.5), weight.shape[0])
    product = jnp.dot(wide, weight[...].reshape(-1, 2 * width), preferred_element_type=f32)
    odd = (marks - 2 * jnp.floor(marks * 0.5))[:, :width]
    trials = odd.shape[0]
    odd = jnp.broadcast_to(odd[:, None, :], (trials, TRIAL, width)).reshape(trials * TRIAL, width)
    chosen = jnp.where(odd > 0.5, product[:, width:], product[:, :width])
    return [chosen[i * BLOCK : (i + 1) * BLOCK].T.astype(bf16) for i in range(blocks)]


def block_of(place_ref, z_step, y_index):
    y_step = jnp.where(y_index < 2, Y - y_index, y_index - 1)
    return lax.rem(place_ref[0] + z_step, Z) * Y + lax.rem(place_ref[1] + y_step, Y)


def z_step_of(index):
    return jnp.where(index % 2 == 1, Z - (index + 1) // 2, index // 2)


def read_in_kernel(weight_hbm, *rest):
    chunk_hbms = rest[:-5]
    out_ref, rows, weight, weight_sems, sems = rest[-5:]
    loads = weight_copies(weight_hbm, weight, weight_sems)
    for index, chunk in enumerate(chunk_hbms):
        loads.append(pltpu.make_async_copy(chunk, rows.at[pl.ds(index * Y, Y)], sems.at[index]))
    start_all(loads)
    wait_all(loads)

    def step(index, carry):
        blocks = project(rows, index * Y, Y, weight)
        for y_index in range(Y):
            out_ref[index * Y + y_index] = blocks[y_index]
        return carry

    lax.fori_loop(0, len(chunk_hbms), step, 0)


def forward_kernel(place_ref, taps_ref, gain_ref, twist_ref, filter_hbm, weight_hbm, *rest):
    early_hbms, (chunk_hbm, *rest) = rest[:2], rest[2:]
    table_hbms, rest = rest[:4], rest[4:]
    gated_hbm, gate_hbm, spectrum_hbm, both, rows, weight, spectra, gated_all, spectrum_all, *rest = rest
    tables = rest[:4]
    weight_sems, early_sems, sems, store_sems = rest[4:]
    loads = weight_copies(weight_hbm, weight, weight_sems)
    others = []
    for early_hbm in early_hbms:
        for index in range(early_hbm.shape[0]):
            number = len(others)
            target = both.at[block_of(place_ref, z_step_of(number // Y), number % Y)]
            others.append(pltpu.make_async_copy(early_hbm.at[index], target, early_sems.at[number]))
    pairs = [(filter_hbm, spectra)] + list(zip(table_hbms, tables))
    others += [pltpu.make_async_copy(source, target, sems.at[index]) for index, (source, target) in enumerate(pairs)]
    loads.append(pltpu.make_async_copy(chunk_hbm, rows, sems.at[len(pairs)]))
    start_all(loads)
    start_all(others)
    wait_all(loads)
    last = project(rows, 0, Y, weight)
    for y_index in range(Y):
        both[block_of(place_ref, z_step_of(Z - 1), y_index)] = last[y_index]
    cosine, sine = twists_of(twist_ref)
    lane = lax.broadcasted_iota(jnp.int32, (BLOCKS, LANE8, BLOCK), 2)
    count = BLOCKS * LANE8
    cube = (BLOCKS, LANE8, BLOCK)
    wait_all(others)
    gate_store = pltpu.make_async_copy(both.at[:, pl.ds(CHANS, CHANS), :], gate_hbm, store_sems.at[0, GROUPS // 2])
    gate_store.start()
    first_ref, second_ref, back_second_ref, back_first_ref = tables

    def stores_of(pair):
        here = pl.ds(pl.multiple_of(pair * 2 * LANE8, 2 * LANE8), 2 * LANE8)
        groups = pl.ds(pair * 2, 2)
        return [
            pltpu.make_async_copy(gated_all.at[:, here, :], gated_hbm.at[:, here, :], store_sems.at[0, pair]),
            pltpu.make_async_copy(spectrum_all.at[groups], spectrum_hbm.at[groups], store_sems.at[1, pair]),
        ]

    def short(value, group):
        taps = taps_ref[:, pl.ds(pl.multiple_of(group * LANE8, LANE8), LANE8), :]
        total = taps[0][None] * value
        for shift in (1, 2):
            rolled = pltpu.roll(value.reshape(count, BLOCK), shift, 1).reshape(cube)
            before = jnp.concatenate([jnp.zeros((1, LANE8, BLOCK), f32), rolled[:-1]], 0)
            total = total + taps[shift][None] * jnp.where(lane < shift, before, rolled)
        return total.astype(bf16).astype(f32).reshape(count, BLOCK)

    def step(pair, carry):
        here = pl.ds(pl.multiple_of(pair * 2 * LANE8, 2 * LANE8), 2 * LANE8)
        there = pl.ds(pl.multiple_of(CHANS + pair * 2 * LANE8, 2 * LANE8), 2 * LANE8)
        value = both[:, here, :].astype(f32)
        gate = both[:, there, :]
        signals = [short(value[:, i * LANE8 : (i + 1) * LANE8], pair * 2 + i) for i in range(2)]
        own = forward(*signals, first_ref, second_ref, cosine, sine)
        spectrum_all[pl.ds(pair * 2, 2)] = own.reshape(2, count, 2 * BLOCK).astype(bf16)
        weight = spectra[pl.ds(pair * 2, 2)].reshape(2 * count, 2 * BLOCK).astype(f32)
        own_re, own_im = own[:, :BLOCK], own[:, BLOCK:]
        filter_re, filter_im = weight[:, :BLOCK], weight[:, BLOCK:]
        mix = jnp.concatenate([own_re * filter_re - own_im * filter_im, own_re * filter_im + own_im * filter_re], 1)
        result = backward(mix, back_second_ref, back_first_ref, cosine, sine)
        signal = jnp.concatenate([piece.reshape(cube) for piece in signals], 1)
        long_part = jnp.concatenate([result[:, i * BLOCK : (i + 1) * BLOCK].reshape(cube) for i in range(2)], 1)
        mixed = (long_part + gain_ref[here, :][None] * signal).astype(bf16).astype(f32)
        gated_all[:, here, :] = (gate.astype(f32) * mixed).astype(bf16)
        start_all(stores_of(pair))
        return carry

    lax.fori_loop(0, GROUPS // 2, step, 0, unroll=2)
    for pair in range(GROUPS // 2):
        wait_all(stores_of(pair))
    gate_store.wait()


def gradient_kernel(grad_ref, gate_ref, spectrum_ref, first_ref, second_ref, back_second_ref, back_first_ref, twist_ref, out_ref):
    cosine, sine = twists_of(twist_ref)
    count = BLOCKS * LANE8
    pair = 2 * LANE8
    for start in range(0, grad_ref.shape[1], pair):
        here = slice(start, start + pair)
        products = (grad_ref[:, here, :].astype(f32) * gate_ref[:, here, :].astype(f32)).astype(bf16).astype(f32)
        signals = [products[:, i * LANE8 : (i + 1) * LANE8].reshape(count, BLOCK) for i in range(2)]
        spectra = forward(*signals, first_ref, second_ref, cosine, sine)
        own = spectrum_ref[start // LANE8 : start // LANE8 + 2].reshape(2 * count, 2 * BLOCK).astype(f32)
        own_re, own_im = own[:, :BLOCK], own[:, BLOCK:]
        grad_re, grad_im = spectra[:, :BLOCK], spectra[:, BLOCK:]
        lag = jnp.concatenate([own_re * grad_re + own_im * grad_im, own_re * grad_im - own_im * grad_re], 1)
        result = backward(lag, back_second_ref, back_first_ref, cosine, sine)
        both = []
        for half in range(2):
            lanes = slice(half * BLOCK, (half + 1) * BLOCK)
            both.append(jnp.concatenate([result[i * LANE8 : (i + 1) * LANE8, lanes] for i in range(BLOCKS)], 1))
        out_ref[here, :] = jnp.concatenate(both, 0).astype(bf16)


def read_out_kernel(place_ref, rows_hbm, marks_hbm, weight_hbm, out_ref, weight, rows_all, chunk_all, weight_sems, sems):
    slots, inner, width = weight.shape
    trials = BLOCK // TRIAL
    first = [pltpu.make_async_copy(rows_hbm, rows_all, sems.at[0]), pltpu.make_async_copy(marks_hbm, chunk_all, sems.at[1])]
    loads = [pltpu.make_async_copy(weight_hbm.at[slot], weight.at[slot], weight_sems.at[slot]) for slot in range(slots)]
    start_all(first)
    start_all(loads)
    wait_all(first)
    places = [block_of(place_ref, 0, index) - place_ref[0] * Y for index in range(Y)]
    rows = jnp.concatenate([rows_all[:, block, :, :].reshape(inner, BLOCK).T for block in places], 0)
    marks = chunk_all[...].astype(f32).reshape(Y * trials, width)
    marks = jnp.broadcast_to(marks[:, None, :], (Y * trials, TRIAL, width)).reshape(Y * BLOCK, width)
    wait_all(loads)
    total = jnp.zeros((Y * BLOCK, width), f32)
    for slot in range(slots):
        product = jnp.dot(rows, weight[slot], preferred_element_type=f32)
        total = jnp.where(marks == slot, product, total)
    for index, block in enumerate(places):
        out_ref[block] = total[index * BLOCK : (index + 1) * BLOCK].astype(bf16)


def sum_kernel(parts_hbm, out_hbm, parts, total, in_sems, out_sems):
    count, rows, _ = parts.shape
    step = 2 * LANE8
    loads = []
    stores = []
    for index in range(rows // step):
        here = pl.ds(index * step, step)
        for part in range(count):
            load = pltpu.make_async_copy(parts_hbm.at[part, here, :], parts.at[part, here, :], in_sems.at[index, part])
            loads.append(load)
        stores.append(pltpu.make_async_copy(total.at[here, :], out_hbm.at[here, :], out_sems.at[index]))
    start_all(loads)
    for index in range(rows // step):
        wait_all(loads[index * count : (index + 1) * count])
        here = slice(index * step, (index + 1) * step)
        running = parts[0, here, :].astype(f32)
        for part in range(1, count):
            running = running + parts[part, here, :].astype(f32)
        total[here, :] = running
        stores[index].start()
    wait_all(stores)


def prepare_kernel(place_ref, session_ref, slot_ref, spikes_ref, weight_hbm, out_hbm, block_ref, own_ref, own_out_hbm, value, gate, sems):
    place = place_ref[0]
    half = weight_hbm.shape[2] // 2
    window = pl.multiple_of(place // 2 * 2 * CHANS, 2 * CHANS)
    loads = [
        pltpu.make_async_copy(weight_hbm.at[:, :, pl.ds(window, 2 * CHANS)], value, sems.at[0]),
        pltpu.make_async_copy(weight_hbm.at[:, :, pl.ds(half + window, 2 * CHANS)], gate, sems.at[1]),
    ]
    start_all(loads)
    moved = pltpu.make_async_copy(out_hbm.at[:, :, lax.rem(place, Y)], own_out_hbm, sems.at[2])
    moved.start()
    trials = BLOCK // TRIAL
    width = block_ref.shape[1]
    row = lax.broadcasted_iota(jnp.int32, (trials, width), 0)
    marks = jnp.zeros((trials, width), jnp.int32)
    for trial in range(trials):
        marks = jnp.where(row == trial, slot_ref[session_ref[0, trial * TRIAL]], marks)
    block_ref[:BLOCK, :] = spikes_ref[0]
    block_ref[BLOCK:, :] = marks.astype(f32).astype(bf16)
    wait_all(loads)
    slots, inner, lanes = own_ref.shape
    odd = place % 2
    low = pltpu.roll(value[...].astype(f32).reshape(slots * inner, lanes), odd * CHANS, 1)
    high = pltpu.roll(gate[...].astype(f32).reshape(slots * inner, lanes), (1 - odd) * CHANS, 1)
    lane = lax.broadcasted_iota(jnp.int32, (slots * inner, lanes), 1)
    own_ref[...] = jnp.where(lane < CHANS, low, high).astype(bf16).reshape(slots, inner, lanes)
    moved.wait()


def along_y(value, step):
    return lax.ppermute(value, "seq", [(z * Y + y, z * Y + (y + step) % Y) for z in range(Z) for y in range(Y)])


def along_z(value, step):
    return lax.ppermute(value, "seq", [(z * Y + y, (z + step) % Z * Y + y) for z in range(Z) for y in range(Y)])


def whole(count):
    return [pl.BlockSpec(memory_space=pltpu.VMEM)] * count


def local(spikes, session_of_bin, session_slot, readin_weight, short_kernel, long_filter, skip_gain, readout_weight, out_grad):
    in_chans = spikes.shape[2]
    place = lax.axis_index("seq")
    scalar = pl.BlockSpec(memory_space=pltpu.SMEM)
    hbm = pl.BlockSpec(memory_space=pltpu.HBM)
    z_groups = [[z * Y + y for z in range(Z)] for y in range(Y)]
    y_groups = [[z * Y + y for y in range(Y)] for z in range(Z)]
    coords = jnp.stack([place // Y, place % Y]).astype(jnp.int32)
    first, second, back_second, back_first, twists = transform_tables()
    params = pltpu.CompilerParams(vmem_limit_bytes=60 << 20)
    spectrum_shape = jax.ShapeDtypeStruct((GROUPS, BLOCKS * LANE8, 2 * BLOCK), bf16)
    plane = (BLOCKS, CHANS, BLOCK)
    work = 2 * GROUPS * (512 * 256 * 128 + 256 * 256 * 256)
    pair = 2 * LANE8
    same = lambda table: pl.BlockSpec(table.shape, lambda i, rank=table.ndim: (0,) * rank)

    own_shape = (2, in_chans, 2 * CHANS)
    out_split = readout_weight.reshape(2, Z, Y, CHANS, in_chans)
    block, own_weights, own_out = pl.pallas_call(
        prepare_kernel,
        out_shape=(
            jax.ShapeDtypeStruct((BLOCK + BLOCK // TRIAL, in_chans), bf16),
            jax.ShapeDtypeStruct(own_shape, bf16),
            jax.ShapeDtypeStruct((2, Z, CHANS, in_chans), bf16),
        ),
        in_specs=[scalar] * 3 + whole(1) + [hbm] * 2,
        out_specs=tuple(whole(2)) + (hbm,),
        scratch_shapes=[pltpu.VMEM(own_shape, bf16), pltpu.VMEM(own_shape, bf16), pltpu.SemaphoreType.DMA((3,))],
        compiler_params=params,
        cost_estimate=pl.CostEstimate(flops=1 << 16, bytes_accessed=1 << 19, transcendentals=0),
        name="prepare",
    )(place.astype(jnp.int32)[None], session_of_bin, session_slot, spikes, readin_weight, out_split)
    chunk = jnp.stack([block, along_y(block, 1), along_y(block, -1), along_y(block, 2)])
    own_marks = chunk[:, BLOCK:, :]
    right, left = along_z(chunk, 1), along_z(chunk, -1)
    chunks = [chunk, right, left]

    in_weights = lax.all_gather(own_weights, "grp", axis=0, tiled=True)
    right, left, own_marks, own_out = lax.optimization_barrier((right, left, own_marks, own_out))
    split = own_out.reshape(2, Z * CHANS, in_chans)
    out_weights = lax.all_gather(split, "grp", axis=0, tiled=True)
    right, left = along_z(right, 1), along_z(left, -1)
    chunks += [right, left]
    turned = out_grad[0].T.reshape(BLOCKS, CHANS, BLOCK)
    taps = lax.dynamic_slice_in_dim(short_kernel, place * CHANS, CHANS, 1)
    taps = jnp.broadcast_to(taps[:, :, None], (short_kernel.shape[0], CHANS, BLOCK))
    gains = jnp.broadcast_to(skip_gain[:, None], (CHANS, BLOCK))
    ready = (right, left, taps, gains, coords, turned)
    right, left, taps, gains, coords, turned = lax.optimization_barrier(ready)
    right, left = along_z(right, 1), along_z(left, -1)
    slot_count = session_slot.shape[0]
    width = 2 * CHANS

    def read_in(pieces):
        blocks = len(pieces) * Y
        return pl.pallas_call(
            read_in_kernel,
            out_shape=jax.ShapeDtypeStruct((blocks, width, BLOCK), bf16),
            in_specs=[hbm] * (1 + len(pieces)),
            out_specs=whole(1)[0],
            scratch_shapes=[
                pltpu.VMEM((blocks,) + chunk.shape[1:], bf16),
                pltpu.VMEM((slot_count // 2, in_chans, 2 * width), bf16),
                pltpu.SemaphoreType.DMA((slot_count,)),
                pltpu.SemaphoreType.DMA((len(pieces),)),
            ],
            compiler_params=params,
            cost_estimate=pl.CostEstimate(flops=work, bytes_accessed=4 << 20, transcendentals=0),
            name="read_in",
        )(in_weights, *pieces)

    early = read_in(chunks)
    right, left, early, long_filter = lax.optimization_barrier((right, left, early, long_filter))
    last = along_z(right, 1)
    later = read_in([right, left])
    filter_spectrum = pl.pallas_call(
        filter_kernel,
        out_shape=spectrum_shape,
        grid=(GROUPS // 2,),
        in_specs=[pl.BlockSpec((pair, LENGTH), lambda i: (i, 0))] + [same(table) for table in (first, second, twists)],
        out_specs=pl.BlockSpec((2,) + spectrum_shape.shape[1:], lambda i: (i, 0, 0)),
        compiler_params=params,
        cost_estimate=pl.CostEstimate(flops=work, bytes_accessed=4 << 20, transcendentals=0),
        name="filter_transform",
    )(long_filter, first, second, twists)
    last, later, filter_spectrum, turned = lax.optimization_barrier((last, later, filter_spectrum, turned))
    grads = lax.all_to_all(turned, "seq", split_axis=0, concat_axis=0, tiled=True)

    tables = (first, second, back_second, back_first)
    gated, gates, spectrum = pl.pallas_call(
        forward_kernel,
        out_shape=(
            jax.ShapeDtypeStruct(plane, bf16),
            jax.ShapeDtypeStruct(plane, bf16),
            spectrum_shape,
        ),
        in_specs=[scalar] + whole(3) + [hbm] * (5 + 4),
        out_specs=(hbm,) * 3,
        scratch_shapes=[
            pltpu.VMEM((BLOCKS, 2 * CHANS, BLOCK), bf16),
            pltpu.VMEM(chunk.shape, bf16),
            pltpu.VMEM((slot_count // 2, in_chans, 4 * CHANS), bf16),
            pltpu.VMEM(spectrum_shape.shape, bf16),
            pltpu.VMEM(plane, bf16),
            pltpu.VMEM(spectrum_shape.shape, bf16),
        ]
        + [pltpu.VMEM(table.shape, bf16) for table in tables]
        + [pltpu.SemaphoreType.DMA((count,)) for count in (slot_count, (Z - 1) * Y, 6)]
        + [pltpu.SemaphoreType.DMA((2, GROUPS // 2 + 1))],
        compiler_params=params,
        cost_estimate=pl.CostEstimate(flops=4 * work, bytes_accessed=8 << 20, transcendentals=0),
        name="long_convolution",
    )(coords, taps, gains, twists, filter_spectrum, in_weights, early, later, last, *tables)

    gated = gated.reshape(Z, Y, CHANS, BLOCK)
    arrived = lax.all_to_all(gated, "seq", split_axis=0, concat_axis=0, tiled=True, axis_index_groups=z_groups)
    own_grad = pl.pallas_call(
        gradient_kernel,
        out_shape=jax.ShapeDtypeStruct((CHANS, LENGTH), bf16),
        grid=(GROUPS // 4,),
        in_specs=[pl.BlockSpec((BLOCKS, 2 * pair, BLOCK), lambda i: (0, i, 0))] * 2
        + [pl.BlockSpec((4,) + spectrum_shape.shape[1:], lambda i: (i, 0, 0))]
        + [same(table) for table in tables + (twists,)],
        out_specs=pl.BlockSpec((2 * pair, LENGTH), lambda i: (i, 0)),
        compiler_params=params,
        cost_estimate=pl.CostEstimate(flops=2 * work, bytes_accessed=4 << 20, transcendentals=0),
        name="filter_gradient",
    )(grads, gates, spectrum, *tables, twists)
    all_grads = lax.all_gather(own_grad, "grp", axis=0, tiled=False)
    devices = all_grads.shape[0]
    filter_grad = pl.pallas_call(
        sum_kernel,
        out_shape=jax.ShapeDtypeStruct((CHANS, LENGTH), f32),
        in_specs=[hbm],
        out_specs=hbm,
        scratch_shapes=[
            pltpu.VMEM(all_grads.shape, bf16),
            pltpu.VMEM((CHANS, LENGTH), f32),
            pltpu.SemaphoreType.DMA((CHANS // pair, devices)),
            pltpu.SemaphoreType.DMA((CHANS // pair,)),
        ],
        compiler_params=params,
        cost_estimate=pl.CostEstimate(flops=all_grads.size, bytes_accessed=5 << 20, transcendentals=0),
        name="sum_gradients",
    )(all_grads)
    partial = pl.pallas_call(
        read_out_kernel,
        out_shape=jax.ShapeDtypeStruct((Y, BLOCK, in_chans), bf16),
        in_specs=[scalar] + [hbm] * 3,
        out_specs=whole(1)[0],
        scratch_shapes=[
            pltpu.VMEM(out_weights.shape, bf16),
            pltpu.VMEM((Z, Y, CHANS, BLOCK), bf16),
            pltpu.VMEM((Y, BLOCK // TRIAL, in_chans), bf16),
        ]
        + [pltpu.SemaphoreType.DMA((count,)) for count in (slot_count, 2)],
        compiler_params=params,
        cost_estimate=pl.CostEstimate(flops=2 * 512 * 512 * 4096, bytes_accessed=6 << 20, transcendentals=0),
        name="read_out",
    )(coords, arrived, own_marks, out_weights)
    pieces = lax.all_to_all(partial, "seq", split_axis=0, concat_axis=0, tiled=True, axis_index_groups=y_groups)
    denoised = jnp.sum(pieces.astype(f32), 0).astype(bf16)
    return denoised[None], filter_grad


def solution(mesh):
    placed = (
        P("grp", "seq", None),
        P("grp", "seq"),
        P(),
        P("grp", None, None),
        P(),
        P("seq", None),
        P("seq"),
        P("grp", None, None),
        P("grp", "seq", None),
    )
    return jax.shard_map(
        local,
        mesh=mesh,
        in_specs=placed,
        out_specs=(P("grp", "seq", None), P("seq", None)),
        check_vma=False,
    )
```

```python
import jax
import jax.numpy as jnp
import numpy as np
from jax import lax
from jax.experimental import pallas as pl
from jax.experimental.pallas import tpu as pltpu
from jax.sharding import PartitionSpec as P

BLOCK = 128
TRIAL = 16
Z = 8
Y = 4
BLOCKS = Z * Y
CHANS = 64
LANE8 = 8
GROUPS = CHANS // LANE8
LENGTH = BLOCKS * BLOCK
f32 = jnp.float32
bf16 = jnp.bfloat16


def transform_tables():
    slow = np.arange(BLOCKS)
    fast = np.arange(BLOCK)
    first = np.exp(-2j * np.pi * (np.outer(slow, slow) / BLOCKS + slow[None, :] / (4.0 * BLOCKS)))
    twist = np.exp(-2j * np.pi * (slow[:, None] + 0.25) * fast[None, :] / LENGTH)
    second = np.exp(-2j * np.pi * np.outer(fast, fast) / BLOCK)
    eye = np.eye(LANE8)
    spread_first = np.concatenate([np.kron(first.real, eye), np.kron(first.imag, eye)], 0)
    forward_second = np.block([[second.real, second.imag], [-second.imag, second.real]])
    back = second.conj()
    back_second = np.block([[back.real, back.imag], [-back.imag, back.real]])
    back_first = first.conj().T / LENGTH
    spread_back = np.concatenate([np.kron(back_first.real, eye), np.kron(-back_first.imag, eye)], 1)
    as_bf16 = lambda table: jnp.asarray(table.astype(np.float32), bf16)
    twists = np.stack([twist.real, twist.imag]).astype(np.float32)
    return (
        as_bf16(spread_first),
        as_bf16(forward_second),
        as_bf16(back_second),
        as_bf16(spread_back),
        jnp.asarray(twists),
    )


def twists_of(twist_ref):
    shape = (BLOCKS, LANE8, BLOCK)
    cosine = jnp.broadcast_to(twist_ref[0][:, None, :], shape).reshape(BLOCKS * LANE8, BLOCK)
    sine = jnp.broadcast_to(twist_ref[1][:, None, :], shape).reshape(BLOCKS * LANE8, BLOCK)
    return cosine, sine


def forward(low, high, first_ref, second_ref, cosine, sine):
    rows = BLOCKS * LANE8
    signals = jnp.concatenate([low, high], 1).astype(bf16)
    part = jnp.dot(first_ref[...], signals, preferred_element_type=f32)
    turned = []
    for lanes in (slice(0, BLOCK), slice(BLOCK, 2 * BLOCK)):
        real, imag = part[:rows, lanes], part[rows:, lanes]
        turned.append(jnp.concatenate([real * cosine - imag * sine, real * sine + imag * cosine], 1))
    return jnp.dot(jnp.concatenate(turned, 0).astype(bf16), second_ref[...], preferred_element_type=f32)


def backward(spectra, back_second_ref, back_first_ref, cosine, sine):
    rows = BLOCKS * LANE8
    part = jnp.dot(spectra.astype(bf16), back_second_ref[...], preferred_element_type=f32)
    turned = []
    for start in (0, rows):
        real, imag = part[start : start + rows, :BLOCK], part[start : start + rows, BLOCK:]
        turned.append(jnp.concatenate([real * cosine + imag * sine, imag * cosine - real * sine], 0))
    return jnp.dot(back_first_ref[...], jnp.concatenate(turned, 1).astype(bf16), preferred_element_type=f32)


def filter_kernel(filter_ref, first_ref, second_ref, twist_ref, spectrum_ref):
    cosine, sine = twists_of(twist_ref)
    rows = BLOCKS * LANE8
    signals = []
    for start in (0, LANE8):
        pieces = [filter_ref[start : start + LANE8, i * BLOCK : (i + 1) * BLOCK] for i in range(BLOCKS)]
        signals.append(jnp.concatenate(pieces, 0))
    spectra = forward(*signals, first_ref, second_ref, cosine, sine)
    spectrum_ref[...] = spectra.astype(bf16).reshape(2, rows, 2 * BLOCK)


def start_all(copies):
    for copy in copies:
        copy.start()


def wait_all(copies):
    for copy in copies:
        copy.wait()


def weight_copies(weight_hbm, weight, sems):
    copies = []
    for slot in range(weight_hbm.shape[0]):
        lanes = pl.ds(slot % 2 * 2 * CHANS, 2 * CHANS)
        copies.append(pltpu.make_async_copy(weight_hbm.at[slot], weight.at[slot // 2, :, lanes], sems.at[slot]))
    return copies


def spread(rows, marks, count):
    trials, width = marks.shape
    marks = jnp.broadcast_to(marks[:, None, :], (trials, TRIAL, width)).reshape(trials * TRIAL, width).astype(bf16)
    nothing = jnp.zeros_like(rows)
    return jnp.concatenate([jnp.where(marks == number, rows, nothing) for number in range(count)], 1)


def project(rows_ref, start, blocks, weight):
    width = 2 * CHANS
    in_chans = rows_ref.shape[2]
    rows = rows_ref[pl.ds(start, blocks), :BLOCK, :].reshape(blocks * BLOCK, in_chans)
    marks = rows_ref[pl.ds(start, blocks), BLOCK:, :].astype(f32).reshape(blocks * BLOCK // TRIAL, in_chans)
    wide = spread(rows, jnp.floor(marks * 0.5), weight.shape[0])
    product = jnp.dot(wide, weight[...].reshape(-1, 2 * width), preferred_element_type=f32)
    odd = (marks - 2 * jnp.floor(marks * 0.5))[:, :width]
    trials = odd.shape[0]
    odd = jnp.broadcast_to(odd[:, None, :], (trials, TRIAL, width)).reshape(trials * TRIAL, width)
    chosen = jnp.where(odd > 0.5, product[:, width:], product[:, :width])
    return [chosen[i * BLOCK : (i + 1) * BLOCK].T.astype(bf16) for i in range(blocks)]


def block_of(place_ref, z_step, y_index):
    y_step = jnp.where(y_index < 2, Y - y_index, y_index - 1)
    return lax.rem(place_ref[0] + z_step, Z) * Y + lax.rem(place_ref[1] + y_step, Y)


def z_step_of(index):
    return jnp.where(index % 2 == 1, Z - (index + 1) // 2, index // 2)


def read_in_kernel(weight_hbm, *rest):
    chunk_hbms = rest[:-5]
    out_ref, rows, weight, weight_sems, sems = rest[-5:]
    loads = weight_copies(weight_hbm, weight, weight_sems)
    for index, chunk in enumerate(chunk_hbms):
        loads.append(pltpu.make_async_copy(chunk, rows.at[pl.ds(index * Y, Y)], sems.at[index]))
    start_all(loads)
    wait_all(loads)

    def step(index, carry):
        blocks = project(rows, index * Y, Y, weight)
        for y_index in range(Y):
            out_ref[index * Y + y_index] = blocks[y_index]
        return carry

    lax.fori_loop(0, len(chunk_hbms), step, 0)


def forward_kernel(place_ref, taps_ref, gain_ref, twist_ref, filter_hbm, weight_hbm, *rest):
    early_hbms, (chunk_hbm, *rest) = rest[:2], rest[2:]
    table_hbms, rest = rest[:4], rest[4:]
    gated_hbm, gate_hbm, spectrum_hbm, both, rows, weight, spectra, gated_all, spectrum_all, *rest = rest
    tables = rest[:4]
    weight_sems, early_sems, sems, store_sems = rest[4:]
    loads = weight_copies(weight_hbm, weight, weight_sems)
    others = []
    for early_hbm in early_hbms:
        for index in range(early_hbm.shape[0]):
            number = len(others)
            target = both.at[block_of(place_ref, z_step_of(number // Y), number % Y)]
            others.append(pltpu.make_async_copy(early_hbm.at[index], target, early_sems.at[number]))
    pairs = [(filter_hbm, spectra)] + list(zip(table_hbms, tables))
    others += [pltpu.make_async_copy(source, target, sems.at[index]) for index, (source, target) in enumerate(pairs)]
    loads.append(pltpu.make_async_copy(chunk_hbm, rows, sems.at[len(pairs)]))
    start_all(loads)
    start_all(others)
    wait_all(loads)
    last = project(rows, 0, Y, weight)
    for y_index in range(Y):
        both[block_of(place_ref, z_step_of(Z - 1), y_index)] = last[y_index]
    cosine, sine = twists_of(twist_ref)
    lane = lax.broadcasted_iota(jnp.int32, (BLOCKS, LANE8, BLOCK), 2)
    count = BLOCKS * LANE8
    cube = (BLOCKS, LANE8, BLOCK)
    wait_all(others)
    gate_store = pltpu.make_async_copy(both.at[:, pl.ds(CHANS, CHANS), :], gate_hbm, store_sems.at[0, GROUPS // 2])
    gate_store.start()
    first_ref, second_ref, back_second_ref, back_first_ref = tables

    def stores_of(pair):
        here = pl.ds(pl.multiple_of(pair * 2 * LANE8, 2 * LANE8), 2 * LANE8)
        groups = pl.ds(pair * 2, 2)
        return [
            pltpu.make_async_copy(gated_all.at[:, here, :], gated_hbm.at[:, here, :], store_sems.at[0, pair]),
            pltpu.make_async_copy(spectrum_all.at[groups], spectrum_hbm.at[groups], store_sems.at[1, pair]),
        ]

    def short(value, group):
        taps = taps_ref[:, pl.ds(pl.multiple_of(group * LANE8, LANE8), LANE8), :]
        total = taps[0][None] * value
        for shift in (1, 2):
            rolled = pltpu.roll(value.reshape(count, BLOCK), shift, 1).reshape(cube)
            before = jnp.concatenate([jnp.zeros((1, LANE8, BLOCK), f32), rolled[:-1]], 0)
            total = total + taps[shift][None] * jnp.where(lane < shift, before, rolled)
        return total.astype(bf16).astype(f32).reshape(count, BLOCK)

    def step(pair, carry):
        here = pl.ds(pl.multiple_of(pair * 2 * LANE8, 2 * LANE8), 2 * LANE8)
        there = pl.ds(pl.multiple_of(CHANS + pair * 2 * LANE8, 2 * LANE8), 2 * LANE8)
        value = both[:, here, :].astype(f32)
        gate = both[:, there, :]
        signals = [short(value[:, i * LANE8 : (i + 1) * LANE8], pair * 2 + i) for i in range(2)]
        own = forward(*signals, first_ref, second_ref, cosine, sine)
        spectrum_all[pl.ds(pair * 2, 2)] = own.reshape(2, count, 2 * BLOCK).astype(bf16)
        weight = spectra[pl.ds(pair * 2, 2)].reshape(2 * count, 2 * BLOCK).astype(f32)
        own_re, own_im = own[:, :BLOCK], own[:, BLOCK:]
        filter_re, filter_im = weight[:, :BLOCK], weight[:, BLOCK:]
        mix = jnp.concatenate([own_re * filter_re - own_im * filter_im, own_re * filter_im + own_im * filter_re], 1)
        result = backward(mix, back_second_ref, back_first_ref, cosine, sine)
        signal = jnp.concatenate([piece.reshape(cube) for piece in signals], 1)
        long_part = jnp.concatenate([result[:, i * BLOCK : (i + 1) * BLOCK].reshape(cube) for i in range(2)], 1)
        mixed = (long_part + gain_ref[here, :][None] * signal).astype(bf16).astype(f32)
        gated_all[:, here, :] = (gate.astype(f32) * mixed).astype(bf16)
        start_all(stores_of(pair))
        return carry

    lax.fori_loop(0, GROUPS // 2, step, 0, unroll=2)
    for pair in range(GROUPS // 2):
        wait_all(stores_of(pair))
    gate_store.wait()


def gradient_kernel(grad_ref, gate_ref, spectrum_ref, first_ref, second_ref, back_second_ref, back_first_ref, twist_ref, out_ref):
    cosine, sine = twists_of(twist_ref)
    count = BLOCKS * LANE8
    pair = 2 * LANE8
    for start in range(0, grad_ref.shape[1], pair):
        here = slice(start, start + pair)
        products = (grad_ref[:, here, :].astype(f32) * gate_ref[:, here, :].astype(f32)).astype(bf16).astype(f32)
        signals = [products[:, i * LANE8 : (i + 1) * LANE8].reshape(count, BLOCK) for i in range(2)]
        spectra = forward(*signals, first_ref, second_ref, cosine, sine)
        own = spectrum_ref[start // LANE8 : start // LANE8 + 2].reshape(2 * count, 2 * BLOCK).astype(f32)
        own_re, own_im = own[:, :BLOCK], own[:, BLOCK:]
        grad_re, grad_im = spectra[:, :BLOCK], spectra[:, BLOCK:]
        lag = jnp.concatenate([own_re * grad_re + own_im * grad_im, own_re * grad_im - own_im * grad_re], 1)
        result = backward(lag, back_second_ref, back_first_ref, cosine, sine)
        both = []
        for half in range(2):
            lanes = slice(half * BLOCK, (half + 1) * BLOCK)
            both.append(jnp.concatenate([result[i * LANE8 : (i + 1) * LANE8, lanes] for i in range(BLOCKS)], 1))
        out_ref[here, :] = jnp.concatenate(both, 0).astype(bf16)


def read_out_kernel(place_ref, rows_hbm, marks_hbm, weight_hbm, out_ref, weight, rows_all, chunk_all, weight_sems, sems):
    slots, inner, width = weight.shape
    trials = BLOCK // TRIAL
    first = [pltpu.make_async_copy(rows_hbm, rows_all, sems.at[0]), pltpu.make_async_copy(marks_hbm, chunk_all, sems.at[1])]
    loads = [pltpu.make_async_copy(weight_hbm.at[slot], weight.at[slot], weight_sems.at[slot]) for slot in range(slots)]
    start_all(first)
    start_all(loads)
    wait_all(first)
    places = [block_of(place_ref, 0, index) - place_ref[0] * Y for index in range(Y)]
    rows = jnp.concatenate([rows_all[:, block, :, :].reshape(inner, BLOCK).T for block in places], 0)
    marks = chunk_all[...].astype(f32).reshape(Y * trials, width)
    marks = jnp.broadcast_to(marks[:, None, :], (Y * trials, TRIAL, width)).reshape(Y * BLOCK, width)
    wait_all(loads)
    total = jnp.zeros((Y * BLOCK, width), f32)
    for slot in range(slots):
        product = jnp.dot(rows, weight[slot], preferred_element_type=f32)
        total = jnp.where(marks == slot, product, total)
    for index, block in enumerate(places):
        out_ref[block] = total[index * BLOCK : (index + 1) * BLOCK].astype(bf16)


def sum_kernel(parts_hbm, out_hbm, parts, total, in_sems, out_sems):
    count, rows, _ = parts.shape
    step = 2 * LANE8
    loads = []
    stores = []
    for index in range(rows // step):
        here = pl.ds(index * step, step)
        for part in range(count):
            load = pltpu.make_async_copy(parts_hbm.at[part, here, :], parts.at[part, here, :], in_sems.at[index, part])
            loads.append(load)
        stores.append(pltpu.make_async_copy(total.at[here, :], out_hbm.at[here, :], out_sems.at[index]))
    start_all(loads)
    for index in range(rows // step):
        wait_all(loads[index * count : (index + 1) * count])
        here = slice(index * step, (index + 1) * step)
        running = parts[0, here, :].astype(f32)
        for part in range(1, count):
            running = running + parts[part, here, :].astype(f32)
        total[here, :] = running
        stores[index].start()
    wait_all(stores)


def prepare_kernel(place_ref, session_ref, slot_ref, spikes_ref, weight_hbm, out_hbm, block_ref, own_ref, own_out_ref, value, gate, sems):
    place = place_ref[0]
    half = weight_hbm.shape[2] // 2
    window = pl.multiple_of(place // 2 * 2 * CHANS, 2 * CHANS)
    loads = [
        pltpu.make_async_copy(weight_hbm.at[:, :, pl.ds(window, 2 * CHANS)], value, sems.at[0]),
        pltpu.make_async_copy(weight_hbm.at[:, :, pl.ds(half + window, 2 * CHANS)], gate, sems.at[1]),
    ]
    start_all(loads)
    moved = pltpu.make_async_copy(out_hbm.at[:, :, lax.rem(place, Y)], own_out_ref, sems.at[2])
    moved.start()
    trials = BLOCK // TRIAL
    width = block_ref.shape[1]
    row = lax.broadcasted_iota(jnp.int32, (trials, width), 0)
    marks = jnp.zeros((trials, width), jnp.int32)
    for trial in range(trials):
        marks = jnp.where(row == trial, slot_ref[session_ref[0, trial * TRIAL]], marks)
    block_ref[:BLOCK, :] = spikes_ref[0]
    block_ref[BLOCK:, :] = marks.astype(f32).astype(bf16)
    wait_all(loads)
    slots, inner, lanes = own_ref.shape
    odd = place % 2
    low = pltpu.roll(value[...].astype(f32).reshape(slots * inner, lanes), odd * CHANS, 1)
    high = pltpu.roll(gate[...].astype(f32).reshape(slots * inner, lanes), (1 - odd) * CHANS, 1)
    lane = lax.broadcasted_iota(jnp.int32, (slots * inner, lanes), 1)
    own_ref[...] = jnp.where(lane < CHANS, low, high).astype(bf16).reshape(slots, inner, lanes)
    moved.wait()


def along_y(value, step):
    return lax.ppermute(value, "seq", [(z * Y + y, z * Y + (y + step) % Y) for z in range(Z) for y in range(Y)])


def along_z(value, step):
    return lax.ppermute(value, "seq", [(z * Y + y, (z + step) % Z * Y + y) for z in range(Z) for y in range(Y)])


def whole(count):
    return [pl.BlockSpec(memory_space=pltpu.VMEM)] * count


def local(spikes, session_of_bin, session_slot, readin_weight, short_kernel, long_filter, skip_gain, readout_weight, out_grad):
    in_chans = spikes.shape[2]
    place = lax.axis_index("seq")
    scalar = pl.BlockSpec(memory_space=pltpu.SMEM)
    hbm = pl.BlockSpec(memory_space=pltpu.HBM)
    z_groups = [[z * Y + y for z in range(Z)] for y in range(Y)]
    y_groups = [[z * Y + y for y in range(Y)] for z in range(Z)]
    coords = jnp.stack([place // Y, place % Y]).astype(jnp.int32)
    first, second, back_second, back_first, twists = transform_tables()
    params = pltpu.CompilerParams(vmem_limit_bytes=60 << 20)
    spectrum_shape = jax.ShapeDtypeStruct((GROUPS, BLOCKS * LANE8, 2 * BLOCK), bf16)
    plane = (BLOCKS, CHANS, BLOCK)
    work = 2 * GROUPS * (512 * 256 * 128 + 256 * 256 * 256)
    pair = 2 * LANE8
    same = lambda table: pl.BlockSpec(table.shape, lambda i, rank=table.ndim: (0,) * rank)

    own_shape = (2, in_chans, 2 * CHANS)
    out_split = readout_weight.reshape(2, Z, Y, CHANS, in_chans)
    block, own_weights, own_out = pl.pallas_call(
        prepare_kernel,
        out_shape=(
            jax.ShapeDtypeStruct((BLOCK + BLOCK // TRIAL, in_chans), bf16),
            jax.ShapeDtypeStruct(own_shape, bf16),
            jax.ShapeDtypeStruct((2, Z, CHANS, in_chans), bf16),
        ),
        in_specs=[scalar] * 3 + whole(1) + [hbm] * 2,
        out_specs=tuple(whole(3)),
        scratch_shapes=[pltpu.VMEM(own_shape, bf16), pltpu.VMEM(own_shape, bf16), pltpu.SemaphoreType.DMA((3,))],
        compiler_params=params,
        cost_estimate=pl.CostEstimate(flops=1 << 16, bytes_accessed=1 << 19, transcendentals=0),
        name="prepare",
    )(place.astype(jnp.int32)[None], session_of_bin, session_slot, spikes, readin_weight, out_split)
    chunk = jnp.stack([block, along_y(block, 1), along_y(block, -1), along_y(block, 2)])
    own_marks = chunk[:, BLOCK:, :]
    right, left = along_z(chunk, 1), along_z(chunk, -1)
    chunks = [chunk, right, left]

    in_weights = lax.all_gather(own_weights, "grp", axis=0, tiled=True)
    right, left, own_marks, own_out = lax.optimization_barrier((right, left, own_marks, own_out))
    split = own_out.reshape(2, Z * CHANS, in_chans)
    out_weights = lax.all_gather(split, "grp", axis=0, tiled=True)
    right, left = along_z(right, 1), along_z(left, -1)
    chunks += [right, left]
    turned = out_grad[0].T.reshape(BLOCKS, CHANS, BLOCK)
    taps = lax.dynamic_slice_in_dim(short_kernel, place * CHANS, CHANS, 1)
    taps = jnp.broadcast_to(taps[:, :, None], (short_kernel.shape[0], CHANS, BLOCK))
    gains = jnp.broadcast_to(skip_gain[:, None], (CHANS, BLOCK))
    ready = (right, left, taps, gains, coords, turned)
    right, left, taps, gains, coords, turned = lax.optimization_barrier(ready)
    right, left = along_z(right, 1), along_z(left, -1)
    slot_count = session_slot.shape[0]
    width = 2 * CHANS

    def read_in(pieces):
        blocks = len(pieces) * Y
        return pl.pallas_call(
            read_in_kernel,
            out_shape=jax.ShapeDtypeStruct((blocks, width, BLOCK), bf16),
            in_specs=[hbm] * (1 + len(pieces)),
            out_specs=whole(1)[0],
            scratch_shapes=[
                pltpu.VMEM((blocks,) + chunk.shape[1:], bf16),
                pltpu.VMEM((slot_count // 2, in_chans, 2 * width), bf16),
                pltpu.SemaphoreType.DMA((slot_count,)),
                pltpu.SemaphoreType.DMA((len(pieces),)),
            ],
            compiler_params=params,
            cost_estimate=pl.CostEstimate(flops=work, bytes_accessed=4 << 20, transcendentals=0),
            name="read_in",
        )(in_weights, *pieces)

    early = read_in(chunks)
    ready = (right, left, early, long_filter, turned)
    right, left, early, long_filter, turned = lax.optimization_barrier(ready)
    grads = lax.all_to_all(turned, "seq", split_axis=0, concat_axis=0, tiled=True)
    last = along_z(right, 1)
    later = read_in([right, left])
    filter_spectrum = pl.pallas_call(
        filter_kernel,
        out_shape=spectrum_shape,
        grid=(GROUPS // 2,),
        in_specs=[pl.BlockSpec((pair, LENGTH), lambda i: (i, 0))] + [same(table) for table in (first, second, twists)],
        out_specs=pl.BlockSpec((2,) + spectrum_shape.shape[1:], lambda i: (i, 0, 0)),
        compiler_params=params,
        cost_estimate=pl.CostEstimate(flops=work, bytes_accessed=4 << 20, transcendentals=0),
        name="filter_transform",
    )(long_filter, first, second, twists)
    last, later, filter_spectrum = lax.optimization_barrier((last, later, filter_spectrum))

    tables = (first, second, back_second, back_first)
    gated, gates, spectrum = pl.pallas_call(
        forward_kernel,
        out_shape=(
            jax.ShapeDtypeStruct(plane, bf16),
            jax.ShapeDtypeStruct(plane, bf16),
            spectrum_shape,
        ),
        in_specs=[scalar] + whole(3) + [hbm] * (5 + 4),
        out_specs=(hbm,) * 3,
        scratch_shapes=[
            pltpu.VMEM((BLOCKS, 2 * CHANS, BLOCK), bf16),
            pltpu.VMEM(chunk.shape, bf16),
            pltpu.VMEM((slot_count // 2, in_chans, 4 * CHANS), bf16),
            pltpu.VMEM(spectrum_shape.shape, bf16),
            pltpu.VMEM(plane, bf16),
            pltpu.VMEM(spectrum_shape.shape, bf16),
        ]
        + [pltpu.VMEM(table.shape, bf16) for table in tables]
        + [pltpu.SemaphoreType.DMA((count,)) for count in (slot_count, (Z - 1) * Y, 6)]
        + [pltpu.SemaphoreType.DMA((2, GROUPS // 2 + 1))],
        compiler_params=params,
        cost_estimate=pl.CostEstimate(flops=4 * work, bytes_accessed=8 << 20, transcendentals=0),
        name="long_convolution",
    )(coords, taps, gains, twists, filter_spectrum, in_weights, early, later, last, *tables)

    gated = gated.reshape(Z, Y, CHANS, BLOCK)
    arrived = lax.all_to_all(gated, "seq", split_axis=0, concat_axis=0, tiled=True, axis_index_groups=z_groups)
    own_grad = pl.pallas_call(
        gradient_kernel,
        out_shape=jax.ShapeDtypeStruct((CHANS, LENGTH), bf16),
        grid=(GROUPS // 4,),
        in_specs=[pl.BlockSpec((BLOCKS, 2 * pair, BLOCK), lambda i: (0, i, 0))] * 2
        + [pl.BlockSpec((4,) + spectrum_shape.shape[1:], lambda i: (i, 0, 0))]
        + [same(table) for table in tables + (twists,)],
        out_specs=pl.BlockSpec((2 * pair, LENGTH), lambda i: (i, 0)),
        compiler_params=params,
        cost_estimate=pl.CostEstimate(flops=2 * work, bytes_accessed=4 << 20, transcendentals=0),
        name="filter_gradient",
    )(grads, gates, spectrum, *tables, twists)
    all_grads = lax.all_gather(own_grad, "grp", axis=0, tiled=False)
    devices = all_grads.shape[0]
    filter_grad = pl.pallas_call(
        sum_kernel,
        out_shape=jax.ShapeDtypeStruct((CHANS, LENGTH), f32),
        in_specs=[hbm],
        out_specs=hbm,
        scratch_shapes=[
            pltpu.VMEM(all_grads.shape, bf16),
            pltpu.VMEM((CHANS, LENGTH), f32),
            pltpu.SemaphoreType.DMA((CHANS // pair, devices)),
            pltpu.SemaphoreType.DMA((CHANS // pair,)),
        ],
        compiler_params=params,
        cost_estimate=pl.CostEstimate(flops=all_grads.size, bytes_accessed=5 << 20, transcendentals=0),
        name="sum_gradients",
    )(all_grads)
    partial = pl.pallas_call(
        read_out_kernel,
        out_shape=jax.ShapeDtypeStruct((Y, BLOCK, in_chans), bf16),
        in_specs=[scalar] + [hbm] * 3,
        out_specs=whole(1)[0],
        scratch_shapes=[
            pltpu.VMEM(out_weights.shape, bf16),
            pltpu.VMEM((Z, Y, CHANS, BLOCK), bf16),
            pltpu.VMEM((Y, BLOCK // TRIAL, in_chans), bf16),
        ]
        + [pltpu.SemaphoreType.DMA((count,)) for count in (slot_count, 2)],
        compiler_params=params,
        cost_estimate=pl.CostEstimate(flops=2 * 512 * 512 * 4096, bytes_accessed=6 << 20, transcendentals=0),
        name="read_out",
    )(coords, arrived, own_marks, out_weights)
    pieces = lax.all_to_all(partial, "seq", split_axis=0, concat_axis=0, tiled=True, axis_index_groups=y_groups)
    denoised = jnp.sum(pieces.astype(f32), 0).astype(bf16)
    return denoised[None], filter_grad


def solution(mesh):
    placed = (
        P("grp", "seq", None),
        P("grp", "seq"),
        P(),
        P("grp", None, None),
        P(),
        P("seq", None),
        P("seq"),
        P("grp", None, None),
        P("grp", "seq", None),
    )
    return jax.shard_map(
        local,
        mesh=mesh,
        in_specs=placed,
        out_specs=(P("grp", "seq", None), P("seq", None)),
        check_vma=False,
    )
```

```python
import jax
import jax.numpy as jnp
import numpy as np
from jax import lax
from jax.experimental import pallas as pl
from jax.experimental.pallas import tpu as pltpu
from jax.sharding import PartitionSpec as P

BLOCK = 128
TRIAL = 16
Z = 8
Y = 4
BLOCKS = Z * Y
CHANS = 64
LANE8 = 8
GROUPS = CHANS // LANE8
LENGTH = BLOCKS * BLOCK
f32 = jnp.float32
bf16 = jnp.bfloat16


def transform_tables():
    slow = np.arange(BLOCKS)
    fast = np.arange(BLOCK)
    first = np.exp(-2j * np.pi * (np.outer(slow, slow) / BLOCKS + slow[None, :] / (4.0 * BLOCKS)))
    twist = np.exp(-2j * np.pi * (slow[:, None] + 0.25) * fast[None, :] / LENGTH)
    second = np.exp(-2j * np.pi * np.outer(fast, fast) / BLOCK)
    eye = np.eye(LANE8)
    spread_first = np.concatenate([np.kron(first.real, eye), np.kron(first.imag, eye)], 0)
    forward_second = np.block([[second.real, second.imag], [-second.imag, second.real]])
    back = second.conj()
    back_second = np.block([[back.real, back.imag], [-back.imag, back.real]])
    back_first = first.conj().T / LENGTH
    spread_back = np.concatenate([np.kron(back_first.real, eye), np.kron(-back_first.imag, eye)], 1)
    as_bf16 = lambda table: jnp.asarray(table.astype(np.float32), bf16)
    twists = np.stack([twist.real, twist.imag]).astype(np.float32)
    return (
        as_bf16(spread_first),
        as_bf16(forward_second),
        as_bf16(back_second),
        as_bf16(spread_back),
        jnp.asarray(twists),
    )


def twists_of(twist_ref):
    shape = (BLOCKS, LANE8, BLOCK)
    cosine = jnp.broadcast_to(twist_ref[0][:, None, :], shape).reshape(BLOCKS * LANE8, BLOCK)
    sine = jnp.broadcast_to(twist_ref[1][:, None, :], shape).reshape(BLOCKS * LANE8, BLOCK)
    return cosine, sine


def forward(low, high, first_ref, second_ref, cosine, sine):
    rows = BLOCKS * LANE8
    signals = jnp.concatenate([low, high], 1).astype(bf16)
    part = jnp.dot(first_ref[...], signals, preferred_element_type=f32)
    turned = []
    for lanes in (slice(0, BLOCK), slice(BLOCK, 2 * BLOCK)):
        real, imag = part[:rows, lanes], part[rows:, lanes]
        turned.append(jnp.concatenate([real * cosine - imag * sine, real * sine + imag * cosine], 1))
    return jnp.dot(jnp.concatenate(turned, 0).astype(bf16), second_ref[...], preferred_element_type=f32)


def backward(spectra, back_second_ref, back_first_ref, cosine, sine):
    rows = BLOCKS * LANE8
    part = jnp.dot(spectra.astype(bf16), back_second_ref[...], preferred_element_type=f32)
    turned = []
    for start in (0, rows):
        real, imag = part[start : start + rows, :BLOCK], part[start : start + rows, BLOCK:]
        turned.append(jnp.concatenate([real * cosine + imag * sine, imag * cosine - real * sine], 0))
    return jnp.dot(back_first_ref[...], jnp.concatenate(turned, 1).astype(bf16), preferred_element_type=f32)


def filter_kernel(filter_ref, first_ref, second_ref, twist_ref, spectrum_ref):
    cosine, sine = twists_of(twist_ref)
    rows = BLOCKS * LANE8
    signals = []
    for start in (0, LANE8):
        pieces = [filter_ref[start : start + LANE8, i * BLOCK : (i + 1) * BLOCK] for i in range(BLOCKS)]
        signals.append(jnp.concatenate(pieces, 0))
    spectra = forward(*signals, first_ref, second_ref, cosine, sine)
    spectrum_ref[...] = spectra.astype(bf16).reshape(2, rows, 2 * BLOCK)


def start_all(copies):
    for copy in copies:
        copy.start()


def wait_all(copies):
    for copy in copies:
        copy.wait()


def weight_copies(weight_hbm, weight, sems):
    copies = []
    for slot in range(weight_hbm.shape[0]):
        lanes = pl.ds(slot % 2 * 2 * CHANS, 2 * CHANS)
        copies.append(pltpu.make_async_copy(weight_hbm.at[slot], weight.at[slot // 2, :, lanes], sems.at[slot]))
    return copies


def spread(rows, marks, count):
    trials, width = marks.shape
    marks = jnp.broadcast_to(marks[:, None, :], (trials, TRIAL, width)).reshape(trials * TRIAL, width).astype(bf16)
    nothing = jnp.zeros_like(rows)
    return jnp.concatenate([jnp.where(marks == number, rows, nothing) for number in range(count)], 1)


def project(rows_ref, start, blocks, weight):
    width = 2 * CHANS
    in_chans = rows_ref.shape[2]
    rows = rows_ref[pl.ds(start, blocks), :BLOCK, :].reshape(blocks * BLOCK, in_chans)
    marks = rows_ref[pl.ds(start, blocks), BLOCK:, :].astype(f32).reshape(blocks * BLOCK // TRIAL, in_chans)
    wide = spread(rows, jnp.floor(marks * 0.5), weight.shape[0])
    product = jnp.dot(wide, weight[...].reshape(-1, 2 * width), preferred_element_type=f32)
    odd = (marks - 2 * jnp.floor(marks * 0.5))[:, :width]
    trials = odd.shape[0]
    odd = jnp.broadcast_to(odd[:, None, :], (trials, TRIAL, width)).reshape(trials * TRIAL, width)
    chosen = jnp.where(odd > 0.5, product[:, width:], product[:, :width])
    return [chosen[i * BLOCK : (i + 1) * BLOCK].T.astype(bf16) for i in range(blocks)]


def block_of(place_ref, z_step, y_index):
    y_step = jnp.where(y_index < 2, Y - y_index, y_index - 1)
    return lax.rem(place_ref[0] + z_step, Z) * Y + lax.rem(place_ref[1] + y_step, Y)


def z_step_of(index):
    return jnp.where(index % 2 == 1, Z - (index + 1) // 2, index // 2)


def read_in_kernel(weight_hbm, *rest):
    chunk_hbms = rest[:-5]
    out_ref, rows, weight, weight_sems, sems = rest[-5:]
    loads = weight_copies(weight_hbm, weight, weight_sems)
    for index, chunk in enumerate(chunk_hbms):
        loads.append(pltpu.make_async_copy(chunk, rows.at[pl.ds(index * Y, Y)], sems.at[index]))
    start_all(loads)
    wait_all(loads)

    def step(index, carry):
        blocks = project(rows, index * Y, Y, weight)
        for y_index in range(Y):
            out_ref[index * Y + y_index] = blocks[y_index]
        return carry

    lax.fori_loop(0, len(chunk_hbms), step, 0)


def forward_kernel(place_ref, taps_ref, gain_ref, twist_ref, filter_hbm, *rest):
    early_hbms, table_hbms, rest = rest[:2], rest[2:6], rest[6:]
    gated_hbm, gate_hbm, spectrum_hbm, both, spectra, gated_all, spectrum_all, *rest = rest
    tables = rest[:4]
    early_sems, sems, store_sems = rest[4:]
    others = []
    for early_hbm in early_hbms:
        for index in range(early_hbm.shape[0]):
            number = len(others)
            target = both.at[block_of(place_ref, z_step_of(number // Y), number % Y)]
            others.append(pltpu.make_async_copy(early_hbm.at[index], target, early_sems.at[number]))
    pairs = [(filter_hbm, spectra)] + list(zip(table_hbms, tables))
    others += [pltpu.make_async_copy(source, target, sems.at[index]) for index, (source, target) in enumerate(pairs)]
    start_all(others)
    cosine, sine = twists_of(twist_ref)
    lane = lax.broadcasted_iota(jnp.int32, (BLOCKS, LANE8, BLOCK), 2)
    count = BLOCKS * LANE8
    cube = (BLOCKS, LANE8, BLOCK)
    wait_all(others)
    gate_store = pltpu.make_async_copy(both.at[:, pl.ds(CHANS, CHANS), :], gate_hbm, store_sems.at[0, GROUPS // 2])
    gate_store.start()
    first_ref, second_ref, back_second_ref, back_first_ref = tables

    def stores_of(pair):
        here = pl.ds(pl.multiple_of(pair * 2 * LANE8, 2 * LANE8), 2 * LANE8)
        groups = pl.ds(pair * 2, 2)
        return [
            pltpu.make_async_copy(gated_all.at[:, here, :], gated_hbm.at[:, here, :], store_sems.at[0, pair]),
            pltpu.make_async_copy(spectrum_all.at[groups], spectrum_hbm.at[groups], store_sems.at[1, pair]),
        ]

    def short(value, group):
        taps = taps_ref[:, pl.ds(pl.multiple_of(group * LANE8, LANE8), LANE8), :]
        total = taps[0][None] * value
        for shift in (1, 2):
            rolled = pltpu.roll(value.reshape(count, BLOCK), shift, 1).reshape(cube)
            before = jnp.concatenate([jnp.zeros((1, LANE8, BLOCK), f32), rolled[:-1]], 0)
            total = total + taps[shift][None] * jnp.where(lane < shift, before, rolled)
        return total.astype(bf16).astype(f32).reshape(count, BLOCK)

    def step(pair, carry):
        here = pl.ds(pl.multiple_of(pair * 2 * LANE8, 2 * LANE8), 2 * LANE8)
        there = pl.ds(pl.multiple_of(CHANS + pair * 2 * LANE8, 2 * LANE8), 2 * LANE8)
        value = both[:, here, :].astype(f32)
        gate = both[:, there, :]
        signals = [short(value[:, i * LANE8 : (i + 1) * LANE8], pair * 2 + i) for i in range(2)]
        own = forward(*signals, first_ref, second_ref, cosine, sine)
        spectrum_all[pl.ds(pair * 2, 2)] = own.reshape(2, count, 2 * BLOCK).astype(bf16)
        weight = spectra[pl.ds(pair * 2, 2)].reshape(2 * count, 2 * BLOCK).astype(f32)
        own_re, own_im = own[:, :BLOCK], own[:, BLOCK:]
        filter_re, filter_im = weight[:, :BLOCK], weight[:, BLOCK:]
        mix = jnp.concatenate([own_re * filter_re - own_im * filter_im, own_re * filter_im + own_im * filter_re], 1)
        result = backward(mix, back_second_ref, back_first_ref, cosine, sine)
        signal = jnp.concatenate([piece.reshape(cube) for piece in signals], 1)
        long_part = jnp.concatenate([result[:, i * BLOCK : (i + 1) * BLOCK].reshape(cube) for i in range(2)], 1)
        mixed = (long_part + gain_ref[here, :][None] * signal).astype(bf16).astype(f32)
        gated_all[:, here, :] = (gate.astype(f32) * mixed).astype(bf16)
        start_all(stores_of(pair))
        return carry

    lax.fori_loop(0, GROUPS // 2, step, 0, unroll=2)
    for pair in range(GROUPS // 2):
        wait_all(stores_of(pair))
    gate_store.wait()


def gradient_kernel(grad_ref, gate_ref, spectrum_ref, first_ref, second_ref, back_second_ref, back_first_ref, twist_ref, out_ref):
    cosine, sine = twists_of(twist_ref)
    count = BLOCKS * LANE8
    pair = 2 * LANE8
    for start in range(0, grad_ref.shape[1], pair):
        here = slice(start, start + pair)
        products = (grad_ref[:, here, :].astype(f32) * gate_ref[:, here, :].astype(f32)).astype(bf16).astype(f32)
        signals = [products[:, i * LANE8 : (i + 1) * LANE8].reshape(count, BLOCK) for i in range(2)]
        spectra = forward(*signals, first_ref, second_ref, cosine, sine)
        own = spectrum_ref[start // LANE8 : start // LANE8 + 2].reshape(2 * count, 2 * BLOCK).astype(f32)
        own_re, own_im = own[:, :BLOCK], own[:, BLOCK:]
        grad_re, grad_im = spectra[:, :BLOCK], spectra[:, BLOCK:]
        lag = jnp.concatenate([own_re * grad_re + own_im * grad_im, own_re * grad_im - own_im * grad_re], 1)
        result = backward(lag, back_second_ref, back_first_ref, cosine, sine)
        both = []
        for half in range(2):
            lanes = slice(half * BLOCK, (half + 1) * BLOCK)
            both.append(jnp.concatenate([result[i * LANE8 : (i + 1) * LANE8, lanes] for i in range(BLOCKS)], 1))
        out_ref[here, :] = jnp.concatenate(both, 0).astype(bf16)


def read_out_kernel(place_ref, rows_hbm, marks_hbm, weight_hbm, out_ref, weight, rows_all, chunk_all, weight_sems, sems):
    slots, inner, width = weight.shape
    trials = BLOCK // TRIAL
    first = [pltpu.make_async_copy(rows_hbm, rows_all, sems.at[0]), pltpu.make_async_copy(marks_hbm, chunk_all, sems.at[1])]
    loads = [pltpu.make_async_copy(weight_hbm.at[slot], weight.at[slot], weight_sems.at[slot]) for slot in range(slots)]
    start_all(first)
    start_all(loads)
    wait_all(first)
    places = [block_of(place_ref, 0, index) - place_ref[0] * Y for index in range(Y)]
    rows = jnp.concatenate([rows_all[:, block, :, :].reshape(inner, BLOCK).T for block in places], 0)
    marks = chunk_all[...].astype(f32).reshape(Y * trials, width)
    marks = jnp.broadcast_to(marks[:, None, :], (Y * trials, TRIAL, width)).reshape(Y * BLOCK, width)
    wait_all(loads)
    total = jnp.zeros((Y * BLOCK, width), f32)
    for slot in range(slots):
        product = jnp.dot(rows, weight[slot], preferred_element_type=f32)
        total = jnp.where(marks == slot, product, total)
    for index, block in enumerate(places):
        out_ref[block] = total[index * BLOCK : (index + 1) * BLOCK].astype(bf16)


def sum_kernel(parts_hbm, out_hbm, parts, total, in_sems, out_sems):
    count, rows, _ = parts.shape
    step = 2 * LANE8
    loads = []
    stores = []
    for index in range(rows // step):
        here = pl.ds(index * step, step)
        for part in range(count):
            load = pltpu.make_async_copy(parts_hbm.at[part, here, :], parts.at[part, here, :], in_sems.at[index, part])
            loads.append(load)
        stores.append(pltpu.make_async_copy(total.at[here, :], out_hbm.at[here, :], out_sems.at[index]))
    start_all(loads)
    for index in range(rows // step):
        wait_all(loads[index * count : (index + 1) * count])
        here = slice(index * step, (index + 1) * step)
        running = parts[0, here, :].astype(f32)
        for part in range(1, count):
            running = running + parts[part, here, :].astype(f32)
        total[here, :] = running
        stores[index].start()
    wait_all(stores)


def prepare_kernel(place_ref, session_ref, slot_ref, spikes_ref, weight_hbm, out_hbm, block_ref, own_ref, own_out_ref, value, gate, sems):
    place = place_ref[0]
    half = weight_hbm.shape[2] // 2
    window = pl.multiple_of(place // 2 * 2 * CHANS, 2 * CHANS)
    loads = [
        pltpu.make_async_copy(weight_hbm.at[:, :, pl.ds(window, 2 * CHANS)], value, sems.at[0]),
        pltpu.make_async_copy(weight_hbm.at[:, :, pl.ds(half + window, 2 * CHANS)], gate, sems.at[1]),
    ]
    start_all(loads)
    moved = pltpu.make_async_copy(out_hbm.at[:, :, lax.rem(place, Y)], own_out_ref, sems.at[2])
    moved.start()
    trials = BLOCK // TRIAL
    width = block_ref.shape[1]
    row = lax.broadcasted_iota(jnp.int32, (trials, width), 0)
    marks = jnp.zeros((trials, width), jnp.int32)
    for trial in range(trials):
        marks = jnp.where(row == trial, slot_ref[session_ref[0, trial * TRIAL]], marks)
    block_ref[:BLOCK, :] = spikes_ref[0]
    block_ref[BLOCK:, :] = marks.astype(f32).astype(bf16)
    wait_all(loads)
    slots, inner, lanes = own_ref.shape
    odd = place % 2
    low = pltpu.roll(value[...].astype(f32).reshape(slots * inner, lanes), odd * CHANS, 1)
    high = pltpu.roll(gate[...].astype(f32).reshape(slots * inner, lanes), (1 - odd) * CHANS, 1)
    lane = lax.broadcasted_iota(jnp.int32, (slots * inner, lanes), 1)
    own_ref[...] = jnp.where(lane < CHANS, low, high).astype(bf16).reshape(slots, inner, lanes)
    moved.wait()


def along_y(value, step):
    return lax.ppermute(value, "seq", [(z * Y + y, z * Y + (y + step) % Y) for z in range(Z) for y in range(Y)])


def along_z(value, step):
    return lax.ppermute(value, "seq", [(z * Y + y, (z + step) % Z * Y + y) for z in range(Z) for y in range(Y)])


def whole(count):
    return [pl.BlockSpec(memory_space=pltpu.VMEM)] * count


def local(spikes, session_of_bin, session_slot, readin_weight, short_kernel, long_filter, skip_gain, readout_weight, out_grad):
    in_chans = spikes.shape[2]
    place = lax.axis_index("seq")
    scalar = pl.BlockSpec(memory_space=pltpu.SMEM)
    hbm = pl.BlockSpec(memory_space=pltpu.HBM)
    z_groups = [[z * Y + y for z in range(Z)] for y in range(Y)]
    y_groups = [[z * Y + y for y in range(Y)] for z in range(Z)]
    coords = jnp.stack([place // Y, place % Y]).astype(jnp.int32)
    first, second, back_second, back_first, twists = transform_tables()
    params = pltpu.CompilerParams(vmem_limit_bytes=60 << 20)
    spectrum_shape = jax.ShapeDtypeStruct((GROUPS, BLOCKS * LANE8, 2 * BLOCK), bf16)
    plane = (BLOCKS, CHANS, BLOCK)
    work = 2 * GROUPS * (512 * 256 * 128 + 256 * 256 * 256)
    pair = 2 * LANE8
    same = lambda table: pl.BlockSpec(table.shape, lambda i, rank=table.ndim: (0,) * rank)

    own_shape = (2, in_chans, 2 * CHANS)
    out_split = readout_weight.reshape(2, Z, Y, CHANS, in_chans)
    block, own_weights, own_out = pl.pallas_call(
        prepare_kernel,
        out_shape=(
            jax.ShapeDtypeStruct((BLOCK + BLOCK // TRIAL, in_chans), bf16),
            jax.ShapeDtypeStruct(own_shape, bf16),
            jax.ShapeDtypeStruct((2, Z, CHANS, in_chans), bf16),
        ),
        in_specs=[scalar] * 3 + whole(1) + [hbm] * 2,
        out_specs=tuple(whole(3)),
        scratch_shapes=[pltpu.VMEM(own_shape, bf16), pltpu.VMEM(own_shape, bf16), pltpu.SemaphoreType.DMA((3,))],
        compiler_params=params,
        cost_estimate=pl.CostEstimate(flops=1 << 16, bytes_accessed=1 << 19, transcendentals=0),
        name="prepare",
    )(place.astype(jnp.int32)[None], session_of_bin, session_slot, spikes, readin_weight, out_split)
    chunk = jnp.stack([block, along_y(block, 1), along_y(block, -1), along_y(block, 2)])
    own_marks = chunk[:, BLOCK:, :]
    right, left = along_z(chunk, 1), along_z(chunk, -1)
    chunks = [chunk, right, left]

    in_weights = lax.all_gather(own_weights, "grp", axis=0, tiled=True)
    right, left, own_marks, own_out = lax.optimization_barrier((right, left, own_marks, own_out))
    split = own_out.reshape(2, Z * CHANS, in_chans)
    out_weights = lax.all_gather(split, "grp", axis=0, tiled=True)
    right, left = along_z(right, 1), along_z(left, -1)
    chunks += [right, left]
    turned = out_grad[0].T.reshape(BLOCKS, CHANS, BLOCK)
    taps = lax.dynamic_slice_in_dim(short_kernel, place * CHANS, CHANS, 1)
    taps = jnp.broadcast_to(taps[:, :, None], (short_kernel.shape[0], CHANS, BLOCK))
    gains = jnp.broadcast_to(skip_gain[:, None], (CHANS, BLOCK))
    ready = (right, left, taps, gains, coords, turned)
    right, left, taps, gains, coords, turned = lax.optimization_barrier(ready)
    right, left = along_z(right, 1), along_z(left, -1)
    slot_count = session_slot.shape[0]
    width = 2 * CHANS

    def read_in(pieces):
        blocks = len(pieces) * Y
        return pl.pallas_call(
            read_in_kernel,
            out_shape=jax.ShapeDtypeStruct((blocks, width, BLOCK), bf16),
            in_specs=[hbm] * (1 + len(pieces)),
            out_specs=whole(1)[0],
            scratch_shapes=[
                pltpu.VMEM((blocks,) + chunk.shape[1:], bf16),
                pltpu.VMEM((slot_count // 2, in_chans, 2 * width), bf16),
                pltpu.SemaphoreType.DMA((slot_count,)),
                pltpu.SemaphoreType.DMA((len(pieces),)),
            ],
            compiler_params=params,
            cost_estimate=pl.CostEstimate(flops=work, bytes_accessed=4 << 20, transcendentals=0),
            name="read_in",
        )(in_weights, *pieces)

    early = read_in(chunks)
    right, left, early, long_filter = lax.optimization_barrier((right, left, early, long_filter))
    last = along_z(right, 1)
    filter_spectrum = pl.pallas_call(
        filter_kernel,
        out_shape=spectrum_shape,
        grid=(GROUPS // 2,),
        in_specs=[pl.BlockSpec((pair, LENGTH), lambda i: (i, 0))] + [same(table) for table in (first, second, twists)],
        out_specs=pl.BlockSpec((2,) + spectrum_shape.shape[1:], lambda i: (i, 0, 0)),
        compiler_params=params,
        cost_estimate=pl.CostEstimate(flops=work, bytes_accessed=4 << 20, transcendentals=0),
        name="filter_transform",
    )(long_filter, first, second, twists)
    ready = (right, left, last, filter_spectrum, turned)
    right, left, last, filter_spectrum, turned = lax.optimization_barrier(ready)
    grads = lax.all_to_all(turned, "seq", split_axis=0, concat_axis=0, tiled=True)
    later = read_in([right, left, last])

    tables = (first, second, back_second, back_first)
    gated, gates, spectrum = pl.pallas_call(
        forward_kernel,
        out_shape=(
            jax.ShapeDtypeStruct(plane, bf16),
            jax.ShapeDtypeStruct(plane, bf16),
            spectrum_shape,
        ),
        in_specs=[scalar] + whole(3) + [hbm] * (3 + 4),
        out_specs=(hbm,) * 3,
        scratch_shapes=[
            pltpu.VMEM((BLOCKS, 2 * CHANS, BLOCK), bf16),
            pltpu.VMEM(spectrum_shape.shape, bf16),
            pltpu.VMEM(plane, bf16),
            pltpu.VMEM(spectrum_shape.shape, bf16),
        ]
        + [pltpu.VMEM(table.shape, bf16) for table in tables]
        + [pltpu.SemaphoreType.DMA((count,)) for count in (BLOCKS, 5)]
        + [pltpu.SemaphoreType.DMA((2, GROUPS // 2 + 1))],
        compiler_params=params,
        cost_estimate=pl.CostEstimate(flops=4 * work, bytes_accessed=8 << 20, transcendentals=0),
        name="long_convolution",
    )(coords, taps, gains, twists, filter_spectrum, early, later, *tables)

    gated = gated.reshape(Z, Y, CHANS, BLOCK)
    arrived = lax.all_to_all(gated, "seq", split_axis=0, concat_axis=0, tiled=True, axis_index_groups=z_groups)
    own_grad = pl.pallas_call(
        gradient_kernel,
        out_shape=jax.ShapeDtypeStruct((CHANS, LENGTH), bf16),
        grid=(GROUPS // 4,),
        in_specs=[pl.BlockSpec((BLOCKS, 2 * pair, BLOCK), lambda i: (0, i, 0))] * 2
        + [pl.BlockSpec((4,) + spectrum_shape.shape[1:], lambda i: (i, 0, 0))]
        + [same(table) for table in tables + (twists,)],
        out_specs=pl.BlockSpec((2 * pair, LENGTH), lambda i: (i, 0)),
        compiler_params=params,
        cost_estimate=pl.CostEstimate(flops=2 * work, bytes_accessed=4 << 20, transcendentals=0),
        name="filter_gradient",
    )(grads, gates, spectrum, *tables, twists)
    all_grads = lax.all_gather(own_grad, "grp", axis=0, tiled=False)
    devices = all_grads.shape[0]
    filter_grad = pl.pallas_call(
        sum_kernel,
        out_shape=jax.ShapeDtypeStruct((CHANS, LENGTH), f32),
        in_specs=[hbm],
        out_specs=hbm,
        scratch_shapes=[
            pltpu.VMEM(all_grads.shape, bf16),
            pltpu.VMEM((CHANS, LENGTH), f32),
            pltpu.SemaphoreType.DMA((CHANS // pair, devices)),
            pltpu.SemaphoreType.DMA((CHANS // pair,)),
        ],
        compiler_params=params,
        cost_estimate=pl.CostEstimate(flops=all_grads.size, bytes_accessed=5 << 20, transcendentals=0),
        name="sum_gradients",
    )(all_grads)
    partial = pl.pallas_call(
        read_out_kernel,
        out_shape=jax.ShapeDtypeStruct((Y, BLOCK, in_chans), bf16),
        in_specs=[scalar] + [hbm] * 3,
        out_specs=whole(1)[0],
        scratch_shapes=[
            pltpu.VMEM(out_weights.shape, bf16),
            pltpu.VMEM((Z, Y, CHANS, BLOCK), bf16),
            pltpu.VMEM((Y, BLOCK // TRIAL, in_chans), bf16),
        ]
        + [pltpu.SemaphoreType.DMA((count,)) for count in (slot_count, 2)],
        compiler_params=params,
        cost_estimate=pl.CostEstimate(flops=2 * 512 * 512 * 4096, bytes_accessed=6 << 20, transcendentals=0),
        name="read_out",
    )(coords, arrived, own_marks, out_weights)
    pieces = lax.all_to_all(partial, "seq", split_axis=0, concat_axis=0, tiled=True, axis_index_groups=y_groups)
    denoised = jnp.sum(pieces.astype(f32), 0).astype(bf16)
    return denoised[None], filter_grad


def solution(mesh):
    placed = (
        P("grp", "seq", None),
        P("grp", "seq"),
        P(),
        P("grp", None, None),
        P(),
        P("seq", None),
        P("seq"),
        P("grp", None, None),
        P("grp", "seq", None),
    )
    return jax.shard_map(
        local,
        mesh=mesh,
        in_specs=placed,
        out_specs=(P("grp", "seq", None), P("seq", None)),
        check_vma=False,
    )
```

```python
import jax
import jax.numpy as jnp
import numpy as np
from jax import lax
from jax.experimental import pallas as pl
from jax.experimental.pallas import tpu as pltpu
from jax.sharding import PartitionSpec as P

BLOCK = 128
TRIAL = 16
Z = 8
Y = 4
BLOCKS = Z * Y
CHANS = 64
LANE8 = 8
GROUPS = CHANS // LANE8
LENGTH = BLOCKS * BLOCK
f32 = jnp.float32
bf16 = jnp.bfloat16


def transform_tables():
    slow = np.arange(BLOCKS)
    fast = np.arange(BLOCK)
    first = np.exp(-2j * np.pi * (np.outer(slow, slow) / BLOCKS + slow[None, :] / (4.0 * BLOCKS)))
    twist = np.exp(-2j * np.pi * (slow[:, None] + 0.25) * fast[None, :] / LENGTH)
    second = np.exp(-2j * np.pi * np.outer(fast, fast) / BLOCK)
    eye = np.eye(LANE8)
    spread_first = np.concatenate([np.kron(first.real, eye), np.kron(first.imag, eye)], 0)
    forward_second = np.block([[second.real, second.imag], [-second.imag, second.real]])
    back = second.conj()
    back_second = np.block([[back.real, back.imag], [-back.imag, back.real]])
    back_first = first.conj().T / LENGTH
    spread_back = np.concatenate([np.kron(back_first.real, eye), np.kron(-back_first.imag, eye)], 1)
    as_bf16 = lambda table: jnp.asarray(table.astype(np.float32), bf16)
    twists = np.stack([twist.real, twist.imag]).astype(np.float32)
    return (
        as_bf16(spread_first),
        as_bf16(forward_second),
        as_bf16(back_second),
        as_bf16(spread_back),
        jnp.asarray(twists),
    )


def twists_of(twist_ref):
    shape = (BLOCKS, LANE8, BLOCK)
    cosine = jnp.broadcast_to(twist_ref[0][:, None, :], shape).reshape(BLOCKS * LANE8, BLOCK)
    sine = jnp.broadcast_to(twist_ref[1][:, None, :], shape).reshape(BLOCKS * LANE8, BLOCK)
    return cosine, sine


def forward(low, high, first_ref, second_ref, cosine, sine):
    rows = BLOCKS * LANE8
    signals = jnp.concatenate([low, high], 1).astype(bf16)
    part = jnp.dot(first_ref[...], signals, preferred_element_type=f32)
    turned = []
    for lanes in (slice(0, BLOCK), slice(BLOCK, 2 * BLOCK)):
        real, imag = part[:rows, lanes], part[rows:, lanes]
        turned.append(jnp.concatenate([real * cosine - imag * sine, real * sine + imag * cosine], 1))
    return jnp.dot(jnp.concatenate(turned, 0).astype(bf16), second_ref[...], preferred_element_type=f32)


def backward(spectra, back_second_ref, back_first_ref, cosine, sine):
    rows = BLOCKS * LANE8
    part = jnp.dot(spectra.astype(bf16), back_second_ref[...], preferred_element_type=f32)
    turned = []
    for start in (0, rows):
        real, imag = part[start : start + rows, :BLOCK], part[start : start + rows, BLOCK:]
        turned.append(jnp.concatenate([real * cosine + imag * sine, imag * cosine - real * sine], 0))
    return jnp.dot(back_first_ref[...], jnp.concatenate(turned, 1).astype(bf16), preferred_element_type=f32)


def filter_kernel(filter_ref, first_ref, second_ref, twist_ref, spectrum_ref):
    cosine, sine = twists_of(twist_ref)
    rows = BLOCKS * LANE8
    signals = []
    for start in (0, LANE8):
        pieces = [filter_ref[start : start + LANE8, i * BLOCK : (i + 1) * BLOCK] for i in range(BLOCKS)]
        signals.append(jnp.concatenate(pieces, 0))
    spectra = forward(*signals, first_ref, second_ref, cosine, sine)
    spectrum_ref[...] = spectra.astype(bf16).reshape(2, rows, 2 * BLOCK)


def start_all(copies):
    for copy in copies:
        copy.start()


def wait_all(copies):
    for copy in copies:
        copy.wait()


def weight_copies(weight_hbm, weight, sems):
    copies = []
    for slot in range(weight_hbm.shape[0]):
        lanes = pl.ds(slot % 2 * 2 * CHANS, 2 * CHANS)
        copies.append(pltpu.make_async_copy(weight_hbm.at[slot], weight.at[slot // 2, :, lanes], sems.at[slot]))
    return copies


def spread(rows, marks, count):
    trials, width = marks.shape
    marks = jnp.broadcast_to(marks[:, None, :], (trials, TRIAL, width)).reshape(trials * TRIAL, width).astype(bf16)
    nothing = jnp.zeros_like(rows)
    return jnp.concatenate([jnp.where(marks == number, rows, nothing) for number in range(count)], 1)


def project(rows_ref, start, blocks, weight):
    width = 2 * CHANS
    in_chans = rows_ref.shape[2]
    rows = rows_ref[pl.ds(start, blocks), :BLOCK, :].reshape(blocks * BLOCK, in_chans)
    marks = rows_ref[pl.ds(start, blocks), BLOCK:, :].astype(f32).reshape(blocks * BLOCK // TRIAL, in_chans)
    wide = spread(rows, jnp.floor(marks * 0.5), weight.shape[0])
    product = jnp.dot(wide, weight[...].reshape(-1, 2 * width), preferred_element_type=f32)
    odd = (marks - 2 * jnp.floor(marks * 0.5))[:, :width]
    trials = odd.shape[0]
    odd = jnp.broadcast_to(odd[:, None, :], (trials, TRIAL, width)).reshape(trials * TRIAL, width)
    chosen = jnp.where(odd > 0.5, product[:, width:], product[:, :width])
    return [chosen[i * BLOCK : (i + 1) * BLOCK].T.astype(bf16) for i in range(blocks)]


def block_of(place_ref, z_step, y_index):
    y_step = jnp.where(y_index < 2, Y - y_index, y_index - 1)
    return lax.rem(place_ref[0] + z_step, Z) * Y + lax.rem(place_ref[1] + y_step, Y)


def z_step_of(index):
    return jnp.where(index % 2 == 1, Z - (index + 1) // 2, index // 2)


def read_in_kernel(weight_hbm, *rest):
    chunk_hbms = rest[:-5]
    out_ref, rows, weight, weight_sems, sems = rest[-5:]
    loads = weight_copies(weight_hbm, weight, weight_sems)
    for index, chunk in enumerate(chunk_hbms):
        loads.append(pltpu.make_async_copy(chunk, rows.at[pl.ds(index * Y, Y)], sems.at[index]))
    start_all(loads)
    wait_all(loads)

    def step(index, carry):
        blocks = project(rows, index * Y, Y, weight)
        for y_index in range(Y):
            out_ref[index * Y + y_index] = blocks[y_index]
        return carry

    lax.fori_loop(0, len(chunk_hbms), step, 0)


def forward_kernel(place_ref, taps_ref, gain_ref, twist_ref, filter_hbm, *rest):
    early_hbms, table_hbms, rest = rest[:3], rest[3:7], rest[7:]
    gated_hbm, gate_hbm, spectrum_hbm, both, spectra, gated_all, spectrum_all, *rest = rest
    tables = rest[:4]
    early_sems, sems, store_sems = rest[4:]
    others = []
    for early_hbm in early_hbms:
        for index in range(early_hbm.shape[0]):
            number = len(others)
            target = both.at[block_of(place_ref, z_step_of(number // Y), number % Y)]
            others.append(pltpu.make_async_copy(early_hbm.at[index], target, early_sems.at[number]))
    pairs = [(filter_hbm, spectra)] + list(zip(table_hbms, tables))
    others += [pltpu.make_async_copy(source, target, sems.at[index]) for index, (source, target) in enumerate(pairs)]
    start_all(others)
    cosine, sine = twists_of(twist_ref)
    lane = lax.broadcasted_iota(jnp.int32, (BLOCKS, LANE8, BLOCK), 2)
    count = BLOCKS * LANE8
    cube = (BLOCKS, LANE8, BLOCK)
    wait_all(others)
    gate_store = pltpu.make_async_copy(both.at[:, pl.ds(CHANS, CHANS), :], gate_hbm, store_sems.at[0, GROUPS // 2])
    gate_store.start()
    first_ref, second_ref, back_second_ref, back_first_ref = tables

    def stores_of(pair):
        here = pl.ds(pl.multiple_of(pair * 2 * LANE8, 2 * LANE8), 2 * LANE8)
        groups = pl.ds(pair * 2, 2)
        return [
            pltpu.make_async_copy(gated_all.at[:, here, :], gated_hbm.at[:, here, :], store_sems.at[0, pair]),
            pltpu.make_async_copy(spectrum_all.at[groups], spectrum_hbm.at[groups], store_sems.at[1, pair]),
        ]

    def short(value, group):
        taps = taps_ref[:, pl.ds(pl.multiple_of(group * LANE8, LANE8), LANE8), :]
        total = taps[0][None] * value
        for shift in (1, 2):
            rolled = pltpu.roll(value.reshape(count, BLOCK), shift, 1).reshape(cube)
            before = jnp.concatenate([jnp.zeros((1, LANE8, BLOCK), f32), rolled[:-1]], 0)
            total = total + taps[shift][None] * jnp.where(lane < shift, before, rolled)
        return total.astype(bf16).astype(f32).reshape(count, BLOCK)

    def step(pair, carry):
        here = pl.ds(pl.multiple_of(pair * 2 * LANE8, 2 * LANE8), 2 * LANE8)
        there = pl.ds(pl.multiple_of(CHANS + pair * 2 * LANE8, 2 * LANE8), 2 * LANE8)
        value = both[:, here, :].astype(f32)
        gate = both[:, there, :]
        signals = [short(value[:, i * LANE8 : (i + 1) * LANE8], pair * 2 + i) for i in range(2)]
        own = forward(*signals, first_ref, second_ref, cosine, sine)
        spectrum_all[pl.ds(pair * 2, 2)] = own.reshape(2, count, 2 * BLOCK).astype(bf16)
        weight = spectra[pl.ds(pair * 2, 2)].reshape(2 * count, 2 * BLOCK).astype(f32)
        own_re, own_im = own[:, :BLOCK], own[:, BLOCK:]
        filter_re, filter_im = weight[:, :BLOCK], weight[:, BLOCK:]
        mix = jnp.concatenate([own_re * filter_re - own_im * filter_im, own_re * filter_im + own_im * filter_re], 1)
        result = backward(mix, back_second_ref, back_first_ref, cosine, sine)
        signal = jnp.concatenate([piece.reshape(cube) for piece in signals], 1)
        long_part = jnp.concatenate([result[:, i * BLOCK : (i + 1) * BLOCK].reshape(cube) for i in range(2)], 1)
        mixed = (long_part + gain_ref[here, :][None] * signal).astype(bf16).astype(f32)
        gated_all[:, here, :] = (gate.astype(f32) * mixed).astype(bf16)
        start_all(stores_of(pair))
        return carry

    lax.fori_loop(0, GROUPS // 2, step, 0, unroll=2)
    for pair in range(GROUPS // 2):
        wait_all(stores_of(pair))
    gate_store.wait()


def gradient_kernel(grad_ref, gate_ref, spectrum_ref, first_ref, second_ref, back_second_ref, back_first_ref, twist_ref, out_ref):
    cosine, sine = twists_of(twist_ref)
    count = BLOCKS * LANE8
    pair = 2 * LANE8
    for start in range(0, grad_ref.shape[1], pair):
        here = slice(start, start + pair)
        products = (grad_ref[:, here, :].astype(f32) * gate_ref[:, here, :].astype(f32)).astype(bf16).astype(f32)
        signals = [products[:, i * LANE8 : (i + 1) * LANE8].reshape(count, BLOCK) for i in range(2)]
        spectra = forward(*signals, first_ref, second_ref, cosine, sine)
        own = spectrum_ref[start // LANE8 : start // LANE8 + 2].reshape(2 * count, 2 * BLOCK).astype(f32)
        own_re, own_im = own[:, :BLOCK], own[:, BLOCK:]
        grad_re, grad_im = spectra[:, :BLOCK], spectra[:, BLOCK:]
        lag = jnp.concatenate([own_re * grad_re + own_im * grad_im, own_re * grad_im - own_im * grad_re], 1)
        result = backward(lag, back_second_ref, back_first_ref, cosine, sine)
        both = []
        for half in range(2):
            lanes = slice(half * BLOCK, (half + 1) * BLOCK)
            both.append(jnp.concatenate([result[i * LANE8 : (i + 1) * LANE8, lanes] for i in range(BLOCKS)], 1))
        out_ref[here, :] = jnp.concatenate(both, 0).astype(bf16)


def read_out_kernel(place_ref, rows_hbm, marks_hbm, weight_hbm, out_ref, weight, rows_all, chunk_all, weight_sems, sems):
    slots, inner, width = weight.shape
    trials = BLOCK // TRIAL
    first = [pltpu.make_async_copy(rows_hbm, rows_all, sems.at[0]), pltpu.make_async_copy(marks_hbm, chunk_all, sems.at[1])]
    loads = [pltpu.make_async_copy(weight_hbm.at[slot], weight.at[slot], weight_sems.at[slot]) for slot in range(slots)]
    start_all(first)
    start_all(loads)
    wait_all(first)
    places = [block_of(place_ref, 0, index) - place_ref[0] * Y for index in range(Y)]
    rows = jnp.concatenate([rows_all[:, block, :, :].reshape(inner, BLOCK).T for block in places], 0)
    marks = chunk_all[...].astype(f32).reshape(Y * trials, width)
    marks = jnp.broadcast_to(marks[:, None, :], (Y * trials, TRIAL, width)).reshape(Y * BLOCK, width)
    wait_all(loads)
    total = jnp.zeros((Y * BLOCK, width), f32)
    for slot in range(slots):
        product = jnp.dot(rows, weight[slot], preferred_element_type=f32)
        total = jnp.where(marks == slot, product, total)
    for index, block in enumerate(places):
        out_ref[block] = total[index * BLOCK : (index + 1) * BLOCK].astype(bf16)


def sum_kernel(parts_hbm, out_hbm, parts, total, in_sems, out_sems):
    count, rows, _ = parts.shape
    step = 2 * LANE8
    loads = []
    stores = []
    for index in range(rows // step):
        here = pl.ds(index * step, step)
        for part in range(count):
            load = pltpu.make_async_copy(parts_hbm.at[part, here, :], parts.at[part, here, :], in_sems.at[index, part])
            loads.append(load)
        stores.append(pltpu.make_async_copy(total.at[here, :], out_hbm.at[here, :], out_sems.at[index]))
    start_all(loads)
    for index in range(rows // step):
        wait_all(loads[index * count : (index + 1) * count])
        here = slice(index * step, (index + 1) * step)
        running = parts[0, here, :].astype(f32)
        for part in range(1, count):
            running = running + parts[part, here, :].astype(f32)
        total[here, :] = running
        stores[index].start()
    wait_all(stores)


def prepare_kernel(place_ref, session_ref, slot_ref, spikes_ref, weight_hbm, out_hbm, block_ref, own_ref, own_out_ref, value, gate, sems):
    place = place_ref[0]
    half = weight_hbm.shape[2] // 2
    window = pl.multiple_of(place // 2 * 2 * CHANS, 2 * CHANS)
    loads = [
        pltpu.make_async_copy(weight_hbm.at[:, :, pl.ds(window, 2 * CHANS)], value, sems.at[0]),
        pltpu.make_async_copy(weight_hbm.at[:, :, pl.ds(half + window, 2 * CHANS)], gate, sems.at[1]),
    ]
    start_all(loads)
    moved = pltpu.make_async_copy(out_hbm.at[:, :, lax.rem(place, Y)], own_out_ref, sems.at[2])
    moved.start()
    trials = BLOCK // TRIAL
    width = block_ref.shape[1]
    row = lax.broadcasted_iota(jnp.int32, (trials, width), 0)
    marks = jnp.zeros((trials, width), jnp.int32)
    for trial in range(trials):
        marks = jnp.where(row == trial, slot_ref[session_ref[0, trial * TRIAL]], marks)
    block_ref[:BLOCK, :] = spikes_ref[0]
    block_ref[BLOCK:, :] = marks.astype(f32).astype(bf16)
    wait_all(loads)
    slots, inner, lanes = own_ref.shape
    odd = place % 2
    low = pltpu.roll(value[...].astype(f32).reshape(slots * inner, lanes), odd * CHANS, 1)
    high = pltpu.roll(gate[...].astype(f32).reshape(slots * inner, lanes), (1 - odd) * CHANS, 1)
    lane = lax.broadcasted_iota(jnp.int32, (slots * inner, lanes), 1)
    own_ref[...] = jnp.where(lane < CHANS, low, high).astype(bf16).reshape(slots, inner, lanes)
    moved.wait()


def along_y(value, step):
    return lax.ppermute(value, "seq", [(z * Y + y, z * Y + (y + step) % Y) for z in range(Z) for y in range(Y)])


def along_z(value, step):
    return lax.ppermute(value, "seq", [(z * Y + y, (z + step) % Z * Y + y) for z in range(Z) for y in range(Y)])


def whole(count):
    return [pl.BlockSpec(memory_space=pltpu.VMEM)] * count


def local(spikes, session_of_bin, session_slot, readin_weight, short_kernel, long_filter, skip_gain, readout_weight, out_grad):
    in_chans = spikes.shape[2]
    place = lax.axis_index("seq")
    scalar = pl.BlockSpec(memory_space=pltpu.SMEM)
    hbm = pl.BlockSpec(memory_space=pltpu.HBM)
    z_groups = [[z * Y + y for z in range(Z)] for y in range(Y)]
    y_groups = [[z * Y + y for y in range(Y)] for z in range(Z)]
    coords = jnp.stack([place // Y, place % Y]).astype(jnp.int32)
    first, second, back_second, back_first, twists = transform_tables()
    params = pltpu.CompilerParams(vmem_limit_bytes=60 << 20)
    spectrum_shape = jax.ShapeDtypeStruct((GROUPS, BLOCKS * LANE8, 2 * BLOCK), bf16)
    plane = (BLOCKS, CHANS, BLOCK)
    work = 2 * GROUPS * (512 * 256 * 128 + 256 * 256 * 256)
    pair = 2 * LANE8
    same = lambda table: pl.BlockSpec(table.shape, lambda i, rank=table.ndim: (0,) * rank)

    own_shape = (2, in_chans, 2 * CHANS)
    out_split = readout_weight.reshape(2, Z, Y, CHANS, in_chans)
    block, own_weights, own_out = pl.pallas_call(
        prepare_kernel,
        out_shape=(
            jax.ShapeDtypeStruct((BLOCK + BLOCK // TRIAL, in_chans), bf16),
            jax.ShapeDtypeStruct(own_shape, bf16),
            jax.ShapeDtypeStruct((2, Z, CHANS, in_chans), bf16),
        ),
        in_specs=[scalar] * 3 + whole(1) + [hbm] * 2,
        out_specs=tuple(whole(3)),
        scratch_shapes=[pltpu.VMEM(own_shape, bf16), pltpu.VMEM(own_shape, bf16), pltpu.SemaphoreType.DMA((3,))],
        compiler_params=params,
        cost_estimate=pl.CostEstimate(flops=1 << 16, bytes_accessed=1 << 19, transcendentals=0),
        name="prepare",
    )(place.astype(jnp.int32)[None], session_of_bin, session_slot, spikes, readin_weight, out_split)
    chunk = jnp.stack([block, along_y(block, 1), along_y(block, -1), along_y(block, 2)])
    own_marks = chunk[:, BLOCK:, :]
    right, left = along_z(chunk, 1), along_z(chunk, -1)
    chunks = [chunk, right, left]

    in_weights = lax.all_gather(own_weights, "grp", axis=0, tiled=True)
    filter_spectrum = pl.pallas_call(
        filter_kernel,
        out_shape=spectrum_shape,
        grid=(GROUPS // 2,),
        in_specs=[pl.BlockSpec((pair, LENGTH), lambda i: (i, 0))] + [same(table) for table in (first, second, twists)],
        out_specs=pl.BlockSpec((2,) + spectrum_shape.shape[1:], lambda i: (i, 0, 0)),
        compiler_params=params,
        cost_estimate=pl.CostEstimate(flops=work, bytes_accessed=4 << 20, transcendentals=0),
        name="filter_transform",
    )(long_filter, first, second, twists)
    ready = (right, left, own_marks, own_out, filter_spectrum)
    right, left, own_marks, own_out, filter_spectrum = lax.optimization_barrier(ready)
    split = own_out.reshape(2, Z * CHANS, in_chans)
    out_weights = lax.all_gather(split, "grp", axis=0, tiled=True)
    right, left = along_z(right, 1), along_z(left, -1)
    chunks += [right, left]
    turned = out_grad[0].T.reshape(BLOCKS, CHANS, BLOCK)
    taps = lax.dynamic_slice_in_dim(short_kernel, place * CHANS, CHANS, 1)
    taps = jnp.broadcast_to(taps[:, :, None], (short_kernel.shape[0], CHANS, BLOCK))
    gains = jnp.broadcast_to(skip_gain[:, None], (CHANS, BLOCK))
    ready = (right, left, taps, gains, coords, turned)
    right, left, taps, gains, coords, turned = lax.optimization_barrier(ready)
    right, left = along_z(right, 1), along_z(left, -1)
    slot_count = session_slot.shape[0]
    width = 2 * CHANS

    def read_in(pieces):
        blocks = len(pieces) * Y
        return pl.pallas_call(
            read_in_kernel,
            out_shape=jax.ShapeDtypeStruct((blocks, width, BLOCK), bf16),
            in_specs=[hbm] * (1 + len(pieces)),
            out_specs=whole(1)[0],
            scratch_shapes=[
                pltpu.VMEM((blocks,) + chunk.shape[1:], bf16),
                pltpu.VMEM((slot_count // 2, in_chans, 2 * width), bf16),
                pltpu.SemaphoreType.DMA((slot_count,)),
                pltpu.SemaphoreType.DMA((len(pieces),)),
            ],
            compiler_params=params,
            cost_estimate=pl.CostEstimate(flops=work, bytes_accessed=4 << 20, transcendentals=0),
            name="read_in",
        )(in_weights, *pieces)

    early = read_in(chunks[:3])
    right, left, early, *chunks = lax.optimization_barrier((right, left, early, *chunks))
    last = along_z(right, 1)
    middle = read_in(chunks[3:])
    right, left, last, middle, turned = lax.optimization_barrier((right, left, last, middle, turned))
    grads = lax.all_to_all(turned, "seq", split_axis=0, concat_axis=0, tiled=True)
    later = read_in([right, left, last])

    tables = (first, second, back_second, back_first)
    gated, gates, spectrum = pl.pallas_call(
        forward_kernel,
        out_shape=(
            jax.ShapeDtypeStruct(plane, bf16),
            jax.ShapeDtypeStruct(plane, bf16),
            spectrum_shape,
        ),
        in_specs=[scalar] + whole(3) + [hbm] * (4 + 4),
        out_specs=(hbm,) * 3,
        scratch_shapes=[
            pltpu.VMEM((BLOCKS, 2 * CHANS, BLOCK), bf16),
            pltpu.VMEM(spectrum_shape.shape, bf16),
            pltpu.VMEM(plane, bf16),
            pltpu.VMEM(spectrum_shape.shape, bf16),
        ]
        + [pltpu.VMEM(table.shape, bf16) for table in tables]
        + [pltpu.SemaphoreType.DMA((count,)) for count in (BLOCKS, 5)]
        + [pltpu.SemaphoreType.DMA((2, GROUPS // 2 + 1))],
        compiler_params=params,
        cost_estimate=pl.CostEstimate(flops=4 * work, bytes_accessed=8 << 20, transcendentals=0),
        name="long_convolution",
    )(coords, taps, gains, twists, filter_spectrum, early, middle, later, *tables)

    gated = gated.reshape(Z, Y, CHANS, BLOCK)
    arrived = lax.all_to_all(gated, "seq", split_axis=0, concat_axis=0, tiled=True, axis_index_groups=z_groups)
    own_grad = pl.pallas_call(
        gradient_kernel,
        out_shape=jax.ShapeDtypeStruct((CHANS, LENGTH), bf16),
        grid=(GROUPS // 4,),
        in_specs=[pl.BlockSpec((BLOCKS, 2 * pair, BLOCK), lambda i: (0, i, 0))] * 2
        + [pl.BlockSpec((4,) + spectrum_shape.shape[1:], lambda i: (i, 0, 0))]
        + [same(table) for table in tables + (twists,)],
        out_specs=pl.BlockSpec((2 * pair, LENGTH), lambda i: (i, 0)),
        compiler_params=params,
        cost_estimate=pl.CostEstimate(flops=2 * work, bytes_accessed=4 << 20, transcendentals=0),
        name="filter_gradient",
    )(grads, gates, spectrum, *tables, twists)
    all_grads = lax.all_gather(own_grad, "grp", axis=0, tiled=False)
    devices = all_grads.shape[0]
    filter_grad = pl.pallas_call(
        sum_kernel,
        out_shape=jax.ShapeDtypeStruct((CHANS, LENGTH), f32),
        in_specs=[hbm],
        out_specs=hbm,
        scratch_shapes=[
            pltpu.VMEM(all_grads.shape, bf16),
            pltpu.VMEM((CHANS, LENGTH), f32),
            pltpu.SemaphoreType.DMA((CHANS // pair, devices)),
            pltpu.SemaphoreType.DMA((CHANS // pair,)),
        ],
        compiler_params=params,
        cost_estimate=pl.CostEstimate(flops=all_grads.size, bytes_accessed=5 << 20, transcendentals=0),
        name="sum_gradients",
    )(all_grads)
    partial = pl.pallas_call(
        read_out_kernel,
        out_shape=jax.ShapeDtypeStruct((Y, BLOCK, in_chans), bf16),
        in_specs=[scalar] + [hbm] * 3,
        out_specs=whole(1)[0],
        scratch_shapes=[
            pltpu.VMEM(out_weights.shape, bf16),
            pltpu.VMEM((Z, Y, CHANS, BLOCK), bf16),
            pltpu.VMEM((Y, BLOCK // TRIAL, in_chans), bf16),
        ]
        + [pltpu.SemaphoreType.DMA((count,)) for count in (slot_count, 2)],
        compiler_params=params,
        cost_estimate=pl.CostEstimate(flops=2 * 512 * 512 * 4096, bytes_accessed=6 << 20, transcendentals=0),
        name="read_out",
    )(coords, arrived, own_marks, out_weights)
    pieces = lax.all_to_all(partial, "seq", split_axis=0, concat_axis=0, tiled=True, axis_index_groups=y_groups)
    denoised = jnp.sum(pieces.astype(f32), 0).astype(bf16)
    return denoised[None], filter_grad


def solution(mesh):
    placed = (
        P("grp", "seq", None),
        P("grp", "seq"),
        P(),
        P("grp", None, None),
        P(),
        P("seq", None),
        P("seq"),
        P("grp", None, None),
        P("grp", "seq", None),
    )
    return jax.shard_map(
        local,
        mesh=mesh,
        in_specs=placed,
        out_specs=(P("grp", "seq", None), P("seq", None)),
        check_vma=False,
    )
```

```python
import jax
import jax.numpy as jnp
import numpy as np
from jax import lax
from jax.experimental import pallas as pl
from jax.experimental.pallas import tpu as pltpu
from jax.sharding import PartitionSpec as P

BLOCK = 128
TRIAL = 16
Z = 8
Y = 4
BLOCKS = Z * Y
CHANS = 64
LANE8 = 8
GROUPS = CHANS // LANE8
LENGTH = BLOCKS * BLOCK
f32 = jnp.float32
bf16 = jnp.bfloat16


def transform_tables():
    slow = np.arange(BLOCKS)
    fast = np.arange(BLOCK)
    first = np.exp(-2j * np.pi * (np.outer(slow, slow) / BLOCKS + slow[None, :] / (4.0 * BLOCKS)))
    twist = np.exp(-2j * np.pi * (slow[:, None] + 0.25) * fast[None, :] / LENGTH)
    second = np.exp(-2j * np.pi * np.outer(fast, fast) / BLOCK)
    eye = np.eye(LANE8)
    spread_first = np.concatenate([np.kron(first.real, eye), np.kron(first.imag, eye)], 0)
    forward_second = np.block([[second.real, second.imag], [-second.imag, second.real]])
    back = second.conj()
    back_second = np.block([[back.real, back.imag], [-back.imag, back.real]])
    back_first = first.conj().T / LENGTH
    spread_back = np.concatenate([np.kron(back_first.real, eye), np.kron(-back_first.imag, eye)], 1)
    as_bf16 = lambda table: jnp.asarray(table.astype(np.float32), bf16)
    twists = np.stack([twist.real, twist.imag]).astype(np.float32)
    return (
        as_bf16(spread_first),
        as_bf16(forward_second),
        as_bf16(back_second),
        as_bf16(spread_back),
        jnp.asarray(twists),
    )


def twists_of(twist_ref):
    shape = (BLOCKS, LANE8, BLOCK)
    cosine = jnp.broadcast_to(twist_ref[0][:, None, :], shape).reshape(BLOCKS * LANE8, BLOCK)
    sine = jnp.broadcast_to(twist_ref[1][:, None, :], shape).reshape(BLOCKS * LANE8, BLOCK)
    return cosine, sine


def forward(low, high, first_ref, second_ref, cosine, sine):
    rows = BLOCKS * LANE8
    signals = jnp.concatenate([low, high], 1).astype(bf16)
    part = jnp.dot(first_ref[...], signals, preferred_element_type=f32)
    turned = []
    for lanes in (slice(0, BLOCK), slice(BLOCK, 2 * BLOCK)):
        real, imag = part[:rows, lanes], part[rows:, lanes]
        turned.append(jnp.concatenate([real * cosine - imag * sine, real * sine + imag * cosine], 1))
    return jnp.dot(jnp.concatenate(turned, 0).astype(bf16), second_ref[...], preferred_element_type=f32)


def backward(spectra, back_second_ref, back_first_ref, cosine, sine):
    rows = BLOCKS * LANE8
    part = jnp.dot(spectra.astype(bf16), back_second_ref[...], preferred_element_type=f32)
    turned = []
    for start in (0, rows):
        real, imag = part[start : start + rows, :BLOCK], part[start : start + rows, BLOCK:]
        turned.append(jnp.concatenate([real * cosine + imag * sine, imag * cosine - real * sine], 0))
    return jnp.dot(back_first_ref[...], jnp.concatenate(turned, 1).astype(bf16), preferred_element_type=f32)


def filter_kernel(filter_ref, first_ref, second_ref, twist_ref, spectrum_ref):
    cosine, sine = twists_of(twist_ref)
    rows = BLOCKS * LANE8
    signals = []
    for start in (0, LANE8):
        pieces = [filter_ref[start : start + LANE8, i * BLOCK : (i + 1) * BLOCK] for i in range(BLOCKS)]
        signals.append(jnp.concatenate(pieces, 0))
    spectra = forward(*signals, first_ref, second_ref, cosine, sine)
    spectrum_ref[...] = spectra.astype(bf16).reshape(2, rows, 2 * BLOCK)


def start_all(copies):
    for copy in copies:
        copy.start()


def wait_all(copies):
    for copy in copies:
        copy.wait()


def weight_copies(weight_hbm, weight, sems):
    copies = []
    for slot in range(weight_hbm.shape[0]):
        lanes = pl.ds(slot % 2 * 2 * CHANS, 2 * CHANS)
        copies.append(pltpu.make_async_copy(weight_hbm.at[slot], weight.at[slot // 2, :, lanes], sems.at[slot]))
    return copies


def spread(rows, marks, count):
    trials, width = marks.shape
    marks = jnp.broadcast_to(marks[:, None, :], (trials, TRIAL, width)).reshape(trials * TRIAL, width).astype(bf16)
    nothing = jnp.zeros_like(rows)
    return jnp.concatenate([jnp.where(marks == number, rows, nothing) for number in range(count)], 1)


def project(rows_ref, start, blocks, weight):
    width = 2 * CHANS
    in_chans = rows_ref.shape[2]
    rows = rows_ref[pl.ds(start, blocks), :BLOCK, :].reshape(blocks * BLOCK, in_chans)
    marks = rows_ref[pl.ds(start, blocks), BLOCK:, :].astype(f32).reshape(blocks * BLOCK // TRIAL, in_chans)
    wide = spread(rows, jnp.floor(marks * 0.5), weight.shape[0])
    product = jnp.dot(wide, weight[...].reshape(-1, 2 * width), preferred_element_type=f32)
    odd = (marks - 2 * jnp.floor(marks * 0.5))[:, :width]
    trials = odd.shape[0]
    odd = jnp.broadcast_to(odd[:, None, :], (trials, TRIAL, width)).reshape(trials * TRIAL, width)
    chosen = jnp.where(odd > 0.5, product[:, width:], product[:, :width])
    return [chosen[i * BLOCK : (i + 1) * BLOCK].T.astype(bf16) for i in range(blocks)]


def block_of(place_ref, z_step, y_index):
    y_step = jnp.where(y_index < 2, Y - y_index, y_index - 1)
    return lax.rem(place_ref[0] + z_step, Z) * Y + lax.rem(place_ref[1] + y_step, Y)


def z_step_of(index):
    return jnp.where(index % 2 == 1, Z - (index + 1) // 2, index // 2)


def read_in_kernel(weight_hbm, *rest):
    chunk_hbms = rest[:-5]
    out_ref, rows, weight, weight_sems, sems = rest[-5:]
    loads = weight_copies(weight_hbm, weight, weight_sems)
    for index, chunk in enumerate(chunk_hbms):
        loads.append(pltpu.make_async_copy(chunk, rows.at[pl.ds(index * Y, Y)], sems.at[index]))
    start_all(loads)
    wait_all(loads)

    def step(index, carry):
        blocks = project(rows, index * Y, Y, weight)
        for y_index in range(Y):
            out_ref[index * Y + y_index] = blocks[y_index]
        return carry

    lax.fori_loop(0, len(chunk_hbms), step, 0)


def forward_kernel(place_ref, taps_ref, gain_ref, twist_ref, filter_hbm, *rest):
    early_hbms, table_hbms, rest = rest[:3], rest[3:7], rest[7:]
    gated_hbm, gate_hbm, spectrum_hbm, both, spectra, gated_all, spectrum_all, *rest = rest
    tables = rest[:4]
    early_sems, sems, store_sems = rest[4:]
    others = []
    for early_hbm in early_hbms:
        for index in range(early_hbm.shape[0]):
            number = len(others)
            target = both.at[block_of(place_ref, z_step_of(number // Y), number % Y)]
            others.append(pltpu.make_async_copy(early_hbm.at[index], target, early_sems.at[number]))
    pairs = [(filter_hbm, spectra)] + list(zip(table_hbms, tables))
    others += [pltpu.make_async_copy(source, target, sems.at[index]) for index, (source, target) in enumerate(pairs)]
    start_all(others)
    cosine, sine = twists_of(twist_ref)
    lane = lax.broadcasted_iota(jnp.int32, (BLOCKS, LANE8, BLOCK), 2)
    count = BLOCKS * LANE8
    cube = (BLOCKS, LANE8, BLOCK)
    wait_all(others)
    gate_store = pltpu.make_async_copy(both.at[:, pl.ds(CHANS, CHANS), :], gate_hbm, store_sems.at[0, GROUPS // 2])
    gate_store.start()
    first_ref, second_ref, back_second_ref, back_first_ref = tables

    def stores_of(pair):
        here = pl.ds(pl.multiple_of(pair * 2 * LANE8, 2 * LANE8), 2 * LANE8)
        groups = pl.ds(pair * 2, 2)
        return [
            pltpu.make_async_copy(gated_all.at[:, here, :], gated_hbm.at[:, here, :], store_sems.at[0, pair]),
            pltpu.make_async_copy(spectrum_all.at[groups], spectrum_hbm.at[groups], store_sems.at[1, pair]),
        ]

    def short(value, group):
        taps = taps_ref[:, pl.ds(pl.multiple_of(group * LANE8, LANE8), LANE8), :]
        total = taps[0][None] * value
        for shift in (1, 2):
            rolled = pltpu.roll(value.reshape(count, BLOCK), shift, 1).reshape(cube)
            before = jnp.concatenate([jnp.zeros((1, LANE8, BLOCK), f32), rolled[:-1]], 0)
            total = total + taps[shift][None] * jnp.where(lane < shift, before, rolled)
        return total.astype(bf16).astype(f32).reshape(count, BLOCK)

    def step(pair, carry):
        here = pl.ds(pl.multiple_of(pair * 2 * LANE8, 2 * LANE8), 2 * LANE8)
        there = pl.ds(pl.multiple_of(CHANS + pair * 2 * LANE8, 2 * LANE8), 2 * LANE8)
        value = both[:, here, :].astype(f32)
        gate = both[:, there, :]
        signals = [short(value[:, i * LANE8 : (i + 1) * LANE8], pair * 2 + i) for i in range(2)]
        own = forward(*signals, first_ref, second_ref, cosine, sine)
        spectrum_all[pl.ds(pair * 2, 2)] = own.reshape(2, count, 2 * BLOCK).astype(bf16)
        weight = spectra[pl.ds(pair * 2, 2)].reshape(2 * count, 2 * BLOCK).astype(f32)
        own_re, own_im = own[:, :BLOCK], own[:, BLOCK:]
        filter_re, filter_im = weight[:, :BLOCK], weight[:, BLOCK:]
        mix = jnp.concatenate([own_re * filter_re - own_im * filter_im, own_re * filter_im + own_im * filter_re], 1)
        result = backward(mix, back_second_ref, back_first_ref, cosine, sine)
        signal = jnp.concatenate([piece.reshape(cube) for piece in signals], 1)
        long_part = jnp.concatenate([result[:, i * BLOCK : (i + 1) * BLOCK].reshape(cube) for i in range(2)], 1)
        mixed = (long_part + gain_ref[here, :][None] * signal).astype(bf16).astype(f32)
        gated_all[:, here, :] = (gate.astype(f32) * mixed).astype(bf16)
        start_all(stores_of(pair))
        return carry

    lax.fori_loop(0, GROUPS // 2, step, 0, unroll=2)
    for pair in range(GROUPS // 2):
        wait_all(stores_of(pair))
    gate_store.wait()


def gradient_kernel(grad_ref, gate_ref, spectrum_ref, first_ref, second_ref, back_second_ref, back_first_ref, twist_ref, out_ref):
    cosine, sine = twists_of(twist_ref)
    count = BLOCKS * LANE8
    pair = 2 * LANE8
    for start in range(0, grad_ref.shape[1], pair):
        here = slice(start, start + pair)
        products = (grad_ref[:, here, :].astype(f32) * gate_ref[:, here, :].astype(f32)).astype(bf16).astype(f32)
        signals = [products[:, i * LANE8 : (i + 1) * LANE8].reshape(count, BLOCK) for i in range(2)]
        spectra = forward(*signals, first_ref, second_ref, cosine, sine)
        own = spectrum_ref[start // LANE8 : start // LANE8 + 2].reshape(2 * count, 2 * BLOCK).astype(f32)
        own_re, own_im = own[:, :BLOCK], own[:, BLOCK:]
        grad_re, grad_im = spectra[:, :BLOCK], spectra[:, BLOCK:]
        lag = jnp.concatenate([own_re * grad_re + own_im * grad_im, own_re * grad_im - own_im * grad_re], 1)
        result = backward(lag, back_second_ref, back_first_ref, cosine, sine)
        both = []
        for half in range(2):
            lanes = slice(half * BLOCK, (half + 1) * BLOCK)
            both.append(jnp.concatenate([result[i * LANE8 : (i + 1) * LANE8, lanes] for i in range(BLOCKS)], 1))
        out_ref[here, :] = jnp.concatenate(both, 0).astype(bf16)


def read_out_kernel(place_ref, rows_hbm, marks_hbm, weight_hbm, out_ref, weight, rows_all, chunk_all, weight_sems, sems):
    slots, inner, width = weight.shape
    trials = BLOCK // TRIAL
    first = [pltpu.make_async_copy(rows_hbm, rows_all, sems.at[0]), pltpu.make_async_copy(marks_hbm, chunk_all, sems.at[1])]
    loads = [pltpu.make_async_copy(weight_hbm.at[slot], weight.at[slot], weight_sems.at[slot]) for slot in range(slots)]
    start_all(first)
    start_all(loads)
    wait_all(first)
    places = [block_of(place_ref, 0, index) - place_ref[0] * Y for index in range(Y)]
    rows = jnp.concatenate([rows_all[:, block, :, :].reshape(inner, BLOCK).T for block in places], 0)
    marks = chunk_all[...].astype(f32).reshape(Y * trials, width)
    marks = jnp.broadcast_to(marks[:, None, :], (Y * trials, TRIAL, width)).reshape(Y * BLOCK, width)
    total = jnp.zeros((Y * BLOCK, width), f32)
    half = slots // 2
    for slot in range(slots):
        if slot % half == 0:
            wait_all(loads[slot : slot + half])
        product = jnp.dot(rows, weight[slot], preferred_element_type=f32)
        total = jnp.where(marks == slot, product, total)
    for index, block in enumerate(places):
        out_ref[block] = total[index * BLOCK : (index + 1) * BLOCK].astype(bf16)


def sum_kernel(parts_hbm, out_hbm, parts, total, in_sems, out_sems):
    count, rows, _ = parts.shape
    step = 2 * LANE8
    loads = []
    stores = []
    for index in range(rows // step):
        here = pl.ds(index * step, step)
        for part in range(count):
            load = pltpu.make_async_copy(parts_hbm.at[part, here, :], parts.at[part, here, :], in_sems.at[index, part])
            loads.append(load)
        stores.append(pltpu.make_async_copy(total.at[here, :], out_hbm.at[here, :], out_sems.at[index]))
    start_all(loads)
    for index in range(rows // step):
        wait_all(loads[index * count : (index + 1) * count])
        here = slice(index * step, (index + 1) * step)
        running = parts[0, here, :].astype(f32)
        for part in range(1, count):
            running = running + parts[part, here, :].astype(f32)
        total[here, :] = running
        stores[index].start()
    wait_all(stores)


def prepare_kernel(place_ref, session_ref, slot_ref, spikes_ref, weight_hbm, out_hbm, block_ref, own_ref, own_out_ref, value, gate, sems):
    place = place_ref[0]
    half = weight_hbm.shape[2] // 2
    window = pl.multiple_of(place // 2 * 2 * CHANS, 2 * CHANS)
    loads = [
        pltpu.make_async_copy(weight_hbm.at[:, :, pl.ds(window, 2 * CHANS)], value, sems.at[0]),
        pltpu.make_async_copy(weight_hbm.at[:, :, pl.ds(half + window, 2 * CHANS)], gate, sems.at[1]),
    ]
    start_all(loads)
    moved = pltpu.make_async_copy(out_hbm.at[:, :, lax.rem(place, Y)], own_out_ref, sems.at[2])
    moved.start()
    trials = BLOCK // TRIAL
    width = block_ref.shape[1]
    row = lax.broadcasted_iota(jnp.int32, (trials, width), 0)
    marks = jnp.zeros((trials, width), jnp.int32)
    for trial in range(trials):
        marks = jnp.where(row == trial, slot_ref[session_ref[0, trial * TRIAL]], marks)
    block_ref[:BLOCK, :] = spikes_ref[0]
    block_ref[BLOCK:, :] = marks.astype(f32).astype(bf16)
    wait_all(loads)
    slots, inner, lanes = own_ref.shape
    odd = place % 2
    low = pltpu.roll(value[...].astype(f32).reshape(slots * inner, lanes), odd * CHANS, 1)
    high = pltpu.roll(gate[...].astype(f32).reshape(slots * inner, lanes), (1 - odd) * CHANS, 1)
    lane = lax.broadcasted_iota(jnp.int32, (slots * inner, lanes), 1)
    own_ref[...] = jnp.where(lane < CHANS, low, high).astype(bf16).reshape(slots, inner, lanes)
    moved.wait()


def along_y(value, step):
    return lax.ppermute(value, "seq", [(z * Y + y, z * Y + (y + step) % Y) for z in range(Z) for y in range(Y)])


def along_z(value, step):
    return lax.ppermute(value, "seq", [(z * Y + y, (z + step) % Z * Y + y) for z in range(Z) for y in range(Y)])


def whole(count):
    return [pl.BlockSpec(memory_space=pltpu.VMEM)] * count


def local(spikes, session_of_bin, session_slot, readin_weight, short_kernel, long_filter, skip_gain, readout_weight, out_grad):
    in_chans = spikes.shape[2]
    place = lax.axis_index("seq")
    scalar = pl.BlockSpec(memory_space=pltpu.SMEM)
    hbm = pl.BlockSpec(memory_space=pltpu.HBM)
    z_groups = [[z * Y + y for z in range(Z)] for y in range(Y)]
    y_groups = [[z * Y + y for y in range(Y)] for z in range(Z)]
    coords = jnp.stack([place // Y, place % Y]).astype(jnp.int32)
    first, second, back_second, back_first, twists = transform_tables()
    params = pltpu.CompilerParams(vmem_limit_bytes=60 << 20)
    spectrum_shape = jax.ShapeDtypeStruct((GROUPS, BLOCKS * LANE8, 2 * BLOCK), bf16)
    plane = (BLOCKS, CHANS, BLOCK)
    work = 2 * GROUPS * (512 * 256 * 128 + 256 * 256 * 256)
    pair = 2 * LANE8
    same = lambda table: pl.BlockSpec(table.shape, lambda i, rank=table.ndim: (0,) * rank)

    own_shape = (2, in_chans, 2 * CHANS)
    out_split = readout_weight.reshape(2, Z, Y, CHANS, in_chans)
    block, own_weights, own_out = pl.pallas_call(
        prepare_kernel,
        out_shape=(
            jax.ShapeDtypeStruct((BLOCK + BLOCK // TRIAL, in_chans), bf16),
            jax.ShapeDtypeStruct(own_shape, bf16),
            jax.ShapeDtypeStruct((2, Z, CHANS, in_chans), bf16),
        ),
        in_specs=[scalar] * 3 + whole(1) + [hbm] * 2,
        out_specs=tuple(whole(3)),
        scratch_shapes=[pltpu.VMEM(own_shape, bf16), pltpu.VMEM(own_shape, bf16), pltpu.SemaphoreType.DMA((3,))],
        compiler_params=params,
        cost_estimate=pl.CostEstimate(flops=1 << 16, bytes_accessed=1 << 19, transcendentals=0),
        name="prepare",
    )(place.astype(jnp.int32)[None], session_of_bin, session_slot, spikes, readin_weight, out_split)
    chunk = jnp.stack([block, along_y(block, 1), along_y(block, -1), along_y(block, 2)])
    own_marks = chunk[:, BLOCK:, :]
    right, left = along_z(chunk, 1), along_z(chunk, -1)
    chunks = [chunk, right, left]

    in_weights = lax.all_gather(own_weights, "grp", axis=0, tiled=True)
    filter_spectrum = pl.pallas_call(
        filter_kernel,
        out_shape=spectrum_shape,
        grid=(GROUPS // 2,),
        in_specs=[pl.BlockSpec((pair, LENGTH), lambda i: (i, 0))] + [same(table) for table in (first, second, twists)],
        out_specs=pl.BlockSpec((2,) + spectrum_shape.shape[1:], lambda i: (i, 0, 0)),
        compiler_params=params,
        cost_estimate=pl.CostEstimate(flops=work, bytes_accessed=4 << 20, transcendentals=0),
        name="filter_transform",
    )(long_filter, first, second, twists)
    ready = (right, left, own_marks, own_out, filter_spectrum)
    right, left, own_marks, own_out, filter_spectrum = lax.optimization_barrier(ready)
    split = own_out.reshape(2, Z * CHANS, in_chans)
    out_weights = lax.all_gather(split, "grp", axis=0, tiled=True)
    right, left = along_z(right, 1), along_z(left, -1)
    chunks += [right, left]
    turned = out_grad[0].T.reshape(BLOCKS, CHANS, BLOCK)
    taps = lax.dynamic_slice_in_dim(short_kernel, place * CHANS, CHANS, 1)
    taps = jnp.broadcast_to(taps[:, :, None], (short_kernel.shape[0], CHANS, BLOCK))
    gains = jnp.broadcast_to(skip_gain[:, None], (CHANS, BLOCK))
    ready = (right, left, taps, gains, coords, turned)
    right, left, taps, gains, coords, turned = lax.optimization_barrier(ready)
    right, left = along_z(right, 1), along_z(left, -1)
    slot_count = session_slot.shape[0]
    width = 2 * CHANS

    def read_in(pieces):
        blocks = len(pieces) * Y
        return pl.pallas_call(
            read_in_kernel,
            out_shape=jax.ShapeDtypeStruct((blocks, width, BLOCK), bf16),
            in_specs=[hbm] * (1 + len(pieces)),
            out_specs=whole(1)[0],
            scratch_shapes=[
                pltpu.VMEM((blocks,) + chunk.shape[1:], bf16),
                pltpu.VMEM((slot_count // 2, in_chans, 2 * width), bf16),
                pltpu.SemaphoreType.DMA((slot_count,)),
                pltpu.SemaphoreType.DMA((len(pieces),)),
            ],
            compiler_params=params,
            cost_estimate=pl.CostEstimate(flops=work, bytes_accessed=4 << 20, transcendentals=0),
            name="read_in",
        )(in_weights, *pieces)

    early = read_in(chunks[:3])
    right, left, early, *chunks = lax.optimization_barrier((right, left, early, *chunks))
    last = along_z(right, 1)
    middle = read_in(chunks[3:])
    right, left, last, middle, turned = lax.optimization_barrier((right, left, last, middle, turned))
    grads = lax.all_to_all(turned, "seq", split_axis=0, concat_axis=0, tiled=True)
    later = read_in([right, left, last])

    tables = (first, second, back_second, back_first)
    gated, gates, spectrum = pl.pallas_call(
        forward_kernel,
        out_shape=(
            jax.ShapeDtypeStruct(plane, bf16),
            jax.ShapeDtypeStruct(plane, bf16),
            spectrum_shape,
        ),
        in_specs=[scalar] + whole(3) + [hbm] * (4 + 4),
        out_specs=(hbm,) * 3,
        scratch_shapes=[
            pltpu.VMEM((BLOCKS, 2 * CHANS, BLOCK), bf16),
            pltpu.VMEM(spectrum_shape.shape, bf16),
            pltpu.VMEM(plane, bf16),
            pltpu.VMEM(spectrum_shape.shape, bf16),
        ]
        + [pltpu.VMEM(table.shape, bf16) for table in tables]
        + [pltpu.SemaphoreType.DMA((count,)) for count in (BLOCKS, 5)]
        + [pltpu.SemaphoreType.DMA((2, GROUPS // 2 + 1))],
        compiler_params=params,
        cost_estimate=pl.CostEstimate(flops=4 * work, bytes_accessed=8 << 20, transcendentals=0),
        name="long_convolution",
    )(coords, taps, gains, twists, filter_spectrum, early, middle, later, *tables)

    gated = gated.reshape(Z, Y, CHANS, BLOCK)
    arrived = lax.all_to_all(gated, "seq", split_axis=0, concat_axis=0, tiled=True, axis_index_groups=z_groups)
    own_grad = pl.pallas_call(
        gradient_kernel,
        out_shape=jax.ShapeDtypeStruct((CHANS, LENGTH), bf16),
        grid=(GROUPS // 4,),
        in_specs=[pl.BlockSpec((BLOCKS, 2 * pair, BLOCK), lambda i: (0, i, 0))] * 2
        + [pl.BlockSpec((4,) + spectrum_shape.shape[1:], lambda i: (i, 0, 0))]
        + [same(table) for table in tables + (twists,)],
        out_specs=pl.BlockSpec((2 * pair, LENGTH), lambda i: (i, 0)),
        compiler_params=params,
        cost_estimate=pl.CostEstimate(flops=2 * work, bytes_accessed=4 << 20, transcendentals=0),
        name="filter_gradient",
    )(grads, gates, spectrum, *tables, twists)
    all_grads = lax.all_gather(own_grad, "grp", axis=0, tiled=False)
    devices = all_grads.shape[0]
    filter_grad = pl.pallas_call(
        sum_kernel,
        out_shape=jax.ShapeDtypeStruct((CHANS, LENGTH), f32),
        in_specs=[hbm],
        out_specs=hbm,
        scratch_shapes=[
            pltpu.VMEM(all_grads.shape, bf16),
            pltpu.VMEM((CHANS, LENGTH), f32),
            pltpu.SemaphoreType.DMA((CHANS // pair, devices)),
            pltpu.SemaphoreType.DMA((CHANS // pair,)),
        ],
        compiler_params=params,
        cost_estimate=pl.CostEstimate(flops=all_grads.size, bytes_accessed=5 << 20, transcendentals=0),
        name="sum_gradients",
    )(all_grads)
    partial = pl.pallas_call(
        read_out_kernel,
        out_shape=jax.ShapeDtypeStruct((Y, BLOCK, in_chans), bf16),
        in_specs=[scalar] + [hbm] * 3,
        out_specs=whole(1)[0],
        scratch_shapes=[
            pltpu.VMEM(out_weights.shape, bf16),
            pltpu.VMEM((Z, Y, CHANS, BLOCK), bf16),
            pltpu.VMEM((Y, BLOCK // TRIAL, in_chans), bf16),
        ]
        + [pltpu.SemaphoreType.DMA((count,)) for count in (slot_count, 2)],
        compiler_params=params,
        cost_estimate=pl.CostEstimate(flops=2 * 512 * 512 * 4096, bytes_accessed=6 << 20, transcendentals=0),
        name="read_out",
    )(coords, arrived, own_marks, out_weights)
    pieces = lax.all_to_all(partial, "seq", split_axis=0, concat_axis=0, tiled=True, axis_index_groups=y_groups)
    denoised = jnp.sum(pieces.astype(f32), 0).astype(bf16)
    return denoised[None], filter_grad


def solution(mesh):
    placed = (
        P("grp", "seq", None),
        P("grp", "seq"),
        P(),
        P("grp", None, None),
        P(),
        P("seq", None),
        P("seq"),
        P("grp", None, None),
        P("grp", "seq", None),
    )
    return jax.shard_map(
        local,
        mesh=mesh,
        in_specs=placed,
        out_specs=(P("grp", "seq", None), P("seq", None)),
        check_vma=False,
    )
```

```python
import jax
import jax.numpy as jnp
import numpy as np
from jax import lax
from jax.experimental import pallas as pl
from jax.experimental.pallas import tpu as pltpu
from jax.sharding import PartitionSpec as P

BLOCK = 128
TRIAL = 16
Z = 8
Y = 4
BLOCKS = Z * Y
CHANS = 64
LANE8 = 8
GROUPS = CHANS // LANE8
LENGTH = BLOCKS * BLOCK
f32 = jnp.float32
bf16 = jnp.bfloat16


def transform_tables():
    slow = np.arange(BLOCKS)
    fast = np.arange(BLOCK)
    first = np.exp(-2j * np.pi * (np.outer(slow, slow) / BLOCKS + slow[None, :] / (4.0 * BLOCKS)))
    twist = np.exp(-2j * np.pi * (slow[:, None] + 0.25) * fast[None, :] / LENGTH)
    second = np.exp(-2j * np.pi * np.outer(fast, fast) / BLOCK)
    eye = np.eye(LANE8)
    spread_first = np.concatenate([np.kron(first.real, eye), np.kron(first.imag, eye)], 0)
    forward_second = np.block([[second.real, second.imag], [-second.imag, second.real]])
    back = second.conj()
    back_second = np.block([[back.real, back.imag], [-back.imag, back.real]])
    back_first = first.conj().T / LENGTH
    spread_back = np.concatenate([np.kron(back_first.real, eye), np.kron(-back_first.imag, eye)], 1)
    as_bf16 = lambda table: jnp.asarray(table.astype(np.float32), bf16)
    twists = np.stack([twist.real, twist.imag]).astype(np.float32)
    return (
        as_bf16(spread_first),
        as_bf16(forward_second),
        as_bf16(back_second),
        as_bf16(spread_back),
        jnp.asarray(twists),
    )


def twists_of(twist_ref):
    shape = (BLOCKS, LANE8, BLOCK)
    cosine = jnp.broadcast_to(twist_ref[0][:, None, :], shape).reshape(BLOCKS * LANE8, BLOCK)
    sine = jnp.broadcast_to(twist_ref[1][:, None, :], shape).reshape(BLOCKS * LANE8, BLOCK)
    return cosine, sine


def forward(low, high, first_ref, second_ref, cosine, sine):
    rows = BLOCKS * LANE8
    signals = jnp.concatenate([low, high], 1).astype(bf16)
    part = jnp.dot(first_ref[...], signals, preferred_element_type=f32)
    turned = []
    for lanes in (slice(0, BLOCK), slice(BLOCK, 2 * BLOCK)):
        real, imag = part[:rows, lanes], part[rows:, lanes]
        turned.append(jnp.concatenate([real * cosine - imag * sine, real * sine + imag * cosine], 1))
    return jnp.dot(jnp.concatenate(turned, 0).astype(bf16), second_ref[...], preferred_element_type=f32)


def backward(spectra, back_second_ref, back_first_ref, cosine, sine):
    rows = BLOCKS * LANE8
    part = jnp.dot(spectra.astype(bf16), back_second_ref[...], preferred_element_type=f32)
    turned = []
    for start in (0, rows):
        real, imag = part[start : start + rows, :BLOCK], part[start : start + rows, BLOCK:]
        turned.append(jnp.concatenate([real * cosine + imag * sine, imag * cosine - real * sine], 0))
    return jnp.dot(back_first_ref[...], jnp.concatenate(turned, 1).astype(bf16), preferred_element_type=f32)


def filter_kernel(filter_ref, first_ref, second_ref, twist_ref, spectrum_ref):
    cosine, sine = twists_of(twist_ref)
    rows = BLOCKS * LANE8
    signals = []
    for start in (0, LANE8):
        pieces = [filter_ref[start : start + LANE8, i * BLOCK : (i + 1) * BLOCK] for i in range(BLOCKS)]
        signals.append(jnp.concatenate(pieces, 0))
    spectra = forward(*signals, first_ref, second_ref, cosine, sine)
    spectrum_ref[...] = spectra.astype(bf16).reshape(2, rows, 2 * BLOCK)


def start_all(copies):
    for copy in copies:
        copy.start()


def wait_all(copies):
    for copy in copies:
        copy.wait()


def weight_copies(weight_hbm, weight, sems):
    copies = []
    for slot in range(weight_hbm.shape[0]):
        lanes = pl.ds(slot % 2 * 2 * CHANS, 2 * CHANS)
        copies.append(pltpu.make_async_copy(weight_hbm.at[slot], weight.at[slot // 2, :, lanes], sems.at[slot]))
    return copies


def spread(rows, marks, count):
    trials, width = marks.shape
    marks = jnp.broadcast_to(marks[:, None, :], (trials, TRIAL, width)).reshape(trials * TRIAL, width).astype(bf16)
    nothing = jnp.zeros_like(rows)
    return jnp.concatenate([jnp.where(marks == number, rows, nothing) for number in range(count)], 1)


def project(rows_ref, start, blocks, weight):
    width = 2 * CHANS
    in_chans = rows_ref.shape[2]
    rows = rows_ref[pl.ds(start, blocks), :BLOCK, :].reshape(blocks * BLOCK, in_chans)
    marks = rows_ref[pl.ds(start, blocks), BLOCK:, :].astype(f32).reshape(blocks * BLOCK // TRIAL, in_chans)
    wide = spread(rows, jnp.floor(marks * 0.5), weight.shape[0])
    product = jnp.dot(wide, weight[...].reshape(-1, 2 * width), preferred_element_type=f32)
    odd = (marks - 2 * jnp.floor(marks * 0.5))[:, :width]
    trials = odd.shape[0]
    odd = jnp.broadcast_to(odd[:, None, :], (trials, TRIAL, width)).reshape(trials * TRIAL, width)
    chosen = jnp.where(odd > 0.5, product[:, width:], product[:, :width])
    return [chosen[i * BLOCK : (i + 1) * BLOCK].T.astype(bf16) for i in range(blocks)]


def block_of(place_ref, z_step, y_index):
    y_step = jnp.where(y_index < 2, Y - y_index, y_index - 1)
    return lax.rem(place_ref[0] + z_step, Z) * Y + lax.rem(place_ref[1] + y_step, Y)


def z_step_of(index):
    return jnp.where(index % 2 == 1, Z - (index + 1) // 2, index // 2)


def read_in_kernel(weight_hbm, *rest):
    chunk_hbms = rest[:-5]
    out_ref, rows, weight, weight_sems, sems = rest[-5:]
    loads = weight_copies(weight_hbm, weight, weight_sems)
    for index, chunk in enumerate(chunk_hbms):
        loads.append(pltpu.make_async_copy(chunk, rows.at[pl.ds(index * Y, Y)], sems.at[index]))
    start_all(loads)
    wait_all(loads)

    def step(index, carry):
        blocks = project(rows, index * Y, Y, weight)
        for y_index in range(Y):
            out_ref[index * Y + y_index] = blocks[y_index]
        return carry

    lax.fori_loop(0, len(chunk_hbms), step, 0)


def forward_kernel(place_ref, taps_ref, gain_ref, twist_ref, filter_hbm, *rest):
    early_hbms, table_hbms, rest = rest[:3], rest[3:7], rest[7:]
    gated_hbm, gate_hbm, spectrum_hbm, both, spectra, gated_all, spectrum_all, *rest = rest
    tables = rest[:4]
    early_sems, sems, store_sems = rest[4:]
    others = []
    for early_hbm in early_hbms:
        for index in range(early_hbm.shape[0]):
            number = len(others)
            target = both.at[block_of(place_ref, z_step_of(number // Y), number % Y)]
            others.append(pltpu.make_async_copy(early_hbm.at[index], target, early_sems.at[number]))
    pairs = [(filter_hbm, spectra)] + list(zip(table_hbms, tables))
    others += [pltpu.make_async_copy(source, target, sems.at[index]) for index, (source, target) in enumerate(pairs)]
    start_all(others)
    cosine, sine = twists_of(twist_ref)
    lane = lax.broadcasted_iota(jnp.int32, (BLOCKS, LANE8, BLOCK), 2)
    count = BLOCKS * LANE8
    cube = (BLOCKS, LANE8, BLOCK)
    wait_all(others)
    gate_store = pltpu.make_async_copy(both.at[:, pl.ds(CHANS, CHANS), :], gate_hbm, store_sems.at[0, GROUPS // 2])
    gate_store.start()
    first_ref, second_ref, back_second_ref, back_first_ref = tables

    def stores_of(pair):
        here = pl.ds(pl.multiple_of(pair * 2 * LANE8, 2 * LANE8), 2 * LANE8)
        groups = pl.ds(pair * 2, 2)
        return [
            pltpu.make_async_copy(gated_all.at[:, here, :], gated_hbm.at[:, here, :], store_sems.at[0, pair]),
            pltpu.make_async_copy(spectrum_all.at[groups], spectrum_hbm.at[groups], store_sems.at[1, pair]),
        ]

    def short(value, group):
        taps = taps_ref[:, pl.ds(pl.multiple_of(group * LANE8, LANE8), LANE8), :]
        total = taps[0][None] * value
        for shift in (1, 2):
            rolled = pltpu.roll(value.reshape(count, BLOCK), shift, 1).reshape(cube)
            before = jnp.concatenate([jnp.zeros((1, LANE8, BLOCK), f32), rolled[:-1]], 0)
            total = total + taps[shift][None] * jnp.where(lane < shift, before, rolled)
        return total.astype(bf16).astype(f32).reshape(count, BLOCK)

    def step(pair, carry):
        here = pl.ds(pl.multiple_of(pair * 2 * LANE8, 2 * LANE8), 2 * LANE8)
        there = pl.ds(pl.multiple_of(CHANS + pair * 2 * LANE8, 2 * LANE8), 2 * LANE8)
        value = both[:, here, :].astype(f32)
        gate = both[:, there, :]
        signals = [short(value[:, i * LANE8 : (i + 1) * LANE8], pair * 2 + i) for i in range(2)]
        own = forward(*signals, first_ref, second_ref, cosine, sine)
        spectrum_all[pl.ds(pair * 2, 2)] = own.reshape(2, count, 2 * BLOCK).astype(bf16)
        weight = spectra[pl.ds(pair * 2, 2)].reshape(2 * count, 2 * BLOCK).astype(f32)
        own_re, own_im = own[:, :BLOCK], own[:, BLOCK:]
        filter_re, filter_im = weight[:, :BLOCK], weight[:, BLOCK:]
        mix = jnp.concatenate([own_re * filter_re - own_im * filter_im, own_re * filter_im + own_im * filter_re], 1)
        result = backward(mix, back_second_ref, back_first_ref, cosine, sine)
        signal = jnp.concatenate([piece.reshape(cube) for piece in signals], 1)
        long_part = jnp.concatenate([result[:, i * BLOCK : (i + 1) * BLOCK].reshape(cube) for i in range(2)], 1)
        mixed = (long_part + gain_ref[here, :][None] * signal).astype(bf16).astype(f32)
        gated_all[:, here, :] = (gate.astype(f32) * mixed).astype(bf16)
        start_all(stores_of(pair))
        return carry

    lax.fori_loop(0, GROUPS // 2, step, 0, unroll=2)
    for pair in range(GROUPS // 2):
        wait_all(stores_of(pair))
    gate_store.wait()


def gradient_kernel(grad_ref, gate_ref, spectrum_ref, first_ref, second_ref, back_second_ref, back_first_ref, twist_ref, out_ref):
    cosine, sine = twists_of(twist_ref)
    count = BLOCKS * LANE8
    pair = 2 * LANE8
    for start in range(0, grad_ref.shape[1], pair):
        here = slice(start, start + pair)
        products = (grad_ref[:, here, :].astype(f32) * gate_ref[:, here, :].astype(f32)).astype(bf16).astype(f32)
        signals = [products[:, i * LANE8 : (i + 1) * LANE8].reshape(count, BLOCK) for i in range(2)]
        spectra = forward(*signals, first_ref, second_ref, cosine, sine)
        own = spectrum_ref[start // LANE8 : start // LANE8 + 2].reshape(2 * count, 2 * BLOCK).astype(f32)
        own_re, own_im = own[:, :BLOCK], own[:, BLOCK:]
        grad_re, grad_im = spectra[:, :BLOCK], spectra[:, BLOCK:]
        lag = jnp.concatenate([own_re * grad_re + own_im * grad_im, own_re * grad_im - own_im * grad_re], 1)
        result = backward(lag, back_second_ref, back_first_ref, cosine, sine)
        both = []
        for half in range(2):
            lanes = slice(half * BLOCK, (half + 1) * BLOCK)
            both.append(jnp.concatenate([result[i * LANE8 : (i + 1) * LANE8, lanes] for i in range(BLOCKS)], 1))
        out_ref[here, :] = jnp.concatenate(both, 0).astype(bf16)


def read_out_kernel(place_ref, rows_hbm, marks_hbm, weight_hbm, out_ref, weight, rows_all, chunk_all, weight_sems, sems):
    slots, inner, width = weight.shape
    trials = BLOCK // TRIAL
    first = [pltpu.make_async_copy(rows_hbm, rows_all, sems.at[0]), pltpu.make_async_copy(marks_hbm, chunk_all, sems.at[1])]
    loads = [pltpu.make_async_copy(weight_hbm.at[slot], weight.at[slot], weight_sems.at[slot]) for slot in range(slots)]
    start_all(first)
    start_all(loads)
    wait_all(first)
    places = [block_of(place_ref, 0, index) - place_ref[0] * Y for index in range(Y)]
    rows = jnp.concatenate([rows_all[:, block, :, :].reshape(inner, BLOCK).T for block in places], 0)
    marks = chunk_all[...].astype(f32).reshape(Y * trials, width)
    marks = jnp.broadcast_to(marks[:, None, :], (Y * trials, TRIAL, width)).reshape(Y * BLOCK, width)
    wait_all(loads)
    total = jnp.zeros((Y * BLOCK, width), f32)
    for slot in range(slots):
        product = jnp.dot(rows, weight[slot], preferred_element_type=f32)
        total = jnp.where(marks == slot, product, total)
    for index, block in enumerate(places):
        out_ref[block] = total[index * BLOCK : (index + 1) * BLOCK].astype(bf16)


def sum_kernel(parts_hbm, out_hbm, parts, total, in_sems, out_sems):
    count, rows, _ = parts.shape
    step = 2 * LANE8
    loads = []
    stores = []
    for index in range(rows // step):
        here = pl.ds(index * step, step)
        for part in range(count):
            load = pltpu.make_async_copy(parts_hbm.at[part, here, :], parts.at[part, here, :], in_sems.at[index, part])
            loads.append(load)
        stores.append(pltpu.make_async_copy(total.at[here, :], out_hbm.at[here, :], out_sems.at[index]))
    start_all(loads)
    for index in range(rows // step):
        wait_all(loads[index * count : (index + 1) * count])
        here = slice(index * step, (index + 1) * step)
        running = parts[0, here, :].astype(f32)
        for part in range(1, count):
            running = running + parts[part, here, :].astype(f32)
        total[here, :] = running
        stores[index].start()
    wait_all(stores)


def prepare_kernel(place_ref, session_ref, slot_ref, spikes_ref, weight_hbm, out_hbm, block_ref, own_ref, own_out_ref, value, gate, sems):
    place = place_ref[0]
    half = weight_hbm.shape[2] // 2
    window = pl.multiple_of(place // 2 * 2 * CHANS, 2 * CHANS)
    loads = [
        pltpu.make_async_copy(weight_hbm.at[:, :, pl.ds(window, 2 * CHANS)], value, sems.at[0]),
        pltpu.make_async_copy(weight_hbm.at[:, :, pl.ds(half + window, 2 * CHANS)], gate, sems.at[1]),
    ]
    start_all(loads)
    moved = pltpu.make_async_copy(out_hbm.at[:, :, lax.rem(place, Y)], own_out_ref, sems.at[2])
    moved.start()
    trials = BLOCK // TRIAL
    width = block_ref.shape[1]
    row = lax.broadcasted_iota(jnp.int32, (trials, width), 0)
    marks = jnp.zeros((trials, width), jnp.int32)
    for trial in range(trials):
        marks = jnp.where(row == trial, slot_ref[session_ref[0, trial * TRIAL]], marks)
    block_ref[:BLOCK, :] = spikes_ref[0]
    block_ref[BLOCK:, :] = marks.astype(f32).astype(bf16)
    wait_all(loads)
    slots, inner, lanes = own_ref.shape
    odd = place % 2
    low = pltpu.roll(value[...].astype(f32).reshape(slots * inner, lanes), odd * CHANS, 1)
    high = pltpu.roll(gate[...].astype(f32).reshape(slots * inner, lanes), (1 - odd) * CHANS, 1)
    lane = lax.broadcasted_iota(jnp.int32, (slots * inner, lanes), 1)
    own_ref[...] = jnp.where(lane < CHANS, low, high).astype(bf16).reshape(slots, inner, lanes)
    moved.wait()


def along_y(value, step):
    return lax.ppermute(value, "seq", [(z * Y + y, z * Y + (y + step) % Y) for z in range(Z) for y in range(Y)])


def along_z(value, step):
    return lax.ppermute(value, "seq", [(z * Y + y, (z + step) % Z * Y + y) for z in range(Z) for y in range(Y)])


def whole(count):
    return [pl.BlockSpec(memory_space=pltpu.VMEM)] * count


def local(spikes, session_of_bin, session_slot, readin_weight, short_kernel, long_filter, skip_gain, readout_weight, out_grad):
    in_chans = spikes.shape[2]
    place = lax.axis_index("seq")
    scalar = pl.BlockSpec(memory_space=pltpu.SMEM)
    hbm = pl.BlockSpec(memory_space=pltpu.HBM)
    z_groups = [[z * Y + y for z in range(Z)] for y in range(Y)]
    y_groups = [[z * Y + y for y in range(Y)] for z in range(Z)]
    coords = jnp.stack([place // Y, place % Y]).astype(jnp.int32)
    first, second, back_second, back_first, twists = transform_tables()
    params = pltpu.CompilerParams(vmem_limit_bytes=60 << 20)
    spectrum_shape = jax.ShapeDtypeStruct((GROUPS, BLOCKS * LANE8, 2 * BLOCK), bf16)
    plane = (BLOCKS, CHANS, BLOCK)
    work = 2 * GROUPS * (512 * 256 * 128 + 256 * 256 * 256)
    pair = 2 * LANE8
    same = lambda table: pl.BlockSpec(table.shape, lambda i, rank=table.ndim: (0,) * rank)

    own_shape = (2, in_chans, 2 * CHANS)
    out_split = readout_weight.reshape(2, Z, Y, CHANS, in_chans)
    block, own_weights, own_out = pl.pallas_call(
        prepare_kernel,
        out_shape=(
            jax.ShapeDtypeStruct((BLOCK + BLOCK // TRIAL, in_chans), bf16),
            jax.ShapeDtypeStruct(own_shape, bf16),
            jax.ShapeDtypeStruct((2, Z, CHANS, in_chans), bf16),
        ),
        in_specs=[scalar] * 3 + whole(1) + [hbm] * 2,
        out_specs=tuple(whole(3)),
        scratch_shapes=[pltpu.VMEM(own_shape, bf16), pltpu.VMEM(own_shape, bf16), pltpu.SemaphoreType.DMA((3,))],
        compiler_params=params,
        cost_estimate=pl.CostEstimate(flops=1 << 16, bytes_accessed=1 << 19, transcendentals=0),
        name="prepare",
    )(place.astype(jnp.int32)[None], session_of_bin, session_slot, spikes, readin_weight, out_split)
    chunk = jnp.stack([block, along_y(block, 1), along_y(block, -1), along_y(block, 2)])
    own_marks = chunk[:, BLOCK:, :]
    right, left = along_z(chunk, 1), along_z(chunk, -1)
    chunks = [chunk, right, left]

    in_weights = lax.all_gather(own_weights, "grp", axis=0, tiled=True)
    filter_spectrum = pl.pallas_call(
        filter_kernel,
        out_shape=spectrum_shape,
        grid=(GROUPS // 2,),
        in_specs=[pl.BlockSpec((pair, LENGTH), lambda i: (i, 0))] + [same(table) for table in (first, second, twists)],
        out_specs=pl.BlockSpec((2,) + spectrum_shape.shape[1:], lambda i: (i, 0, 0)),
        compiler_params=params,
        cost_estimate=pl.CostEstimate(flops=work, bytes_accessed=4 << 20, transcendentals=0),
        name="filter_transform",
    )(long_filter, first, second, twists)
    ready = (right, left, own_marks, own_out, filter_spectrum)
    right, left, own_marks, own_out, filter_spectrum = lax.optimization_barrier(ready)
    split = own_out.reshape(2, Z * CHANS, in_chans)
    out_weights = lax.all_gather(split, "grp", axis=0, tiled=True)
    right, left = along_z(right, 1), along_z(left, -1)
    chunks += [right, left]
    turned = out_grad[0].T.reshape(BLOCKS, CHANS, BLOCK)
    taps = lax.dynamic_slice_in_dim(short_kernel, place * CHANS, CHANS, 1)
    taps = jnp.broadcast_to(taps[:, :, None], (short_kernel.shape[0], CHANS, BLOCK))
    gains = jnp.broadcast_to(skip_gain[:, None], (CHANS, BLOCK))
    ready = (right, left, taps, gains, coords, turned)
    right, left, taps, gains, coords, turned = lax.optimization_barrier(ready)
    right, left = along_z(right, 1), along_z(left, -1)
    slot_count = session_slot.shape[0]
    width = 2 * CHANS

    def read_in(pieces):
        blocks = len(pieces) * Y
        return pl.pallas_call(
            read_in_kernel,
            out_shape=jax.ShapeDtypeStruct((blocks, width, BLOCK), bf16),
            in_specs=[hbm] * (1 + len(pieces)),
            out_specs=whole(1)[0],
            scratch_shapes=[
                pltpu.VMEM((blocks,) + chunk.shape[1:], bf16),
                pltpu.VMEM((slot_count // 2, in_chans, 2 * width), bf16),
                pltpu.SemaphoreType.DMA((slot_count,)),
                pltpu.SemaphoreType.DMA((len(pieces),)),
            ],
            compiler_params=params,
            cost_estimate=pl.CostEstimate(flops=work, bytes_accessed=4 << 20, transcendentals=0),
            name="read_in",
        )(in_weights, *pieces)

    early = read_in(chunks[:3])
    right, left, early, *chunks = lax.optimization_barrier((right, left, early, *chunks))
    last = along_z(right, 1)
    middle = read_in(chunks[3:])
    right, left, last, middle, turned = lax.optimization_barrier((right, left, last, middle, turned))
    grads = lax.all_to_all(turned, "seq", split_axis=0, concat_axis=0, tiled=True)
    later = read_in([right, left, last])

    tables = (first, second, back_second, back_first)
    gated, gates, spectrum = pl.pallas_call(
        forward_kernel,
        out_shape=(
            jax.ShapeDtypeStruct(plane, bf16),
            jax.ShapeDtypeStruct(plane, bf16),
            spectrum_shape,
        ),
        in_specs=[scalar] + whole(3) + [hbm] * (4 + 4),
        out_specs=(hbm,) * 3,
        scratch_shapes=[
            pltpu.VMEM((BLOCKS, 2 * CHANS, BLOCK), bf16),
            pltpu.VMEM(spectrum_shape.shape, bf16),
            pltpu.VMEM(plane, bf16),
            pltpu.VMEM(spectrum_shape.shape, bf16),
        ]
        + [pltpu.VMEM(table.shape, bf16) for table in tables]
        + [pltpu.SemaphoreType.DMA((count,)) for count in (BLOCKS, 5)]
        + [pltpu.SemaphoreType.DMA((2, GROUPS // 2 + 1))],
        compiler_params=params,
        cost_estimate=pl.CostEstimate(flops=4 * work, bytes_accessed=8 << 20, transcendentals=0),
        name="long_convolution",
    )(coords, taps, gains, twists, filter_spectrum, early, middle, later, *tables)

    gated = gated.reshape(Z, Y, CHANS, BLOCK)
    arrived = lax.all_to_all(gated, "seq", split_axis=0, concat_axis=0, tiled=True, axis_index_groups=z_groups)
    own_grad = pl.pallas_call(
        gradient_kernel,
        out_shape=jax.ShapeDtypeStruct((CHANS, LENGTH), bf16),
        grid=(GROUPS // 8,),
        in_specs=[pl.BlockSpec((BLOCKS, 4 * pair, BLOCK), lambda i: (0, i, 0))] * 2
        + [pl.BlockSpec((8,) + spectrum_shape.shape[1:], lambda i: (i, 0, 0))]
        + [same(table) for table in tables + (twists,)],
        out_specs=pl.BlockSpec((4 * pair, LENGTH), lambda i: (i, 0)),
        compiler_params=params,
        cost_estimate=pl.CostEstimate(flops=2 * work, bytes_accessed=4 << 20, transcendentals=0),
        name="filter_gradient",
    )(grads, gates, spectrum, *tables, twists)
    all_grads = lax.all_gather(own_grad, "grp", axis=0, tiled=False)
    devices = all_grads.shape[0]
    filter_grad = pl.pallas_call(
        sum_kernel,
        out_shape=jax.ShapeDtypeStruct((CHANS, LENGTH), f32),
        in_specs=[hbm],
        out_specs=hbm,
        scratch_shapes=[
            pltpu.VMEM(all_grads.shape, bf16),
            pltpu.VMEM((CHANS, LENGTH), f32),
            pltpu.SemaphoreType.DMA((CHANS // pair, devices)),
            pltpu.SemaphoreType.DMA((CHANS // pair,)),
        ],
        compiler_params=params,
        cost_estimate=pl.CostEstimate(flops=all_grads.size, bytes_accessed=5 << 20, transcendentals=0),
        name="sum_gradients",
    )(all_grads)
    partial = pl.pallas_call(
        read_out_kernel,
        out_shape=jax.ShapeDtypeStruct((Y, BLOCK, in_chans), bf16),
        in_specs=[scalar] + [hbm] * 3,
        out_specs=whole(1)[0],
        scratch_shapes=[
            pltpu.VMEM(out_weights.shape, bf16),
            pltpu.VMEM((Z, Y, CHANS, BLOCK), bf16),
            pltpu.VMEM((Y, BLOCK // TRIAL, in_chans), bf16),
        ]
        + [pltpu.SemaphoreType.DMA((count,)) for count in (slot_count, 2)],
        compiler_params=params,
        cost_estimate=pl.CostEstimate(flops=2 * 512 * 512 * 4096, bytes_accessed=6 << 20, transcendentals=0),
        name="read_out",
    )(coords, arrived, own_marks, out_weights)
    pieces = lax.all_to_all(partial, "seq", split_axis=0, concat_axis=0, tiled=True, axis_index_groups=y_groups)
    denoised = jnp.sum(pieces.astype(f32), 0).astype(bf16)
    return denoised[None], filter_grad


def solution(mesh):
    placed = (
        P("grp", "seq", None),
        P("grp", "seq"),
        P(),
        P("grp", None, None),
        P(),
        P("seq", None),
        P("seq"),
        P("grp", None, None),
        P("grp", "seq", None),
    )
    return jax.shard_map(
        local,
        mesh=mesh,
        in_specs=placed,
        out_specs=(P("grp", "seq", None), P("seq", None)),
        check_vma=False,
    )
```
